128 devices in a mesh: site: 32 (over z, y, core), branch: 4 (over x).
Axes of the slice: x: 4, y: 4, z: 4, core: 2. Of those that a mesh axis runs over, the one named last changes fastest.
Arguments:
- states: int32 [256, 8192], P(None, 'site'), may hold values from 0 to 63, as said below
- gap_mask: int32 [256, 8192], P(None, 'site'), may hold values 0 or 1
- weights: int32 [8192], P('site'), may hold values from 1 to 9
- leaf_order: int32 [256], replicated, may hold values from 0 to 255, each once
- exchanges: float32 [64, 64], replicated, may hold values from 0.3 to 3
- codon_freq: float32 [64], replicated, may hold values from 0.3 to 3
- omega_ratio: float32 [8], replicated, may hold values from 0.1 to 2
- lengths: float32 [508], P('branch'), may hold values from 0.05 to 1.5
- classes: int32 [508], P('branch'), may hold values from 0 to 7
Outputs:
- grad_exch: float32 [64, 64], replicated
- grad_omega: float32 [8], replicated
- grad_length: float32 [508], P('branch')
- loglik: float32 [], replicated
The draws below stay inside these ranges and needn't reach their ends.
Inputs may be any that keep to these rules, and one draw needn't show every extreme that they name: `states`: every state is a sense codon: never 10, 11 or 14.
All inputs are finite; a program needn't handle non-finite values. No bound on the sum of `gap_mask` on one device may be relied on, other than what follows from the above.
Results may differ from the reference program's by a relative error of at most 0.0003.
Values sent between devices are 32-bit elements; how exact they have to be, the bound alone decides.
A program may use at most 192 MiB of HBM per device.

```python
import math
import jax
import jax.numpy as jnp
import numpy as np
from jax import lax

LEVELS = 6
LEAF_DEV = 64
EDGES = 127
TAXA = 256
BRANCHES = 508
S_DEV = 256
SITES = 8192
CLASSES = 8
N_SITE = 32
N_BRANCH = 4


def draw_states(key, part):
    raw_state = jax.random.randint(key, (TAXA, SITES), 0, 61)
    return (raw_state + 2 * (raw_state >= 10).astype(jnp.int32) + (raw_state >= 12).astype(jnp.int32)).astype(jnp.int32)


def draw_weights(key, part):
    base_weight = jax.random.randint(key, (SITES,), 1, 4)
    position = jnp.arange(SITES, dtype=jnp.int32)
    tier_factor = 1 + 3 * position // SITES
    return (base_weight * tier_factor).astype(jnp.int32)


def with_ends(drawn, key, smallest, top_value):
    shape = drawn.shape
    place = [jax.random.randint(jax.random.fold_in(key, axis), (), 0, shape[axis]) for axis in range(len(shape))]
    drawn = drawn.at[tuple(place)].set(smallest)
    longest = shape.index(max(shape))
    place[longest] = (place[longest] + 1) % shape[longest]
    return drawn.at[tuple(place)].set(top_value)


def block_scale(own_key, shape, split, least, top_value):
    def one(axis_at, shards_of):
        draws = jax.random.uniform(jax.random.fold_in(jax.random.fold_in(own_key, 6), axis_at), (shards_of,), jnp.float32, least / len(split), top_value / len(split))
        return jnp.repeat(jnp.exp(draws), shape[axis_at] // shards_of).reshape((-1,) + (1,) * (len(shape) - axis_at - 1))

    loudness = one(*split[0])
    for cut in split[1:]:
        loudness = loudness * one(*cut)
    return loudness


def setup_inputs(seed: int = 0) -> dict:
    key_of = jax.random.split(jax.random.key(seed), 10)
    states = draw_states(jax.random.fold_in(key_of[9], 71), 0)
    gap_mask = with_ends((jax.random.randint(key_of[1], (TAXA, SITES), 0, 8) < 1).astype(jnp.int32), jax.random.fold_in(key_of[1], 1), 0, 1)
    weights = draw_weights(jax.random.fold_in(key_of[9], 71), 0)
    leaf_order = jax.random.permutation(key_of[3], TAXA).astype(jnp.int32)
    exchanges = jnp.clip(jnp.exp(jax.random.uniform(key_of[4], (64, 64), jnp.float32, math.log(0.3), math.log(3.0))), 0.3, 3.0)
    codon_freq = jnp.clip(jnp.exp(jax.random.uniform(key_of[5], (64,), jnp.float32, math.log(0.3), math.log(3.0))), 0.3, 3.0)
    omega_ratio = jnp.clip(jnp.exp(jax.random.uniform(key_of[6], (CLASSES,), jnp.float32, math.log(0.1), math.log(2.0))), 0.1, 2.0)
    lengths = jnp.clip(jnp.exp(math.log(1.5) - 3.4011974 * jax.random.uniform(key_of[7], (BRANCHES,), jnp.float32) ** block_scale(key_of[7], (BRANCHES,), ((0, 4),), -0.2, 0.2)), 0.05, 1.5)
    classes = with_ends(jax.random.randint(key_of[8], (BRANCHES,), 0, CLASSES), jax.random.fold_in(key_of[8], 1), 0, CLASSES - 1).astype(jnp.int32)
    return dict(states=states, gap_mask=gap_mask, weights=weights, leaf_order=leaf_order, exchanges=exchanges, codon_freq=codon_freq, omega_ratio=omega_ratio, lengths=lengths, classes=classes)


CODE_TABLE = 'FFLLSSSSYYXXCCXWLLLLPPPPHHQQRRRRIIIMTTTTNNKKSSRRVVVVAAAADDEEGGGG'

def codon_tables():
    amino_acid = np.array(list(CODE_TABLE))
    codon_index = np.arange(64)
    digits = np.stack([codon_index // 16, codon_index // 4 % 4, codon_index % 4], 1)
    differ = (digits[:, None, :] != digits[None, :, :]).sum(-1)
    is_sense = amino_acid != 'X'
    single = (differ == 1) & is_sense[:, None] & is_sense[None, :]
    nonsyn = single & (amino_acid[:, None] != amino_acid[None, :])
    return (is_sense.astype(np.float32), single.astype(np.float32), nonsyn.astype(np.float32))

def build_rates(exchanges, codon_freq, omega_ratio):
    is_sense, single, nonsyn = codon_tables()
    stationary = codon_freq * is_sense / jnp.sum(codon_freq * is_sense)
    symmetric = 0.5 * (exchanges + exchanges.T)
    factor = 1.0 + nonsyn[None, :, :] * (omega_ratio[:, None, None] - 1.0)
    off_diag = symmetric[None, :, :] * stationary[None, None, :] * factor * single[None, :, :]
    row_total = lax.optimization_barrier(jnp.sum(off_diag, axis=2))
    mean_rate = lax.optimization_barrier(jnp.sum(stationary[None, :] * row_total, axis=1))
    identity = jnp.eye(64, dtype=exchanges.dtype)
    rate_matrix = (off_diag - row_total[:, :, None] * identity[None]) / mean_rate[:, None, None]
    return (rate_matrix, stationary)

def product(left, right):
    return jnp.einsum('bij,bjk->bik', left, right, precision=lax.Precision.HIGHEST)

def expm_taylor(scaled):
    reduced = scaled / 16.0
    identity = jnp.eye(64, dtype=scaled.dtype)
    series = jnp.broadcast_to(identity, scaled.shape)
    for degree in range(8, 0, -1):
        series = identity + product(reduced, series) / degree
    for square_step in range(4):
        series = product(series, series)
    return series

def forward(probs, vectors):
    return jnp.einsum('bij,bjs->bis', probs, vectors, precision=lax.Precision.HIGHEST)

def carried(probs, vectors):
    return jnp.einsum('bji,bjs->bis', probs, vectors, precision=lax.Precision.HIGHEST)

def leaf_partials(leaf_states, gap_rows):
    codon_axis = jnp.arange(64, dtype=jnp.int32)
    indicator = (leaf_states[:, None, :] == codon_axis[None, :, None]).astype(jnp.float32)
    return jnp.where(gap_rows[:, None, :] > 0, jnp.float32(1.0), indicator)

def up_pass(probs, leaves):
    levels = [leaves]
    messages = []
    logscale = jnp.zeros(leaves.shape[2:], jnp.float32)
    current = leaves
    for height in range(LEVELS):
        amount = current.shape[0]
        offset = 2 * LEAF_DEV - 2 * amount
        message = forward(probs[offset:offset + amount], current)
        messages.append(message)
        raw_parent = message[0::2] * message[1::2]
        scaling = lax.optimization_barrier(jnp.sum(raw_parent, axis=1))
        current = raw_parent / scaling[:, None, :]
        logscale = logscale + lax.optimization_barrier(jnp.sum(jnp.log(scaling), axis=0))
        levels.append(current)
    messages.append(forward(probs[EDGES - 1:EDGES], current))
    return (levels, messages, logscale)

def root_terms(stationary, top_messages, top_logs):
    members = top_messages.shape[0]
    joint = stationary[:, None] * top_messages[0]
    for member in range(1, members):
        joint = joint * top_messages[member]
    site_ll = jnp.log(lax.optimization_barrier(jnp.sum(joint, axis=0))) + lax.optimization_barrier(jnp.sum(top_logs, axis=0))
    above_list = []
    for member in range(members):
        vector = jnp.broadcast_to(stationary[:, None], top_messages.shape[1:])
        for other in range(members):
            if other != member:
                vector = vector * top_messages[other]
        above_list.append(vector)
    return (site_ll, jnp.stack(above_list))

def down_pass(probs, levels, messages, above_top):
    a_list = [above_top]
    current = above_top
    for height in range(LEVELS, 0, -1):
        amount = levels[height].shape[0]
        offset = 2 * LEAF_DEV - 2 * amount
        down_part = carried(probs[offset:offset + amount], current)
        down_part = down_part / lax.optimization_barrier(jnp.sum(down_part, axis=1, keepdims=True))
        message = messages[height - 1]
        current = jnp.stack([down_part * message[1::2], down_part * message[0::2]], axis=1).reshape(message.shape)
        a_list.append(current)
    return a_list[::-1]

def weigh(a_list, messages, site_weight, total_sites):
    weighted = []
    for vector, message in zip(a_list, messages):
        likelihood = lax.optimization_barrier(jnp.sum(vector * message, axis=1))
        weighted.append(vector * (site_weight / (likelihood * total_sites))[:, None, :])
    return weighted

def reference(states, gap_mask, weights, leaf_order, exchanges, codon_freq, omega_ratio, lengths, classes):
    rate_matrix, stationary = build_rates(exchanges, codon_freq, omega_ratio)
    class_pick = (classes[:, None] == jnp.arange(CLASSES, dtype=jnp.int32)[None, :]).astype(jnp.float32)
    branch_rates = jnp.einsum('bc,cij->bij', class_pick, rate_matrix, precision=lax.Precision.HIGHEST)
    scaled = branch_rates * lengths[:, None, None]
    probs_all, pullback = jax.vjp(expm_taylor, scaled)
    probs_tree = probs_all.reshape(N_BRANCH, EDGES, 64, 64)
    state_blocks = states.reshape(TAXA, N_SITE, S_DEV).transpose(1, 0, 2)
    gap_blocks = gap_mask.reshape(TAXA, N_SITE, S_DEV).transpose(1, 0, 2)
    weight_blocks = weights.reshape(N_SITE, S_DEV).astype(jnp.float32)

    def block_step(carry, inputs):
        counts_sum, log_sum = carry
        block_states, block_gaps, site_weight = inputs
        level_sets = []
        message_sets = []
        top_list = []
        log_list = []
        for member in range(N_BRANCH):
            taxon_rows = leaf_order[member * LEAF_DEV:(member + 1) * LEAF_DEV]
            leaves = leaf_partials(jnp.take(block_states, taxon_rows, axis=0), jnp.take(block_gaps, taxon_rows, axis=0))
            levels, messages, logscale = up_pass(probs_tree[member], leaves)
            level_sets.append(levels)
            message_sets.append(messages)
            top_list.append(messages[-1])
            log_list.append(logscale)
        top_messages = jnp.concatenate(top_list, axis=0)
        top_logs = jnp.stack(log_list)
        site_ll, above_all = root_terms(stationary, top_messages, top_logs)
        block_counts = []
        for member in range(N_BRANCH):
            a_list = down_pass(probs_tree[member], level_sets[member], message_sets[member], above_all[member:member + 1])
            weighted = weigh(a_list, message_sets[member], site_weight, SITES)
            for vector, partial_value in zip(weighted, level_sets[member]):
                block_counts.append(jnp.einsum('bis,bjs->bij', vector, partial_value, precision=lax.Precision.HIGHEST))
        new_counts = counts_sum + jnp.concatenate(block_counts, axis=0)
        return ((new_counts, log_sum + jnp.sum(site_weight * site_ll)), None)
    start_carry = (jnp.zeros((N_BRANCH * EDGES, 64, 64), jnp.float32), jnp.float32(0.0))
    (counts, log_total), unused = lax.scan(block_step, start_carry, (state_blocks, gap_blocks, weight_blocks))
    d_scaled = pullback(counts)[0]
    grad_length = lax.optimization_barrier(jnp.sum(d_scaled * branch_rates, axis=(1, 2)))
    d_rates = jnp.einsum('bc,bij->cij', class_pick, d_scaled * lengths[:, None, None], precision=lax.Precision.HIGHEST)
    unused_rates, pull_rates = jax.vjp(lambda table, ratio: build_rates(table, codon_freq, ratio)[0], exchanges, omega_ratio)
    grad_exch, grad_omega = pull_rates(d_rates)
    loglik = log_total / SITES / TAXA
    return (grad_exch, grad_omega, grad_length, loglik)
```

```python
import jax
import jax.numpy as jnp
import numpy as np
from jax import lax
from jax.sharding import PartitionSpec as P

LEVELS = 6
LEAF_DEV = 64
EDGES = 127
SLOTS = 128
CLASSES = 8


CODE_TABLE = "FFLLSSSSYYXXCCXWLLLLPPPPHHQQRRRRIIIMTTTTNNKKSSRRVVVVAAAADDEEGGGG"


def codon_tables():
    amino_acid = np.array(list(CODE_TABLE))
    codon_index = np.arange(64)
    digits = np.stack([codon_index // 16, codon_index // 4 % 4, codon_index % 4], 1)
    differ = (digits[:, None, :] != digits[None, :, :]).sum(-1)
    is_sense = amino_acid != "X"
    single = (differ == 1) & is_sense[:, None] & is_sense[None, :]
    nonsyn = single & (amino_acid[:, None] != amino_acid[None, :])
    return (is_sense.astype(np.float32), single.astype(np.float32), nonsyn.astype(np.float32))


def build_rates(exchanges, codon_freq, omega_ratio):
    is_sense, single, nonsyn = codon_tables()
    stationary = codon_freq * is_sense / jnp.sum(codon_freq * is_sense)
    symmetric = 0.5 * (exchanges + exchanges.T)
    factor = 1.0 + nonsyn[None, :, :] * (omega_ratio[:, None, None] - 1.0)
    off_diag = symmetric[None, :, :] * stationary[None, None, :] * factor * single[None, :, :]
    row_total = jnp.sum(off_diag, axis=2)
    mean_rate = jnp.sum(stationary[None, :] * row_total, axis=1)
    identity = jnp.eye(64, dtype=exchanges.dtype)
    rate_matrix = (off_diag - row_total[:, :, None] * identity[None]) / mean_rate[:, None, None]
    return (rate_matrix, stationary)


def product(left, right):
    return jnp.einsum("bij,bjk->bik", left, right, precision=lax.Precision.HIGHEST)


def expm_taylor(scaled):
    reduced = scaled / 16.0
    identity = jnp.eye(64, dtype=scaled.dtype)
    series = jnp.broadcast_to(identity, scaled.shape)
    for degree in range(8, 0, -1):
        series = identity + product(reduced, series) / degree
    for square_step in range(4):
        series = product(series, series)
    return series


def forward(probs, vectors):
    return jnp.einsum("bij,bjs->bis", probs, vectors, precision=lax.Precision.HIGHEST)


def carried(probs, vectors):
    return jnp.einsum("bji,bjs->bis", probs, vectors, precision=lax.Precision.HIGHEST)


def leaf_partials(leaf_states, gap_rows):
    codon_axis = jnp.arange(64, dtype=jnp.int32)
    indicator = (leaf_states[:, None, :] == codon_axis[None, :, None]).astype(jnp.float32)
    return jnp.where(gap_rows[:, None, :] > 0, jnp.float32(1.0), indicator)


def up_pass(probs, leaves):
    levels = [leaves]
    messages = []
    logscale = jnp.zeros(leaves.shape[2:], jnp.float32)
    current = leaves
    for height in range(LEVELS):
        amount = current.shape[0]
        offset = 2 * LEAF_DEV - 2 * amount
        message = forward(probs[offset : offset + amount], current)
        messages.append(message)
        raw_parent = message[0::2] * message[1::2]
        scaling = jnp.sum(raw_parent, axis=1)
        current = raw_parent / scaling[:, None, :]
        logscale = logscale + jnp.sum(jnp.log(scaling), axis=0)
        levels.append(current)
    messages.append(forward(probs[EDGES - 1 : EDGES], current))
    return (levels, messages, logscale)


def root_terms(stationary, top_messages, top_logs):
    members = top_messages.shape[0]
    joint = stationary[:, None] * top_messages[0]
    for member in range(1, members):
        joint = joint * top_messages[member]
    site_ll = jnp.log(jnp.sum(joint, axis=0)) + jnp.sum(top_logs, axis=0)
    above_list = []
    for member in range(members):
        vector = jnp.broadcast_to(stationary[:, None], top_messages.shape[1:])
        for other in range(members):
            if other != member:
                vector = vector * top_messages[other]
        above_list.append(vector)
    return (site_ll, jnp.stack(above_list))


def down_pass(probs, levels, messages, above_top):
    a_list = [above_top]
    current = above_top
    for height in range(LEVELS, 0, -1):
        amount = levels[height].shape[0]
        offset = 2 * LEAF_DEV - 2 * amount
        down_part = carried(probs[offset : offset + amount], current)
        down_part = down_part / jnp.sum(down_part, axis=1, keepdims=True)
        message = messages[height - 1]
        current = jnp.stack([down_part * message[1::2], down_part * message[0::2]], axis=1).reshape(
            message.shape
        )
        a_list.append(current)
    return a_list[::-1]


def weigh(a_list, messages, site_weight, total_sites):
    weighted = []
    for vector, message in zip(a_list, messages):
        likelihood = jnp.sum(vector * message, axis=1)
        weighted.append(vector * (site_weight / (likelihood * total_sites))[:, None, :])
    return weighted


def body(
    states, gap_mask, weights, leaf_order, exchanges, codon_freq, omega_ratio, lengths, classes
):
    site_count = lax.axis_size("site")
    site_pos = lax.axis_index("site")
    subtree = lax.axis_index("branch")
    site_span = states.shape[1]
    total_sites = site_span * site_count
    total_taxa = LEAF_DEV * lax.axis_size("branch")
    rate_matrix, stationary = build_rates(exchanges, codon_freq, omega_ratio)
    slot_len = jnp.concatenate([lengths, jnp.zeros((1,), lengths.dtype)])
    slot_cls = jnp.concatenate([classes, jnp.zeros((1,), jnp.int32)])
    class_pick = (slot_cls[:, None] == jnp.arange(CLASSES, dtype=jnp.int32)[None, :]).astype(
        jnp.float32
    )
    slot_rates = jnp.einsum("bc,cij->bij", class_pick, rate_matrix, precision=lax.Precision.HIGHEST)
    scaled = slot_rates * slot_len[:, None, None]
    per_dev = SLOTS // site_count
    own_start = site_pos * per_dev
    own_scaled = lax.dynamic_slice_in_dim(scaled, own_start, per_dev, 0)
    own_pull = None
    own_probs, own_pull = jax.vjp(expm_taylor, own_scaled)
    probs = lax.all_to_all(
        jnp.broadcast_to(own_probs[None], (site_count,) + own_probs.shape).reshape(
            (site_count * per_dev,) + own_probs.shape[1:]
        ),
        "site",
        0,
        0,
        tiled=True,
    )
    taxon_rows = lax.dynamic_slice_in_dim(leaf_order, subtree * LEAF_DEV, LEAF_DEV, 0)
    leaves = leaf_partials(
        jnp.take(states, taxon_rows, axis=0), jnp.take(gap_mask, taxon_rows, axis=0)
    )
    levels, messages, logscale = up_pass(probs, leaves)
    top_pack = jnp.concatenate([messages[-1][0], logscale[None, :]], axis=0)
    top_all = lax.all_gather(top_pack, "branch", axis=0, tiled=False)
    top_messages, top_logs = top_all[:, :64, :], top_all[:, 64, :]
    site_ll, above_all = root_terms(stationary, top_messages, top_logs)
    site_weight = weights.astype(jnp.float32)
    loglik_part = jnp.sum(site_weight * site_ll)
    above_top = lax.dynamic_slice_in_dim(above_all, subtree, 1, 0)
    a_list = down_pass(probs, levels, messages, above_top)
    weighted = weigh(a_list, messages, site_weight, total_sites)
    padding = jnp.zeros((1, 64, site_span), jnp.float32)
    weighted_all = jnp.concatenate(weighted + [padding], axis=0)
    partial_all = jnp.concatenate(levels + [padding], axis=0)
    part_above = lax.slice_in_dim(weighted_all, 0, lax.axis_size("site") * per_dev, axis=0)
    part_below = lax.slice_in_dim(partial_all, 0, lax.axis_size("site") * per_dev, axis=0)
    part_counts = jnp.einsum("bis,bjs->bij", part_above, part_below, precision=lax.Precision.HIGHEST)
    own_counts = jnp.sum(
        lax.all_to_all(part_counts, "site", 0, 0, tiled=True).reshape((site_count, per_dev, 64, 64)),
        axis=0,
    )
    d_scaled = own_pull(own_counts)[0]
    use_rates = lax.dynamic_slice_in_dim(slot_rates, own_start, per_dev, 0)
    use_len = lax.dynamic_slice_in_dim(slot_len, own_start, per_dev, 0)
    use_pick = lax.dynamic_slice_in_dim(class_pick, own_start, per_dev, 0)
    d_length = jnp.sum(d_scaled * use_rates, axis=(1, 2))
    d_rates = jnp.einsum(
        "bc,bij->cij", use_pick, d_scaled * use_len[:, None, None], precision=lax.Precision.HIGHEST
    )
    unused_rates, pull_rates = jax.vjp(
        lambda table, ratio: build_rates(table, codon_freq, ratio)[0], exchanges, omega_ratio
    )
    d_exch, d_omega = pull_rates(d_rates)
    n_branch = lax.axis_size("branch")
    length_slab = jnp.zeros((n_branch, SLOTS), jnp.float32)
    length_slab = lax.dynamic_update_slice(length_slab, d_length[None, :], (subtree, own_start))
    loglik_keep = jnp.where(subtree == 0, loglik_part, jnp.float32(0.0))
    packed = jnp.concatenate(
        [d_exch.reshape(-1), d_omega, length_slab.reshape(-1), loglik_keep[None]]
    )
    summed = lax.psum(packed, ("site", "branch"))
    grad_exch = summed[: 64 * 64].reshape(64, 64)
    grad_omega = summed[64 * 64 : 64 * 64 + CLASSES]
    length_all = summed[64 * 64 + CLASSES : 64 * 64 + CLASSES + n_branch * SLOTS].reshape(n_branch, SLOTS)
    log_total = summed[64 * 64 + CLASSES + n_branch * SLOTS]
    loglik = log_total / total_sites / total_taxa
    length_out = lax.dynamic_index_in_dim(length_all, subtree, 0, keepdims=False)[:EDGES]
    return (grad_exch, grad_omega, length_out, loglik)


def solution(mesh):
    return jax.shard_map(
        body,
        mesh=mesh,
        in_specs=(
            P(None, "site"),
            P(None, "site"),
            P("site"),
            P(),
            P(),
            P(),
            P(),
            P("branch"),
            P("branch"),
        ),
        out_specs=(P(), P(), P("branch"), P()),
        check_vma=False,
    )
```

```python
import jax
import jax.numpy as jnp
import numpy as np
from jax import lax
from jax.sharding import PartitionSpec as P
from jax.experimental import pallas as pl
from jax.experimental.pallas import tpu as pltpu
import functools

MESH_ID = pl.DeviceIdType.MESH

LEVELS = 6
LEAF_DEV = 64
EDGES = 127
SLOTS = 128
CLASSES = 8


CODE_TABLE = "FFLLSSSSYYXXCCXWLLLLPPPPHHQQRRRRIIIMTTTTNNKKSSRRVVVVAAAADDEEGGGG"


def codon_tables():
    amino_acid = np.array(list(CODE_TABLE))
    codon_index = np.arange(64)
    digits = np.stack([codon_index // 16, codon_index // 4 % 4, codon_index % 4], 1)
    differ = (digits[:, None, :] != digits[None, :, :]).sum(-1)
    is_sense = amino_acid != "X"
    single = (differ == 1) & is_sense[:, None] & is_sense[None, :]
    nonsyn = single & (amino_acid[:, None] != amino_acid[None, :])
    return (is_sense.astype(np.float32), single.astype(np.float32), nonsyn.astype(np.float32))


def build_rates(exchanges, codon_freq, omega_ratio):
    is_sense, single, nonsyn = codon_tables()
    stationary = codon_freq * is_sense / jnp.sum(codon_freq * is_sense)
    symmetric = 0.5 * (exchanges + exchanges.T)
    factor = 1.0 + nonsyn[None, :, :] * (omega_ratio[:, None, None] - 1.0)
    off_diag = symmetric[None, :, :] * stationary[None, None, :] * factor * single[None, :, :]
    row_total = jnp.sum(off_diag, axis=2)
    mean_rate = jnp.sum(stationary[None, :] * row_total, axis=1)
    identity = jnp.eye(64, dtype=exchanges.dtype)
    rate_matrix = (off_diag - row_total[:, :, None] * identity[None]) / mean_rate[:, None, None]
    return (rate_matrix, stationary)


def product(left, right):
    return jnp.einsum("bij,bjk->bik", left, right, precision=lax.Precision.HIGHEST)


def expm_taylor(scaled):
    reduced = scaled / 16.0
    identity = jnp.eye(64, dtype=scaled.dtype)
    series = jnp.broadcast_to(identity, scaled.shape)
    for degree in range(8, 0, -1):
        series = identity + product(reduced, series) / degree
    for square_step in range(4):
        series = product(series, series)
    return series


def forward(probs, vectors):
    return jnp.einsum("bij,bjs->bis", probs, vectors, precision=lax.Precision.HIGHEST)


def carried(probs, vectors):
    return jnp.einsum("bji,bjs->bis", probs, vectors, precision=lax.Precision.HIGHEST)


def leaf_partials(leaf_states, gap_rows):
    codon_axis = jnp.arange(64, dtype=jnp.int32)
    indicator = (leaf_states[:, None, :] == codon_axis[None, :, None]).astype(jnp.float32)
    return jnp.where(gap_rows[:, None, :] > 0, jnp.float32(1.0), indicator)


def up_pass(probs, leaves):
    levels = [leaves]
    messages = []
    logscale = jnp.zeros(leaves.shape[2:], jnp.float32)
    current = leaves
    for height in range(LEVELS):
        amount = current.shape[0]
        offset = 2 * LEAF_DEV - 2 * amount
        message = forward(probs[offset : offset + amount], current)
        messages.append(message)
        raw_parent = message[0::2] * message[1::2]
        scaling = jnp.sum(raw_parent, axis=1)
        current = raw_parent / scaling[:, None, :]
        logscale = logscale + jnp.sum(jnp.log(scaling), axis=0)
        levels.append(current)
    messages.append(forward(probs[EDGES - 1 : EDGES], current))
    return (levels, messages, logscale)


def root_terms(stationary, top_messages, top_logs):
    members = top_messages.shape[0]
    joint = stationary[:, None] * top_messages[0]
    for member in range(1, members):
        joint = joint * top_messages[member]
    site_ll = jnp.log(jnp.sum(joint, axis=0)) + jnp.sum(top_logs, axis=0)
    above_list = []
    for member in range(members):
        vector = jnp.broadcast_to(stationary[:, None], top_messages.shape[1:])
        for other in range(members):
            if other != member:
                vector = vector * top_messages[other]
        above_list.append(vector)
    return (site_ll, jnp.stack(above_list))


def down_pass(probs, levels, messages, above_top):
    a_list = [above_top]
    current = above_top
    for height in range(LEVELS, 0, -1):
        amount = levels[height].shape[0]
        offset = 2 * LEAF_DEV - 2 * amount
        down_part = carried(probs[offset : offset + amount], current)
        down_part = down_part / jnp.sum(down_part, axis=1, keepdims=True)
        message = messages[height - 1]
        current = jnp.stack([down_part * message[1::2], down_part * message[0::2]], axis=1).reshape(
            message.shape
        )
        a_list.append(current)
    return a_list[::-1]


def weigh(a_list, messages, site_weight, total_sites):
    weighted = []
    for vector, message in zip(a_list, messages):
        likelihood = jnp.sum(vector * message, axis=1)
        weighted.append(vector * (site_weight / (likelihood * total_sites))[:, None, :])
    return weighted


def sum_groups(n_site, n_branch):
    s = lax.axis_index("site")
    k = lax.axis_index("branch")
    core = s % 2
    y = (s // 2) % 4
    z = s // 8
    n_z = n_site // 8
    return [
        (2, core, lambda c: (s - core + c, k)),
        (n_branch, k, lambda c: (s, c)),
        (4, y, lambda c: (s - 2 * y + 2 * c, k)),
        (n_z, z, lambda c: (s - 8 * z + 8 * c, k)),
    ]


def allreduce_kernel(n_site, n_branch, x_ref, o_ref, held, send_sems, recv_sems):
    stages = sum_groups(n_site, n_branch)
    barrier = pltpu.get_barrier_semaphore()
    count = 0
    for size, mine, where in stages:
        for d in range(1, size):
            other = lax.rem(mine + d, size)
            pl.semaphore_signal(barrier, inc=1, device_id=where(other), device_id_type=MESH_ID)
            count += 1
    pl.semaphore_wait(barrier, count)
    total = x_ref[...]
    for st, (size, mine, where) in enumerate(stages):
        held[st, mine] = total
        sends = []
        for d in range(1, size):
            other = lax.rem(mine + d, size)
            copy = pltpu.make_async_remote_copy(
                src_ref=held.at[st, mine],
                dst_ref=held.at[st, mine],
                send_sem=send_sems.at[st, other],
                recv_sem=recv_sems.at[st, mine],
                device_id=where(other),
                device_id_type=MESH_ID,
            )
            copy.start()
            sends.append(copy)
        for d in range(1, size):
            other = lax.rem(mine + d, size)
            incoming = pltpu.make_async_remote_copy(
                src_ref=held.at[st, other],
                dst_ref=held.at[st, other],
                send_sem=send_sems.at[st, other],
                recv_sem=recv_sems.at[st, other],
                device_id=where(other),
                device_id_type=MESH_ID,
            )
            incoming.wait_recv()
        for copy in sends:
            copy.wait_send()
        total = held[st, 0]
        for c in range(1, size):
            total = total + held[st, c]
    o_ref[...] = total


def allreduce_all(x, n_site, n_branch):
    rows = x.shape[0]
    return pl.pallas_call(
        functools.partial(allreduce_kernel, n_site, n_branch),
        out_shape=jax.ShapeDtypeStruct(x.shape, jnp.float32),
        in_specs=[pl.BlockSpec(memory_space=pltpu.VMEM)],
        out_specs=pl.BlockSpec(memory_space=pltpu.VMEM),
        scratch_shapes=[
            pltpu.VMEM((4, 4, rows, 128), jnp.float32),
            pltpu.SemaphoreType.DMA((4, 4)),
            pltpu.SemaphoreType.DMA((4, 4)),
        ],
        compiler_params=pltpu.CompilerParams(collective_id=0, has_side_effects=True),
    )(x)


def body(
    states, gap_mask, weights, leaf_order, exchanges, codon_freq, omega_ratio, lengths, classes
):
    site_count = lax.axis_size("site")
    site_pos = lax.axis_index("site")
    subtree = lax.axis_index("branch")
    site_span = states.shape[1]
    total_sites = site_span * site_count
    total_taxa = LEAF_DEV * lax.axis_size("branch")
    rate_matrix, stationary = build_rates(exchanges, codon_freq, omega_ratio)
    slot_len = jnp.concatenate([lengths, jnp.zeros((1,), lengths.dtype)])
    slot_cls = jnp.concatenate([classes, jnp.zeros((1,), jnp.int32)])
    class_pick = (slot_cls[:, None] == jnp.arange(CLASSES, dtype=jnp.int32)[None, :]).astype(
        jnp.float32
    )
    slot_rates = jnp.einsum("bc,cij->bij", class_pick, rate_matrix, precision=lax.Precision.HIGHEST)
    scaled = slot_rates * slot_len[:, None, None]
    per_dev = SLOTS // site_count
    own_start = site_pos * per_dev
    own_scaled = lax.dynamic_slice_in_dim(scaled, own_start, per_dev, 0)
    own_pull = None
    own_probs, own_pull = jax.vjp(expm_taylor, own_scaled)
    probs = lax.all_to_all(
        jnp.broadcast_to(own_probs[None], (site_count,) + own_probs.shape).reshape(
            (site_count * per_dev,) + own_probs.shape[1:]
        ),
        "site",
        0,
        0,
        tiled=True,
    )
    taxon_rows = lax.dynamic_slice_in_dim(leaf_order, subtree * LEAF_DEV, LEAF_DEV, 0)
    leaves = leaf_partials(
        jnp.take(states, taxon_rows, axis=0), jnp.take(gap_mask, taxon_rows, axis=0)
    )
    levels, messages, logscale = up_pass(probs, leaves)
    top_pack = jnp.concatenate([messages[-1][0], logscale[None, :]], axis=0)
    top_all = lax.all_gather(top_pack, "branch", axis=0, tiled=False)
    top_messages, top_logs = top_all[:, :64, :], top_all[:, 64, :]
    site_ll, above_all = root_terms(stationary, top_messages, top_logs)
    site_weight = weights.astype(jnp.float32)
    loglik_part = jnp.sum(site_weight * site_ll)
    above_top = lax.dynamic_slice_in_dim(above_all, subtree, 1, 0)
    a_list = down_pass(probs, levels, messages, above_top)
    weighted = weigh(a_list, messages, site_weight, total_sites)
    padding = jnp.zeros((1, 64, site_span), jnp.float32)
    weighted_all = jnp.concatenate(weighted + [padding], axis=0)
    partial_all = jnp.concatenate(levels + [padding], axis=0)
    part_above = lax.slice_in_dim(weighted_all, 0, lax.axis_size("site") * per_dev, axis=0)
    part_below = lax.slice_in_dim(partial_all, 0, lax.axis_size("site") * per_dev, axis=0)
    part_counts = jnp.einsum("bis,bjs->bij", part_above, part_below, precision=lax.Precision.HIGHEST)
    own_counts = jnp.sum(
        lax.all_to_all(part_counts, "site", 0, 0, tiled=True).reshape((site_count, per_dev, 64, 64)),
        axis=0,
    )
    d_scaled = own_pull(own_counts)[0]
    use_rates = lax.dynamic_slice_in_dim(slot_rates, own_start, per_dev, 0)
    use_len = lax.dynamic_slice_in_dim(slot_len, own_start, per_dev, 0)
    use_pick = lax.dynamic_slice_in_dim(class_pick, own_start, per_dev, 0)
    d_length = jnp.sum(d_scaled * use_rates, axis=(1, 2))
    d_rates = jnp.einsum(
        "bc,bij->cij", use_pick, d_scaled * use_len[:, None, None], precision=lax.Precision.HIGHEST
    )
    unused_rates, pull_rates = jax.vjp(
        lambda table, ratio: build_rates(table, codon_freq, ratio)[0], exchanges, omega_ratio
    )
    d_exch, d_omega = pull_rates(d_rates)
    n_branch = lax.axis_size("branch")
    length_slab = jnp.zeros((n_branch, SLOTS), jnp.float32)
    length_slab = lax.dynamic_update_slice(length_slab, d_length[None, :], (subtree, own_start))
    loglik_keep = jnp.where(subtree == 0, loglik_part, jnp.float32(0.0))
    packed = jnp.concatenate(
        [d_exch.reshape(-1), d_omega, length_slab.reshape(-1), loglik_keep[None]]
    )
    rows = -(-packed.shape[0] // (8 * 128)) * 8
    packed = jnp.pad(packed, (0, rows * 128 - packed.shape[0])).reshape(rows, 128)
    summed = allreduce_all(packed, site_count, n_branch).reshape(-1)
    grad_exch = summed[: 64 * 64].reshape(64, 64)
    grad_omega = summed[64 * 64 : 64 * 64 + CLASSES]
    length_all = summed[64 * 64 + CLASSES : 64 * 64 + CLASSES + n_branch * SLOTS].reshape(n_branch, SLOTS)
    log_total = summed[64 * 64 + CLASSES + n_branch * SLOTS]
    loglik = log_total / total_sites / total_taxa
    length_out = lax.dynamic_index_in_dim(length_all, subtree, 0, keepdims=False)[:EDGES]
    return (grad_exch, grad_omega, length_out, loglik)


def solution(mesh):
    return jax.shard_map(
        body,
        mesh=mesh,
        in_specs=(
            P(None, "site"),
            P(None, "site"),
            P("site"),
            P(),
            P(),
            P(),
            P(),
            P("branch"),
            P("branch"),
        ),
        out_specs=(P(), P(), P("branch"), P()),
        check_vma=False,
    )
```

```python
import jax
import jax.numpy as jnp
import numpy as np
from jax import lax
from jax.sharding import PartitionSpec as P
from jax.experimental import pallas as pl
from jax.experimental.pallas import tpu as pltpu
import functools

MESH_ID = pl.DeviceIdType.MESH

LEVELS = 6
LEAF_DEV = 64
EDGES = 127
SLOTS = 128
CLASSES = 8


CODE_TABLE = "FFLLSSSSYYXXCCXWLLLLPPPPHHQQRRRRIIIMTTTTNNKKSSRRVVVVAAAADDEEGGGG"


def codon_tables():
    amino_acid = np.array(list(CODE_TABLE))
    codon_index = np.arange(64)
    digits = np.stack([codon_index // 16, codon_index // 4 % 4, codon_index % 4], 1)
    differ = (digits[:, None, :] != digits[None, :, :]).sum(-1)
    is_sense = amino_acid != "X"
    single = (differ == 1) & is_sense[:, None] & is_sense[None, :]
    nonsyn = single & (amino_acid[:, None] != amino_acid[None, :])
    return (is_sense.astype(np.float32), single.astype(np.float32), nonsyn.astype(np.float32))


def build_rates(exchanges, codon_freq, omega_ratio):
    is_sense, single, nonsyn = codon_tables()
    stationary = codon_freq * is_sense / jnp.sum(codon_freq * is_sense)
    symmetric = 0.5 * (exchanges + exchanges.T)
    factor = 1.0 + nonsyn[None, :, :] * (omega_ratio[:, None, None] - 1.0)
    off_diag = symmetric[None, :, :] * stationary[None, None, :] * factor * single[None, :, :]
    row_total = jnp.sum(off_diag, axis=2)
    mean_rate = jnp.sum(stationary[None, :] * row_total, axis=1)
    identity = jnp.eye(64, dtype=exchanges.dtype)
    rate_matrix = (off_diag - row_total[:, :, None] * identity[None]) / mean_rate[:, None, None]
    return (rate_matrix, stationary)


def product(left, right):
    return jnp.einsum("bij,bjk->bik", left, right, precision=lax.Precision.HIGHEST)


def expm_taylor(scaled):
    reduced = scaled / 16.0
    identity = jnp.eye(64, dtype=scaled.dtype)
    series = jnp.broadcast_to(identity, scaled.shape)
    for degree in range(8, 0, -1):
        series = identity + product(reduced, series) / degree
    for square_step in range(4):
        series = product(series, series)
    return series


def forward(probs, vectors):
    return jnp.einsum("bij,bjs->bis", probs, vectors, precision=lax.Precision.HIGHEST)


def carried(probs, vectors):
    return jnp.einsum("bji,bjs->bis", probs, vectors, precision=lax.Precision.HIGHEST)


def leaf_partials(leaf_states, gap_rows):
    codon_axis = jnp.arange(64, dtype=jnp.int32)
    indicator = (leaf_states[:, None, :] == codon_axis[None, :, None]).astype(jnp.float32)
    return jnp.where(gap_rows[:, None, :] > 0, jnp.float32(1.0), indicator)


def up_pass(probs, leaves):
    levels = [leaves]
    messages = []
    logscale = jnp.zeros(leaves.shape[2:], jnp.float32)
    current = leaves
    for height in range(LEVELS):
        amount = current.shape[0]
        offset = 2 * LEAF_DEV - 2 * amount
        message = forward(probs[offset : offset + amount], current)
        messages.append(message)
        raw_parent = message[0::2] * message[1::2]
        scaling = jnp.sum(raw_parent, axis=1)
        current = raw_parent / scaling[:, None, :]
        logscale = logscale + jnp.sum(jnp.log(scaling), axis=0)
        levels.append(current)
    messages.append(forward(probs[EDGES - 1 : EDGES], current))
    return (levels, messages, logscale)


def root_terms(stationary, top_messages, top_logs):
    members = top_messages.shape[0]
    joint = stationary[:, None] * top_messages[0]
    for member in range(1, members):
        joint = joint * top_messages[member]
    site_ll = jnp.log(jnp.sum(joint, axis=0)) + jnp.sum(top_logs, axis=0)
    above_list = []
    for member in range(members):
        vector = jnp.broadcast_to(stationary[:, None], top_messages.shape[1:])
        for other in range(members):
            if other != member:
                vector = vector * top_messages[other]
        above_list.append(vector)
    return (site_ll, jnp.stack(above_list))


def down_pass(probs, levels, messages, above_top):
    a_list = [above_top]
    current = above_top
    for height in range(LEVELS, 0, -1):
        amount = levels[height].shape[0]
        offset = 2 * LEAF_DEV - 2 * amount
        down_part = carried(probs[offset : offset + amount], current)
        down_part = down_part / jnp.sum(down_part, axis=1, keepdims=True)
        message = messages[height - 1]
        current = jnp.stack([down_part * message[1::2], down_part * message[0::2]], axis=1).reshape(
            message.shape
        )
        a_list.append(current)
    return a_list[::-1]


def weigh(a_list, messages, site_weight, total_sites):
    weighted = []
    for vector, message in zip(a_list, messages):
        likelihood = jnp.sum(vector * message, axis=1)
        weighted.append(vector * (site_weight / (likelihood * total_sites))[:, None, :])
    return weighted


def sum_groups(n_site, n_branch):
    s = lax.axis_index("site")
    k = lax.axis_index("branch")
    core = s % 2
    y = (s // 2) % 4
    z = s // 8
    n_z = n_site // 8
    return [
        (2, core, lambda c: (s - core + c, k)),
        (n_branch, k, lambda c: (s, c)),
        (4, y, lambda c: (s - 2 * y + 2 * c, k)),
        (n_z, z, lambda c: (s - 8 * z + 8 * c, k)),
    ]


def allreduce_kernel(n_site, n_branch, x_ref, o_ref, held, send_sems, recv_sems):
    stages = sum_groups(n_site, n_branch)
    barrier = pltpu.get_barrier_semaphore()
    count = 0
    for size, mine, where in stages:
        for d in range(1, size):
            other = lax.rem(mine + d, size)
            pl.semaphore_signal(barrier, inc=1, device_id=where(other), device_id_type=MESH_ID)
            count += 1
    pl.semaphore_wait(barrier, count)
    total = x_ref[...]
    for st, (size, mine, where) in enumerate(stages):
        held[st, mine] = total
        sends = []
        for d in range(1, size):
            other = lax.rem(mine + d, size)
            copy = pltpu.make_async_remote_copy(
                src_ref=held.at[st, mine],
                dst_ref=held.at[st, mine],
                send_sem=send_sems.at[st, other],
                recv_sem=recv_sems.at[st, mine],
                device_id=where(other),
                device_id_type=MESH_ID,
            )
            copy.start()
            sends.append(copy)
        for d in range(1, size):
            other = lax.rem(mine + d, size)
            incoming = pltpu.make_async_remote_copy(
                src_ref=held.at[st, other],
                dst_ref=held.at[st, other],
                send_sem=send_sems.at[st, other],
                recv_sem=recv_sems.at[st, other],
                device_id=where(other),
                device_id_type=MESH_ID,
            )
            incoming.wait_recv()
        for copy in sends:
            copy.wait_send()
        total = held[st, 0]
        for c in range(1, size):
            total = total + held[st, c]
    o_ref[...] = total


def allreduce_all(x, n_site, n_branch):
    rows = x.shape[0]
    return pl.pallas_call(
        functools.partial(allreduce_kernel, n_site, n_branch),
        out_shape=jax.ShapeDtypeStruct(x.shape, jnp.float32),
        in_specs=[pl.BlockSpec(memory_space=pltpu.VMEM)],
        out_specs=pl.BlockSpec(memory_space=pltpu.VMEM),
        scratch_shapes=[
            pltpu.VMEM((4, 4, rows, 128), jnp.float32),
            pltpu.SemaphoreType.DMA((4, 4)),
            pltpu.SemaphoreType.DMA((4, 4)),
        ],
        compiler_params=pltpu.CompilerParams(collective_id=0, has_side_effects=True),
    )(x)


def exchange_kernel(axis, gather, x_ref, o_ref, held, send_sems, recv_sems):
    n = held.shape[0]
    me = lax.axis_index(axis)
    other_axis = "branch" if axis == "site" else "site"
    fixed = lax.axis_index(other_axis)

    def device(p):
        return (p, fixed) if axis == "site" else (fixed, p)

    barrier = pltpu.get_barrier_semaphore()

    def greet(d, carry):
        pl.semaphore_signal(
            barrier, inc=1, device_id=device(lax.rem(me + d, n)), device_id_type=MESH_ID
        )
        return carry

    lax.fori_loop(1, n, greet, 0)
    pl.semaphore_wait(barrier, n - 1)
    if gather:
        held[me] = x_ref[...]
    else:
        held[me] = x_ref[me]

    def outgoing(d):
        p = lax.rem(me + d, n)
        return pltpu.make_async_remote_copy(
            src_ref=x_ref if gather else x_ref.at[p],
            dst_ref=held.at[me],
            send_sem=send_sems.at[p],
            recv_sem=recv_sems.at[me],
            device_id=device(p),
            device_id_type=MESH_ID,
        )

    def send(d, carry):
        outgoing(d).start()
        return carry

    lax.fori_loop(1, n, send, 0)

    def receive(d, carry):
        p = lax.rem(me + n - d, n)
        pltpu.make_async_remote_copy(
            src_ref=held.at[p],
            dst_ref=held.at[p],
            send_sem=send_sems.at[p],
            recv_sem=recv_sems.at[p],
            device_id=device(p),
            device_id_type=MESH_ID,
        ).wait_recv()
        return carry

    lax.fori_loop(1, n, receive, 0)

    def sent(d, carry):
        outgoing(d).wait_send()
        return carry

    lax.fori_loop(1, n, sent, 0)
    if gather:
        o_ref[...] = held[...]
    else:
        o_ref[...] = lax.fori_loop(1, n, lambda j, acc: acc + held[j], held[0])


def exchange(x, axis, n, gather, collective_id):
    chunk = x.shape if gather else x.shape[1:]
    out_shape = (n,) + chunk if gather else chunk
    return pl.pallas_call(
        functools.partial(exchange_kernel, axis, gather),
        out_shape=jax.ShapeDtypeStruct(out_shape, jnp.float32),
        in_specs=[pl.BlockSpec(memory_space=pltpu.VMEM)],
        out_specs=pl.BlockSpec(memory_space=pltpu.VMEM),
        scratch_shapes=[
            pltpu.VMEM((n,) + chunk, jnp.float32),
            pltpu.SemaphoreType.DMA((n,)),
            pltpu.SemaphoreType.DMA((n,)),
        ],
        compiler_params=pltpu.CompilerParams(collective_id=collective_id, has_side_effects=True),
    )(x)


def body(
    states, gap_mask, weights, leaf_order, exchanges, codon_freq, omega_ratio, lengths, classes
):
    site_count = lax.axis_size("site")
    site_pos = lax.axis_index("site")
    subtree = lax.axis_index("branch")
    site_span = states.shape[1]
    total_sites = site_span * site_count
    total_taxa = LEAF_DEV * lax.axis_size("branch")
    rate_matrix, stationary = build_rates(exchanges, codon_freq, omega_ratio)
    slot_len = jnp.concatenate([lengths, jnp.zeros((1,), lengths.dtype)])
    slot_cls = jnp.concatenate([classes, jnp.zeros((1,), jnp.int32)])
    class_pick = (slot_cls[:, None] == jnp.arange(CLASSES, dtype=jnp.int32)[None, :]).astype(
        jnp.float32
    )
    slot_rates = jnp.einsum("bc,cij->bij", class_pick, rate_matrix, precision=lax.Precision.HIGHEST)
    scaled = slot_rates * slot_len[:, None, None]
    per_dev = SLOTS // site_count
    own_start = site_pos * per_dev
    own_scaled = lax.dynamic_slice_in_dim(scaled, own_start, per_dev, 0)
    own_pull = None
    own_probs, own_pull = jax.vjp(expm_taylor, own_scaled)
    dense = exchange(own_probs.reshape(-1, 128), "site", site_count, True, 1)
    probs = dense.reshape((site_count * per_dev,) + own_probs.shape[1:])
    taxon_rows = lax.dynamic_slice_in_dim(leaf_order, subtree * LEAF_DEV, LEAF_DEV, 0)
    leaves = leaf_partials(
        jnp.take(states, taxon_rows, axis=0), jnp.take(gap_mask, taxon_rows, axis=0)
    )
    levels, messages, logscale = up_pass(probs, leaves)
    top_pack = jnp.concatenate([messages[-1][0], logscale[None, :]], axis=0)
    top_all = exchange(top_pack, "branch", lax.axis_size("branch"), True, 3)
    top_messages, top_logs = top_all[:, :64, :], top_all[:, 64, :]
    site_ll, above_all = root_terms(stationary, top_messages, top_logs)
    site_weight = weights.astype(jnp.float32)
    loglik_part = jnp.sum(site_weight * site_ll)
    above_top = lax.dynamic_slice_in_dim(above_all, subtree, 1, 0)
    a_list = down_pass(probs, levels, messages, above_top)
    weighted = weigh(a_list, messages, site_weight, total_sites)
    padding = jnp.zeros((1, 64, site_span), jnp.float32)
    weighted_all = jnp.concatenate(weighted + [padding], axis=0)
    partial_all = jnp.concatenate(levels + [padding], axis=0)
    part_above = lax.slice_in_dim(weighted_all, 0, lax.axis_size("site") * per_dev, axis=0)
    part_below = lax.slice_in_dim(partial_all, 0, lax.axis_size("site") * per_dev, axis=0)
    part_counts = jnp.einsum("bis,bjs->bij", part_above, part_below, precision=lax.Precision.HIGHEST)
    own_counts = exchange(
        part_counts.reshape(site_count, -1, 128), "site", site_count, False, 2
    ).reshape((per_dev, 64, 64))
    d_scaled = own_pull(own_counts)[0]
    use_rates = lax.dynamic_slice_in_dim(slot_rates, own_start, per_dev, 0)
    use_len = lax.dynamic_slice_in_dim(slot_len, own_start, per_dev, 0)
    use_pick = lax.dynamic_slice_in_dim(class_pick, own_start, per_dev, 0)
    d_length = jnp.sum(d_scaled * use_rates, axis=(1, 2))
    d_rates = jnp.einsum(
        "bc,bij->cij", use_pick, d_scaled * use_len[:, None, None], precision=lax.Precision.HIGHEST
    )
    unused_rates, pull_rates = jax.vjp(
        lambda table, ratio: build_rates(table, codon_freq, ratio)[0], exchanges, omega_ratio
    )
    d_exch, d_omega = pull_rates(d_rates)
    n_branch = lax.axis_size("branch")
    length_slab = jnp.zeros((n_branch, SLOTS), jnp.float32)
    length_slab = lax.dynamic_update_slice(length_slab, d_length[None, :], (subtree, own_start))
    loglik_keep = jnp.where(subtree == 0, loglik_part, jnp.float32(0.0))
    packed = jnp.concatenate(
        [d_exch.reshape(-1), d_omega, length_slab.reshape(-1), loglik_keep[None]]
    )
    rows = -(-packed.shape[0] // (8 * 128)) * 8
    packed = jnp.pad(packed, (0, rows * 128 - packed.shape[0])).reshape(rows, 128)
    summed = allreduce_all(packed, site_count, n_branch).reshape(-1)
    grad_exch = summed[: 64 * 64].reshape(64, 64)
    grad_omega = summed[64 * 64 : 64 * 64 + CLASSES]
    length_all = summed[64 * 64 + CLASSES : 64 * 64 + CLASSES + n_branch * SLOTS].reshape(n_branch, SLOTS)
    log_total = summed[64 * 64 + CLASSES + n_branch * SLOTS]
    loglik = log_total / total_sites / total_taxa
    length_out = lax.dynamic_index_in_dim(length_all, subtree, 0, keepdims=False)[:EDGES]
    return (grad_exch, grad_omega, length_out, loglik)


def solution(mesh):
    return jax.shard_map(
        body,
        mesh=mesh,
        in_specs=(
            P(None, "site"),
            P(None, "site"),
            P("site"),
            P(),
            P(),
            P(),
            P(),
            P("branch"),
            P("branch"),
        ),
        out_specs=(P(), P(), P("branch"), P()),
        check_vma=False,
    )
```

```python
import jax
import jax.numpy as jnp
import numpy as np
from jax import lax
from jax.sharding import PartitionSpec as P
from jax.experimental import pallas as pl
from jax.experimental.pallas import tpu as pltpu
import functools

MESH_ID = pl.DeviceIdType.MESH

LEVELS = 6
LEAF_DEV = 64
EDGES = 127
SLOTS = 128
CLASSES = 8


CODE_TABLE = "FFLLSSSSYYXXCCXWLLLLPPPPHHQQRRRRIIIMTTTTNNKKSSRRVVVVAAAADDEEGGGG"


def codon_tables():
    amino_acid = np.array(list(CODE_TABLE))
    codon_index = np.arange(64)
    digits = np.stack([codon_index // 16, codon_index // 4 % 4, codon_index % 4], 1)
    differ = (digits[:, None, :] != digits[None, :, :]).sum(-1)
    is_sense = amino_acid != "X"
    single = (differ == 1) & is_sense[:, None] & is_sense[None, :]
    nonsyn = single & (amino_acid[:, None] != amino_acid[None, :])
    return (is_sense.astype(np.float32), single.astype(np.float32), nonsyn.astype(np.float32))


def build_rates(exchanges, codon_freq, omega_ratio):
    is_sense, single, nonsyn = codon_tables()
    stationary = codon_freq * is_sense / jnp.sum(codon_freq * is_sense)
    symmetric = 0.5 * (exchanges + exchanges.T)
    factor = 1.0 + nonsyn[None, :, :] * (omega_ratio[:, None, None] - 1.0)
    off_diag = symmetric[None, :, :] * stationary[None, None, :] * factor * single[None, :, :]
    row_total = jnp.sum(off_diag, axis=2)
    mean_rate = jnp.sum(stationary[None, :] * row_total, axis=1)
    identity = jnp.eye(64, dtype=exchanges.dtype)
    rate_matrix = (off_diag - row_total[:, :, None] * identity[None]) / mean_rate[:, None, None]
    return (rate_matrix, stationary)


def product(left, right):
    return jnp.einsum("bij,bjk->bik", left, right, precision=lax.Precision.HIGHEST)


def expm_taylor(scaled):
    reduced = scaled / 16.0
    identity = jnp.eye(64, dtype=scaled.dtype)
    series = jnp.broadcast_to(identity, scaled.shape)
    for degree in range(8, 0, -1):
        series = identity + product(reduced, series) / degree
    for square_step in range(4):
        series = product(series, series)
    return series


def forward(probs, vectors):
    return jnp.einsum("bij,bjs->bis", probs, vectors, precision=lax.Precision.HIGHEST)


def carried(probs, vectors):
    return jnp.einsum("bji,bjs->bis", probs, vectors, precision=lax.Precision.HIGHEST)


def leaf_partials(leaf_states, gap_rows):
    codon_axis = jnp.arange(64, dtype=jnp.int32)
    indicator = (leaf_states[:, None, :] == codon_axis[None, :, None]).astype(jnp.float32)
    return jnp.where(gap_rows[:, None, :] > 0, jnp.float32(1.0), indicator)


def up_pass(probs, leaves):
    levels = [leaves]
    messages = []
    logscale = jnp.zeros(leaves.shape[2:], jnp.float32)
    current = leaves
    for height in range(LEVELS):
        amount = current.shape[0]
        offset = 2 * LEAF_DEV - 2 * amount
        message = forward(probs[offset : offset + amount], current)
        messages.append(message)
        raw_parent = message[0::2] * message[1::2]
        scaling = jnp.sum(raw_parent, axis=1)
        current = raw_parent / scaling[:, None, :]
        logscale = logscale + jnp.sum(jnp.log(scaling), axis=0)
        levels.append(current)
    messages.append(forward(probs[EDGES - 1 : EDGES], current))
    return (levels, messages, logscale)


def root_terms(stationary, top_messages, top_logs):
    members = top_messages.shape[0]
    joint = stationary[:, None] * top_messages[0]
    for member in range(1, members):
        joint = joint * top_messages[member]
    site_ll = jnp.log(jnp.sum(joint, axis=0)) + jnp.sum(top_logs, axis=0)
    above_list = []
    for member in range(members):
        vector = jnp.broadcast_to(stationary[:, None], top_messages.shape[1:])
        for other in range(members):
            if other != member:
                vector = vector * top_messages[other]
        above_list.append(vector)
    return (site_ll, jnp.stack(above_list))


def down_pass(probs, levels, messages, above_top):
    a_list = [above_top]
    current = above_top
    for height in range(LEVELS, 0, -1):
        amount = levels[height].shape[0]
        offset = 2 * LEAF_DEV - 2 * amount
        down_part = carried(probs[offset : offset + amount], current)
        down_part = down_part / jnp.sum(down_part, axis=1, keepdims=True)
        message = messages[height - 1]
        current = jnp.stack([down_part * message[1::2], down_part * message[0::2]], axis=1).reshape(
            message.shape
        )
        a_list.append(current)
    return a_list[::-1]


def weigh(a_list, messages, site_weight, total_sites):
    weighted = []
    for vector, message in zip(a_list, messages):
        likelihood = jnp.sum(vector * message, axis=1)
        weighted.append(vector * (site_weight / (likelihood * total_sites))[:, None, :])
    return weighted


def sum_groups(n_site, n_branch):
    s = lax.axis_index("site")
    k = lax.axis_index("branch")
    core = s % 2
    y = (s // 2) % 4
    z = s // 8
    n_z = n_site // 8
    return [
        (2, core, lambda c: (s - core + c, k)),
        (n_branch, k, lambda c: (s, c)),
        (4, y, lambda c: (s - 2 * y + 2 * c, k)),
        (n_z, z, lambda c: (s - 8 * z + 8 * c, k)),
    ]


def allreduce_kernel(n_site, n_branch, x_ref, o_ref, held, send_sems, recv_sems):
    stages = sum_groups(n_site, n_branch)
    barrier = pltpu.get_barrier_semaphore()
    count = 0
    for size, mine, where in stages:
        for d in range(1, size):
            other = lax.rem(mine + d, size)
            pl.semaphore_signal(barrier, inc=1, device_id=where(other), device_id_type=MESH_ID)
            count += 1
    pl.semaphore_wait(barrier, count)
    total = x_ref[...]
    for st, (size, mine, where) in enumerate(stages):
        held[st, mine] = total
        sends = []
        for d in range(1, size):
            other = lax.rem(mine + d, size)
            copy = pltpu.make_async_remote_copy(
                src_ref=held.at[st, mine],
                dst_ref=held.at[st, mine],
                send_sem=send_sems.at[st, other],
                recv_sem=recv_sems.at[st, mine],
                device_id=where(other),
                device_id_type=MESH_ID,
            )
            copy.start()
            sends.append(copy)
        for d in range(1, size):
            other = lax.rem(mine + d, size)
            incoming = pltpu.make_async_remote_copy(
                src_ref=held.at[st, other],
                dst_ref=held.at[st, other],
                send_sem=send_sems.at[st, other],
                recv_sem=recv_sems.at[st, other],
                device_id=where(other),
                device_id_type=MESH_ID,
            )
            incoming.wait_recv()
        for copy in sends:
            copy.wait_send()
        total = held[st, 0]
        for c in range(1, size):
            total = total + held[st, c]
    o_ref[...] = total


def allreduce_all(x, n_site, n_branch):
    rows = x.shape[0]
    return pl.pallas_call(
        functools.partial(allreduce_kernel, n_site, n_branch),
        out_shape=jax.ShapeDtypeStruct(x.shape, jnp.float32),
        in_specs=[pl.BlockSpec(memory_space=pltpu.VMEM)],
        out_specs=pl.BlockSpec(memory_space=pltpu.VMEM),
        scratch_shapes=[
            pltpu.VMEM((4, 4, rows, 128), jnp.float32),
            pltpu.SemaphoreType.DMA((4, 4)),
            pltpu.SemaphoreType.DMA((4, 4)),
        ],
        compiler_params=pltpu.CompilerParams(collective_id=0, has_side_effects=True),
    )(x)


def exchange_kernel(axis, gather, x_ref, o_ref, held, send_sems, recv_sems):
    n = held.shape[0]
    me = lax.axis_index(axis)
    other_axis = "branch" if axis == "site" else "site"
    fixed = lax.axis_index(other_axis)

    def device(p):
        return (p, fixed) if axis == "site" else (fixed, p)

    barrier = pltpu.get_barrier_semaphore()

    def greet(d, carry):
        pl.semaphore_signal(
            barrier, inc=1, device_id=device(lax.rem(me + d, n)), device_id_type=MESH_ID
        )
        return carry

    lax.fori_loop(1, n, greet, 0)
    pl.semaphore_wait(barrier, n - 1)
    if gather:
        held[me] = x_ref[...]
    else:
        held[me] = x_ref[me]

    def outgoing(d):
        p = lax.rem(me + d, n)
        return pltpu.make_async_remote_copy(
            src_ref=x_ref if gather else x_ref.at[p],
            dst_ref=held.at[me],
            send_sem=send_sems.at[p],
            recv_sem=recv_sems.at[me],
            device_id=device(p),
            device_id_type=MESH_ID,
        )

    def send(d, carry):
        outgoing(d).start()
        return carry

    lax.fori_loop(1, n, send, 0)

    def receive(d, carry):
        p = lax.rem(me + n - d, n)
        pltpu.make_async_remote_copy(
            src_ref=held.at[p],
            dst_ref=held.at[p],
            send_sem=send_sems.at[p],
            recv_sem=recv_sems.at[p],
            device_id=device(p),
            device_id_type=MESH_ID,
        ).wait_recv()
        return carry

    lax.fori_loop(1, n, receive, 0)

    def sent(d, carry):
        outgoing(d).wait_send()
        return carry

    lax.fori_loop(1, n, sent, 0)
    if gather:
        o_ref[...] = held[...]
    else:
        o_ref[...] = lax.fori_loop(1, n, lambda j, acc: acc + held[j], held[0])


def exchange(x, axis, n, gather, collective_id):
    chunk = x.shape if gather else x.shape[1:]
    out_shape = (n,) + chunk if gather else chunk
    return pl.pallas_call(
        functools.partial(exchange_kernel, axis, gather),
        out_shape=jax.ShapeDtypeStruct(out_shape, jnp.float32),
        in_specs=[pl.BlockSpec(memory_space=pltpu.VMEM)],
        out_specs=pl.BlockSpec(memory_space=pltpu.VMEM),
        scratch_shapes=[
            pltpu.VMEM((n,) + chunk, jnp.float32),
            pltpu.SemaphoreType.DMA((n,)),
            pltpu.SemaphoreType.DMA((n,)),
        ],
        compiler_params=pltpu.CompilerParams(collective_id=collective_id, has_side_effects=True),
    )(x)


def body(
    states, gap_mask, weights, leaf_order, exchanges, codon_freq, omega_ratio, lengths, classes
):
    site_count = lax.axis_size("site")
    site_pos = lax.axis_index("site")
    subtree = lax.axis_index("branch")
    site_span = states.shape[1]
    total_sites = site_span * site_count
    total_taxa = LEAF_DEV * lax.axis_size("branch")
    rate_matrix, stationary = build_rates(exchanges, codon_freq, omega_ratio)
    slot_len = jnp.concatenate([lengths, jnp.zeros((1,), lengths.dtype)])
    slot_cls = jnp.concatenate([classes, jnp.zeros((1,), jnp.int32)])
    class_pick = (slot_cls[:, None] == jnp.arange(CLASSES, dtype=jnp.int32)[None, :]).astype(
        jnp.float32
    )
    slot_rates = jnp.einsum("bc,cij->bij", class_pick, rate_matrix, precision=lax.Precision.HIGHEST)
    scaled = slot_rates * slot_len[:, None, None]
    per_dev = SLOTS // site_count
    own_start = site_pos * per_dev
    own_scaled = lax.dynamic_slice_in_dim(scaled, own_start, per_dev, 0)
    own_pull = None
    own_probs, own_pull = jax.vjp(expm_taylor, own_scaled)
    probs = lax.all_to_all(
        jnp.broadcast_to(own_probs[None], (site_count,) + own_probs.shape).reshape(
            (site_count * per_dev,) + own_probs.shape[1:]
        ),
        "site",
        0,
        0,
        tiled=True,
    )
    taxon_rows = lax.dynamic_slice_in_dim(leaf_order, subtree * LEAF_DEV, LEAF_DEV, 0)
    leaves = leaf_partials(
        jnp.take(states, taxon_rows, axis=0), jnp.take(gap_mask, taxon_rows, axis=0)
    )
    levels, messages, logscale = up_pass(probs, leaves)
    top_pack = jnp.concatenate([messages[-1][0], logscale[None, :]], axis=0)
    top_all = lax.all_gather(top_pack, "branch", axis=0, tiled=False)
    top_messages, top_logs = top_all[:, :64, :], top_all[:, 64, :]
    site_ll, above_all = root_terms(stationary, top_messages, top_logs)
    site_weight = weights.astype(jnp.float32)
    loglik_part = jnp.sum(site_weight * site_ll)
    above_top = lax.dynamic_slice_in_dim(above_all, subtree, 1, 0)
    a_list = down_pass(probs, levels, messages, above_top)
    weighted = weigh(a_list, messages, site_weight, total_sites)
    padding = jnp.zeros((1, 64, site_span), jnp.float32)
    weighted_all = jnp.concatenate(weighted + [padding], axis=0)
    partial_all = jnp.concatenate(levels + [padding], axis=0)
    part_above = lax.slice_in_dim(weighted_all, 0, lax.axis_size("site") * per_dev, axis=0)
    part_below = lax.slice_in_dim(partial_all, 0, lax.axis_size("site") * per_dev, axis=0)
    part_counts = jnp.einsum("bis,bjs->bij", part_above, part_below, precision=lax.Precision.HIGHEST)
    own_counts = exchange(
        part_counts.reshape(site_count, -1, 128), "site", site_count, False, 2
    ).reshape((per_dev, 64, 64))
    d_scaled = own_pull(own_counts)[0]
    use_rates = lax.dynamic_slice_in_dim(slot_rates, own_start, per_dev, 0)
    use_len = lax.dynamic_slice_in_dim(slot_len, own_start, per_dev, 0)
    use_pick = lax.dynamic_slice_in_dim(class_pick, own_start, per_dev, 0)
    d_length = jnp.sum(d_scaled * use_rates, axis=(1, 2))
    d_rates = jnp.einsum(
        "bc,bij->cij", use_pick, d_scaled * use_len[:, None, None], precision=lax.Precision.HIGHEST
    )
    unused_rates, pull_rates = jax.vjp(
        lambda table, ratio: build_rates(table, codon_freq, ratio)[0], exchanges, omega_ratio
    )
    d_exch, d_omega = pull_rates(d_rates)
    n_branch = lax.axis_size("branch")
    length_slab = jnp.zeros((n_branch, SLOTS), jnp.float32)
    length_slab = lax.dynamic_update_slice(length_slab, d_length[None, :], (subtree, own_start))
    loglik_keep = jnp.where(subtree == 0, loglik_part, jnp.float32(0.0))
    packed = jnp.concatenate(
        [d_exch.reshape(-1), d_omega, length_slab.reshape(-1), loglik_keep[None]]
    )
    rows = -(-packed.shape[0] // (8 * 128)) * 8
    packed = jnp.pad(packed, (0, rows * 128 - packed.shape[0])).reshape(rows, 128)
    summed = allreduce_all(packed, site_count, n_branch).reshape(-1)
    grad_exch = summed[: 64 * 64].reshape(64, 64)
    grad_omega = summed[64 * 64 : 64 * 64 + CLASSES]
    length_all = summed[64 * 64 + CLASSES : 64 * 64 + CLASSES + n_branch * SLOTS].reshape(n_branch, SLOTS)
    log_total = summed[64 * 64 + CLASSES + n_branch * SLOTS]
    loglik = log_total / total_sites / total_taxa
    length_out = lax.dynamic_index_in_dim(length_all, subtree, 0, keepdims=False)[:EDGES]
    return (grad_exch, grad_omega, length_out, loglik)


def solution(mesh):
    return jax.shard_map(
        body,
        mesh=mesh,
        in_specs=(
            P(None, "site"),
            P(None, "site"),
            P("site"),
            P(),
            P(),
            P(),
            P(),
            P("branch"),
            P("branch"),
        ),
        out_specs=(P(), P(), P("branch"), P()),
        check_vma=False,
    )
```

```python
import jax
import jax.numpy as jnp
import numpy as np
from jax import lax
from jax.sharding import PartitionSpec as P
from jax.experimental import pallas as pl
from jax.experimental.pallas import tpu as pltpu
import functools

MESH_ID = pl.DeviceIdType.MESH

LEVELS = 6
LEAF_DEV = 64
EDGES = 127
SLOTS = 128
CLASSES = 8


CODE_TABLE = "FFLLSSSSYYXXCCXWLLLLPPPPHHQQRRRRIIIMTTTTNNKKSSRRVVVVAAAADDEEGGGG"


def codon_tables():
    amino_acid = np.array(list(CODE_TABLE))
    codon_index = np.arange(64)
    digits = np.stack([codon_index // 16, codon_index // 4 % 4, codon_index % 4], 1)
    differ = (digits[:, None, :] != digits[None, :, :]).sum(-1)
    is_sense = amino_acid != "X"
    single = (differ == 1) & is_sense[:, None] & is_sense[None, :]
    nonsyn = single & (amino_acid[:, None] != amino_acid[None, :])
    return (is_sense.astype(np.float32), single.astype(np.float32), nonsyn.astype(np.float32))


def build_rates(exchanges, codon_freq, omega_ratio):
    is_sense, single, nonsyn = codon_tables()
    stationary = codon_freq * is_sense / jnp.sum(codon_freq * is_sense)
    symmetric = 0.5 * (exchanges + exchanges.T)
    factor = 1.0 + nonsyn[None, :, :] * (omega_ratio[:, None, None] - 1.0)
    off_diag = symmetric[None, :, :] * stationary[None, None, :] * factor * single[None, :, :]
    row_total = jnp.sum(off_diag, axis=2)
    mean_rate = jnp.sum(stationary[None, :] * row_total, axis=1)
    identity = jnp.eye(64, dtype=exchanges.dtype)
    rate_matrix = (off_diag - row_total[:, :, None] * identity[None]) / mean_rate[:, None, None]
    return (rate_matrix, stationary)


def product(left, right):
    return jnp.einsum("bij,bjk->bik", left, right, precision=lax.Precision.HIGH)


def expm_taylor(scaled):
    reduced = scaled / 16.0
    identity = jnp.eye(64, dtype=scaled.dtype)
    series = jnp.broadcast_to(identity, scaled.shape)
    for degree in range(8, 0, -1):
        series = identity + product(reduced, series) / degree
    for square_step in range(4):
        series = product(series, series)
    return series


def forward(probs, vectors):
    return jnp.einsum("bij,bjs->bis", probs, vectors, precision=lax.Precision.HIGH)


def carried(probs, vectors):
    return jnp.einsum("bji,bjs->bis", probs, vectors, precision=lax.Precision.HIGH)


def leaf_partials(leaf_states, gap_rows):
    codon_axis = jnp.arange(64, dtype=jnp.int32)
    indicator = (leaf_states[:, None, :] == codon_axis[None, :, None]).astype(jnp.float32)
    return jnp.where(gap_rows[:, None, :] > 0, jnp.float32(1.0), indicator)


def up_pass(probs, leaves):
    levels = [leaves]
    messages = []
    logscale = jnp.zeros(leaves.shape[2:], jnp.float32)
    current = leaves
    for height in range(LEVELS):
        amount = current.shape[0]
        offset = 2 * LEAF_DEV - 2 * amount
        message = forward(probs[offset : offset + amount], current)
        messages.append(message)
        raw_parent = message[0::2] * message[1::2]
        scaling = jnp.sum(raw_parent, axis=1)
        current = raw_parent / scaling[:, None, :]
        logscale = logscale + jnp.sum(jnp.log(scaling), axis=0)
        levels.append(current)
    messages.append(forward(probs[EDGES - 1 : EDGES], current))
    return (levels, messages, logscale)


def root_terms(stationary, top_messages, top_logs):
    members = top_messages.shape[0]
    joint = stationary[:, None] * top_messages[0]
    for member in range(1, members):
        joint = joint * top_messages[member]
    site_ll = jnp.log(jnp.sum(joint, axis=0)) + jnp.sum(top_logs, axis=0)
    above_list = []
    for member in range(members):
        vector = jnp.broadcast_to(stationary[:, None], top_messages.shape[1:])
        for other in range(members):
            if other != member:
                vector = vector * top_messages[other]
        above_list.append(vector)
    return (site_ll, jnp.stack(above_list))


def down_pass(probs, levels, messages, above_top):
    a_list = [above_top]
    current = above_top
    for height in range(LEVELS, 0, -1):
        amount = levels[height].shape[0]
        offset = 2 * LEAF_DEV - 2 * amount
        down_part = carried(probs[offset : offset + amount], current)
        down_part = down_part / jnp.sum(down_part, axis=1, keepdims=True)
        message = messages[height - 1]
        current = jnp.stack([down_part * message[1::2], down_part * message[0::2]], axis=1).reshape(
            message.shape
        )
        a_list.append(current)
    return a_list[::-1]


def weigh(a_list, messages, site_weight, total_sites):
    weighted = []
    for vector, message in zip(a_list, messages):
        likelihood = jnp.sum(vector * message, axis=1)
        weighted.append(vector * (site_weight / (likelihood * total_sites))[:, None, :])
    return weighted


def sum_groups(n_site, n_branch):
    s = lax.axis_index("site")
    k = lax.axis_index("branch")
    core = s % 2
    y = (s // 2) % 4
    z = s // 8
    n_z = n_site // 8
    return [
        (2, core, lambda c: (s - core + c, k)),
        (n_branch, k, lambda c: (s, c)),
        (4, y, lambda c: (s - 2 * y + 2 * c, k)),
        (n_z, z, lambda c: (s - 8 * z + 8 * c, k)),
    ]


def allreduce_kernel(n_site, n_branch, x_ref, o_ref, held, send_sems, recv_sems):
    stages = sum_groups(n_site, n_branch)
    barrier = pltpu.get_barrier_semaphore()
    count = 0
    for size, mine, where in stages:
        for d in range(1, size):
            other = lax.rem(mine + d, size)
            pl.semaphore_signal(barrier, inc=1, device_id=where(other), device_id_type=MESH_ID)
            count += 1
    pl.semaphore_wait(barrier, count)
    total = x_ref[...]
    for st, (size, mine, where) in enumerate(stages):
        held[st, mine] = total
        sends = []
        for d in range(1, size):
            other = lax.rem(mine + d, size)
            copy = pltpu.make_async_remote_copy(
                src_ref=held.at[st, mine],
                dst_ref=held.at[st, mine],
                send_sem=send_sems.at[st, other],
                recv_sem=recv_sems.at[st, mine],
                device_id=where(other),
                device_id_type=MESH_ID,
            )
            copy.start()
            sends.append(copy)
        for d in range(1, size):
            other = lax.rem(mine + d, size)
            incoming = pltpu.make_async_remote_copy(
                src_ref=held.at[st, other],
                dst_ref=held.at[st, other],
                send_sem=send_sems.at[st, other],
                recv_sem=recv_sems.at[st, other],
                device_id=where(other),
                device_id_type=MESH_ID,
            )
            incoming.wait_recv()
        for copy in sends:
            copy.wait_send()
        total = held[st, 0]
        for c in range(1, size):
            total = total + held[st, c]
    o_ref[...] = total


def allreduce_all(x, n_site, n_branch):
    rows = x.shape[0]
    return pl.pallas_call(
        functools.partial(allreduce_kernel, n_site, n_branch),
        out_shape=jax.ShapeDtypeStruct(x.shape, jnp.float32),
        in_specs=[pl.BlockSpec(memory_space=pltpu.VMEM)],
        out_specs=pl.BlockSpec(memory_space=pltpu.VMEM),
        scratch_shapes=[
            pltpu.VMEM((4, 4, rows, 128), jnp.float32),
            pltpu.SemaphoreType.DMA((4, 4)),
            pltpu.SemaphoreType.DMA((4, 4)),
        ],
        compiler_params=pltpu.CompilerParams(collective_id=0, has_side_effects=True),
    )(x)


def exchange_kernel(axis, gather, x_ref, o_ref, held, send_sems, recv_sems):
    n = held.shape[0]
    me = lax.axis_index(axis)
    other_axis = "branch" if axis == "site" else "site"
    fixed = lax.axis_index(other_axis)

    def device(p):
        return (p, fixed) if axis == "site" else (fixed, p)

    barrier = pltpu.get_barrier_semaphore()

    def greet(d, carry):
        pl.semaphore_signal(
            barrier, inc=1, device_id=device(lax.rem(me + d, n)), device_id_type=MESH_ID
        )
        return carry

    lax.fori_loop(1, n, greet, 0)
    pl.semaphore_wait(barrier, n - 1)
    if gather:
        held[me] = x_ref[...]
    else:
        held[me] = x_ref[me]

    def outgoing(d):
        p = lax.rem(me + d, n)
        return pltpu.make_async_remote_copy(
            src_ref=x_ref if gather else x_ref.at[p],
            dst_ref=held.at[me],
            send_sem=send_sems.at[p],
            recv_sem=recv_sems.at[me],
            device_id=device(p),
            device_id_type=MESH_ID,
        )

    def send(d, carry):
        outgoing(d).start()
        return carry

    lax.fori_loop(1, n, send, 0)

    def receive(d, carry):
        p = lax.rem(me + n - d, n)
        pltpu.make_async_remote_copy(
            src_ref=held.at[p],
            dst_ref=held.at[p],
            send_sem=send_sems.at[p],
            recv_sem=recv_sems.at[p],
            device_id=device(p),
            device_id_type=MESH_ID,
        ).wait_recv()
        return carry

    lax.fori_loop(1, n, receive, 0)

    def sent(d, carry):
        outgoing(d).wait_send()
        return carry

    lax.fori_loop(1, n, sent, 0)
    if gather:
        o_ref[...] = held[...]
    else:
        o_ref[...] = lax.fori_loop(1, n, lambda j, acc: acc + held[j], held[0])


def exchange(x, axis, n, gather, collective_id):
    chunk = x.shape if gather else x.shape[1:]
    out_shape = (n,) + chunk if gather else chunk
    return pl.pallas_call(
        functools.partial(exchange_kernel, axis, gather),
        out_shape=jax.ShapeDtypeStruct(out_shape, jnp.float32),
        in_specs=[pl.BlockSpec(memory_space=pltpu.VMEM)],
        out_specs=pl.BlockSpec(memory_space=pltpu.VMEM),
        scratch_shapes=[
            pltpu.VMEM((n,) + chunk, jnp.float32),
            pltpu.SemaphoreType.DMA((n,)),
            pltpu.SemaphoreType.DMA((n,)),
        ],
        compiler_params=pltpu.CompilerParams(collective_id=collective_id, has_side_effects=True),
    )(x)


def body(
    states, gap_mask, weights, leaf_order, exchanges, codon_freq, omega_ratio, lengths, classes
):
    site_count = lax.axis_size("site")
    site_pos = lax.axis_index("site")
    subtree = lax.axis_index("branch")
    site_span = states.shape[1]
    total_sites = site_span * site_count
    total_taxa = LEAF_DEV * lax.axis_size("branch")
    rate_matrix, stationary = build_rates(exchanges, codon_freq, omega_ratio)
    slot_len = jnp.concatenate([lengths, jnp.zeros((1,), lengths.dtype)])
    slot_cls = jnp.concatenate([classes, jnp.zeros((1,), jnp.int32)])
    class_pick = (slot_cls[:, None] == jnp.arange(CLASSES, dtype=jnp.int32)[None, :]).astype(
        jnp.float32
    )
    slot_rates = jnp.einsum("bc,cij->bij", class_pick, rate_matrix, precision=lax.Precision.HIGH)
    scaled = slot_rates * slot_len[:, None, None]
    per_dev = SLOTS // site_count
    own_start = site_pos * per_dev
    own_scaled = lax.dynamic_slice_in_dim(scaled, own_start, per_dev, 0)
    own_pull = None
    own_probs, own_pull = jax.vjp(expm_taylor, own_scaled)
    probs = lax.all_to_all(
        jnp.broadcast_to(own_probs[None], (site_count,) + own_probs.shape).reshape(
            (site_count * per_dev,) + own_probs.shape[1:]
        ),
        "site",
        0,
        0,
        tiled=True,
    )
    taxon_rows = lax.dynamic_slice_in_dim(leaf_order, subtree * LEAF_DEV, LEAF_DEV, 0)
    leaves = leaf_partials(
        jnp.take(states, taxon_rows, axis=0), jnp.take(gap_mask, taxon_rows, axis=0)
    )
    levels, messages, logscale = up_pass(probs, leaves)
    top_pack = jnp.concatenate([messages[-1][0], logscale[None, :]], axis=0)
    top_all = lax.all_gather(top_pack, "branch", axis=0, tiled=False)
    top_messages, top_logs = top_all[:, :64, :], top_all[:, 64, :]
    site_ll, above_all = root_terms(stationary, top_messages, top_logs)
    site_weight = weights.astype(jnp.float32)
    loglik_part = jnp.sum(site_weight * site_ll)
    above_top = lax.dynamic_slice_in_dim(above_all, subtree, 1, 0)
    a_list = down_pass(probs, levels, messages, above_top)
    weighted = weigh(a_list, messages, site_weight, total_sites)
    padding = jnp.zeros((1, 64, site_span), jnp.float32)
    weighted_all = jnp.concatenate(weighted + [padding], axis=0)
    partial_all = jnp.concatenate(levels + [padding], axis=0)
    part_above = lax.slice_in_dim(weighted_all, 0, lax.axis_size("site") * per_dev, axis=0)
    part_below = lax.slice_in_dim(partial_all, 0, lax.axis_size("site") * per_dev, axis=0)
    part_counts = jnp.einsum("bis,bjs->bij", part_above, part_below, precision=lax.Precision.HIGH)
    own_counts = exchange(
        part_counts.reshape(site_count, -1, 128), "site", site_count, False, 2
    ).reshape((per_dev, 64, 64))
    d_scaled = own_pull(own_counts)[0]
    use_rates = lax.dynamic_slice_in_dim(slot_rates, own_start, per_dev, 0)
    use_len = lax.dynamic_slice_in_dim(slot_len, own_start, per_dev, 0)
    use_pick = lax.dynamic_slice_in_dim(class_pick, own_start, per_dev, 0)
    d_length = jnp.sum(d_scaled * use_rates, axis=(1, 2))
    d_rates = jnp.einsum(
        "bc,bij->cij", use_pick, d_scaled * use_len[:, None, None], precision=lax.Precision.HIGH
    )
    unused_rates, pull_rates = jax.vjp(
        lambda table, ratio: build_rates(table, codon_freq, ratio)[0], exchanges, omega_ratio
    )
    d_exch, d_omega = pull_rates(d_rates)
    n_branch = lax.axis_size("branch")
    length_slab = jnp.zeros((n_branch, SLOTS), jnp.float32)
    length_slab = lax.dynamic_update_slice(length_slab, d_length[None, :], (subtree, own_start))
    loglik_keep = jnp.where(subtree == 0, loglik_part, jnp.float32(0.0))
    packed = jnp.concatenate(
        [d_exch.reshape(-1), d_omega, length_slab.reshape(-1), loglik_keep[None]]
    )
    rows = -(-packed.shape[0] // (8 * 128)) * 8
    packed = jnp.pad(packed, (0, rows * 128 - packed.shape[0])).reshape(rows, 128)
    summed = allreduce_all(packed, site_count, n_branch).reshape(-1)
    grad_exch = summed[: 64 * 64].reshape(64, 64)
    grad_omega = summed[64 * 64 : 64 * 64 + CLASSES]
    length_all = summed[64 * 64 + CLASSES : 64 * 64 + CLASSES + n_branch * SLOTS].reshape(n_branch, SLOTS)
    log_total = summed[64 * 64 + CLASSES + n_branch * SLOTS]
    loglik = log_total / total_sites / total_taxa
    length_out = lax.dynamic_index_in_dim(length_all, subtree, 0, keepdims=False)[:EDGES]
    return (grad_exch, grad_omega, length_out, loglik)


def solution(mesh):
    return jax.shard_map(
        body,
        mesh=mesh,
        in_specs=(
            P(None, "site"),
            P(None, "site"),
            P("site"),
            P(),
            P(),
            P(),
            P(),
            P("branch"),
            P("branch"),
        ),
        out_specs=(P(), P(), P("branch"), P()),
        check_vma=False,
    )
```

```python
import jax
import jax.numpy as jnp
import numpy as np
from jax import lax
from jax.sharding import PartitionSpec as P
from jax.experimental import pallas as pl
from jax.experimental.pallas import tpu as pltpu
import functools

MESH_ID = pl.DeviceIdType.MESH

LEVELS = 6
LEAF_DEV = 64
EDGES = 127
SLOTS = 128
CLASSES = 8


CODE_TABLE = "FFLLSSSSYYXXCCXWLLLLPPPPHHQQRRRRIIIMTTTTNNKKSSRRVVVVAAAADDEEGGGG"


def codon_tables():
    amino_acid = np.array(list(CODE_TABLE))
    codon_index = np.arange(64)
    digits = np.stack([codon_index // 16, codon_index // 4 % 4, codon_index % 4], 1)
    differ = (digits[:, None, :] != digits[None, :, :]).sum(-1)
    is_sense = amino_acid != "X"
    single = (differ == 1) & is_sense[:, None] & is_sense[None, :]
    nonsyn = single & (amino_acid[:, None] != amino_acid[None, :])
    return (is_sense.astype(np.float32), single.astype(np.float32), nonsyn.astype(np.float32))


def build_rates(exchanges, codon_freq, omega_ratio):
    is_sense, single, nonsyn = codon_tables()
    stationary = codon_freq * is_sense / jnp.sum(codon_freq * is_sense)
    symmetric = 0.5 * (exchanges + exchanges.T)
    factor = 1.0 + nonsyn[None, :, :] * (omega_ratio[:, None, None] - 1.0)
    off_diag = symmetric[None, :, :] * stationary[None, None, :] * factor * single[None, :, :]
    row_total = jnp.sum(off_diag, axis=2)
    mean_rate = jnp.sum(stationary[None, :] * row_total, axis=1)
    identity = jnp.eye(64, dtype=exchanges.dtype)
    rate_matrix = (off_diag - row_total[:, :, None] * identity[None]) / mean_rate[:, None, None]
    return (rate_matrix, stationary)


def product(left, right):
    return jnp.einsum("bij,bjk->bik", left, right, precision=lax.Precision.HIGH)


def expm_taylor(scaled):
    reduced = scaled / 16.0
    identity = jnp.eye(64, dtype=scaled.dtype)
    series = jnp.broadcast_to(identity, scaled.shape)
    for degree in range(8, 0, -1):
        series = identity + product(reduced, series) / degree
    for square_step in range(4):
        series = product(series, series)
    return series


def forward(probs, vectors):
    return jnp.einsum("bij,bjs->bis", probs, vectors, precision=lax.Precision.HIGH)


def carried(probs, vectors):
    return jnp.einsum("bji,bjs->bis", probs, vectors, precision=lax.Precision.HIGH)


def leaf_partials(leaf_states, gap_rows):
    codon_axis = jnp.arange(64, dtype=jnp.int32)
    indicator = (leaf_states[:, None, :] == codon_axis[None, :, None]).astype(jnp.float32)
    return jnp.where(gap_rows[:, None, :] > 0, jnp.float32(1.0), indicator)


def up_pass(probs, leaves):
    levels = [leaves]
    messages = []
    logscale = jnp.zeros(leaves.shape[2:], jnp.float32)
    current = leaves
    for height in range(LEVELS):
        amount = current.shape[0]
        offset = 2 * LEAF_DEV - 2 * amount
        message = forward(probs[offset : offset + amount], current)
        messages.append(message)
        raw_parent = message[0::2] * message[1::2]
        scaling = jnp.sum(raw_parent, axis=1)
        current = raw_parent / scaling[:, None, :]
        logscale = logscale + jnp.sum(jnp.log(scaling), axis=0)
        levels.append(current)
    messages.append(forward(probs[EDGES - 1 : EDGES], current))
    return (levels, messages, logscale)


def root_terms(stationary, top_messages, top_logs):
    members = top_messages.shape[0]
    joint = stationary[:, None] * top_messages[0]
    for member in range(1, members):
        joint = joint * top_messages[member]
    site_ll = jnp.log(jnp.sum(joint, axis=0)) + jnp.sum(top_logs, axis=0)
    above_list = []
    for member in range(members):
        vector = jnp.broadcast_to(stationary[:, None], top_messages.shape[1:])
        for other in range(members):
            if other != member:
                vector = vector * top_messages[other]
        above_list.append(vector)
    return (site_ll, jnp.stack(above_list))


def down_pass(probs, levels, messages, above_top):
    a_list = [above_top]
    current = above_top
    for height in range(LEVELS, 0, -1):
        amount = levels[height].shape[0]
        offset = 2 * LEAF_DEV - 2 * amount
        down_part = carried(probs[offset : offset + amount], current)
        down_part = down_part / jnp.sum(down_part, axis=1, keepdims=True)
        message = messages[height - 1]
        current = jnp.stack([down_part * message[1::2], down_part * message[0::2]], axis=1).reshape(
            message.shape
        )
        a_list.append(current)
    return a_list[::-1]


def weigh(a_list, messages, site_weight, total_sites):
    weighted = []
    for vector, message in zip(a_list, messages):
        likelihood = jnp.sum(vector * message, axis=1)
        weighted.append(vector * (site_weight / (likelihood * total_sites))[:, None, :])
    return weighted


def sum_groups(n_site, n_branch):
    s = lax.axis_index("site")
    k = lax.axis_index("branch")
    core = s % 2
    y = (s // 2) % 4
    z = s // 8
    n_z = n_site // 8
    return [
        (2, core, lambda c: (s - core + c, k)),
        (n_branch, k, lambda c: (s, c)),
        (4, y, lambda c: (s - 2 * y + 2 * c, k)),
        (n_z, z, lambda c: (s - 8 * z + 8 * c, k)),
    ]


def allreduce_kernel(n_site, n_branch, x_ref, o_ref, held, send_sems, recv_sems):
    stages = sum_groups(n_site, n_branch)
    barrier = pltpu.get_barrier_semaphore()
    count = 0
    for size, mine, where in stages:
        for d in range(1, size):
            other = lax.rem(mine + d, size)
            pl.semaphore_signal(barrier, inc=1, device_id=where(other), device_id_type=MESH_ID)
            count += 1
    pl.semaphore_wait(barrier, count)
    total = x_ref[...]
    for st, (size, mine, where) in enumerate(stages):
        held[st, mine] = total
        sends = []
        for d in range(1, size):
            other = lax.rem(mine + d, size)
            copy = pltpu.make_async_remote_copy(
                src_ref=held.at[st, mine],
                dst_ref=held.at[st, mine],
                send_sem=send_sems.at[st, other],
                recv_sem=recv_sems.at[st, mine],
                device_id=where(other),
                device_id_type=MESH_ID,
            )
            copy.start()
            sends.append(copy)
        for d in range(1, size):
            other = lax.rem(mine + d, size)
            incoming = pltpu.make_async_remote_copy(
                src_ref=held.at[st, other],
                dst_ref=held.at[st, other],
                send_sem=send_sems.at[st, other],
                recv_sem=recv_sems.at[st, other],
                device_id=where(other),
                device_id_type=MESH_ID,
            )
            incoming.wait_recv()
        for copy in sends:
            copy.wait_send()
        total = held[st, 0]
        for c in range(1, size):
            total = total + held[st, c]
    o_ref[...] = total


def allreduce_all(x, n_site, n_branch):
    rows = x.shape[0]
    return pl.pallas_call(
        functools.partial(allreduce_kernel, n_site, n_branch),
        out_shape=jax.ShapeDtypeStruct(x.shape, jnp.float32),
        in_specs=[pl.BlockSpec(memory_space=pltpu.VMEM)],
        out_specs=pl.BlockSpec(memory_space=pltpu.VMEM),
        scratch_shapes=[
            pltpu.VMEM((4, 4, rows, 128), jnp.float32),
            pltpu.SemaphoreType.DMA((4, 4)),
            pltpu.SemaphoreType.DMA((4, 4)),
        ],
        compiler_params=pltpu.CompilerParams(collective_id=0, has_side_effects=True),
    )(x)


def exchange_kernel(axis, gather, x_ref, o_ref, held, send_sems, recv_sems):
    n = held.shape[0]
    me = lax.axis_index(axis)
    other_axis = "branch" if axis == "site" else "site"
    fixed = lax.axis_index(other_axis)

    def device(p):
        return (p, fixed) if axis == "site" else (fixed, p)

    barrier = pltpu.get_barrier_semaphore()

    def greet(d, carry):
        pl.semaphore_signal(
            barrier, inc=1, device_id=device(lax.rem(me + d, n)), device_id_type=MESH_ID
        )
        return carry

    lax.fori_loop(1, n, greet, 0)
    pl.semaphore_wait(barrier, n - 1)
    if gather:
        held[me] = x_ref[...]
    else:
        held[me] = x_ref[me]

    def outgoing(d):
        p = lax.rem(me + d, n)
        return pltpu.make_async_remote_copy(
            src_ref=x_ref if gather else x_ref.at[p],
            dst_ref=held.at[me],
            send_sem=send_sems.at[p],
            recv_sem=recv_sems.at[me],
            device_id=device(p),
            device_id_type=MESH_ID,
        )

    def send(d, carry):
        outgoing(d).start()
        return carry

    lax.fori_loop(1, n, send, 0)

    def receive(d, carry):
        p = lax.rem(me + n - d, n)
        pltpu.make_async_remote_copy(
            src_ref=held.at[p],
            dst_ref=held.at[p],
            send_sem=send_sems.at[p],
            recv_sem=recv_sems.at[p],
            device_id=device(p),
            device_id_type=MESH_ID,
        ).wait_recv()
        return carry

    lax.fori_loop(1, n, receive, 0)

    def sent(d, carry):
        outgoing(d).wait_send()
        return carry

    lax.fori_loop(1, n, sent, 0)
    if gather:
        o_ref[...] = held[...]
    else:
        o_ref[...] = lax.fori_loop(1, n, lambda j, acc: acc + held[j], held[0])


def exchange(x, axis, n, gather, collective_id):
    chunk = x.shape if gather else x.shape[1:]
    out_shape = (n,) + chunk if gather else chunk
    return pl.pallas_call(
        functools.partial(exchange_kernel, axis, gather),
        out_shape=jax.ShapeDtypeStruct(out_shape, jnp.float32),
        in_specs=[pl.BlockSpec(memory_space=pltpu.VMEM)],
        out_specs=pl.BlockSpec(memory_space=pltpu.VMEM),
        scratch_shapes=[
            pltpu.VMEM((n,) + chunk, jnp.float32),
            pltpu.SemaphoreType.DMA((n,)),
            pltpu.SemaphoreType.DMA((n,)),
        ],
        compiler_params=pltpu.CompilerParams(collective_id=collective_id, has_side_effects=True),
    )(x)


def pair_scatter_kernel(x_ref, o_ref, pair_buf, pair_sum, held, sems_a, sems_b, sems_c, sems_d):
    n = x_ref.shape[0]
    chips = n // 2
    s = lax.axis_index("site")
    k = lax.axis_index("branch")
    core = s % 2
    chip = s // 2
    partner = s - core + (1 - core)
    barrier = pltpu.get_barrier_semaphore()
    pl.semaphore_signal(barrier, inc=1, device_id=(partner, k), device_id_type=MESH_ID)

    def greet(d, carry):
        peer = 2 * lax.rem(chip + d, chips) + core
        pl.semaphore_signal(barrier, inc=1, device_id=(peer, k), device_id_type=MESH_ID)
        return carry

    lax.fori_loop(1, chips, greet, 0)
    pl.semaphore_wait(barrier, chips)

    def to_partner(m):
        return pltpu.make_async_remote_copy(
            src_ref=x_ref.at[2 * m + 1 - core],
            dst_ref=pair_buf.at[m],
            send_sem=sems_a.at[m],
            recv_sem=sems_b.at[m],
            device_id=(partner, k),
            device_id_type=MESH_ID,
        )

    def first_send(m, carry):
        to_partner(m).start()
        return carry

    lax.fori_loop(0, chips, first_send, 0)

    def first_recv(m, carry):
        to_partner(m).wait_recv()
        return carry

    lax.fori_loop(0, chips, first_recv, 0)

    def first_sent(m, carry):
        to_partner(m).wait_send()
        return carry

    lax.fori_loop(0, chips, first_sent, 0)

    def add_pair(m, carry):
        pair_sum[m] = x_ref[2 * m + core] + pair_buf[m]
        return carry

    lax.fori_loop(0, chips, add_pair, 0)
    held[chip] = pair_sum[chip]

    def to_chip(d):
        c = lax.rem(chip + d, chips)
        return pltpu.make_async_remote_copy(
            src_ref=pair_sum.at[c],
            dst_ref=held.at[chip],
            send_sem=sems_c.at[c],
            recv_sem=sems_d.at[chip],
            device_id=(2 * c + core, k),
            device_id_type=MESH_ID,
        )

    def second_send(d, carry):
        to_chip(d).start()
        return carry

    lax.fori_loop(1, chips, second_send, 0)

    def second_recv(d, carry):
        c = lax.rem(chip + chips - d, chips)
        pltpu.make_async_remote_copy(
            src_ref=held.at[c],
            dst_ref=held.at[c],
            send_sem=sems_c.at[c],
            recv_sem=sems_d.at[c],
            device_id=(2 * c + core, k),
            device_id_type=MESH_ID,
        ).wait_recv()
        return carry

    lax.fori_loop(1, chips, second_recv, 0)

    def second_sent(d, carry):
        to_chip(d).wait_send()
        return carry

    lax.fori_loop(1, chips, second_sent, 0)
    o_ref[...] = lax.fori_loop(1, chips, lambda j, acc: acc + held[j], held[0])


def pair_scatter(x, collective_id):
    n = x.shape[0]
    chunk = x.shape[1:]
    return pl.pallas_call(
        pair_scatter_kernel,
        out_shape=jax.ShapeDtypeStruct(chunk, jnp.float32),
        in_specs=[pl.BlockSpec(memory_space=pltpu.VMEM)],
        out_specs=pl.BlockSpec(memory_space=pltpu.VMEM),
        scratch_shapes=[
            pltpu.VMEM((n // 2,) + chunk, jnp.float32),
            pltpu.VMEM((n // 2,) + chunk, jnp.float32),
            pltpu.VMEM((n // 2,) + chunk, jnp.float32),
            pltpu.SemaphoreType.DMA((n // 2,)),
            pltpu.SemaphoreType.DMA((n // 2,)),
            pltpu.SemaphoreType.DMA((n // 2,)),
            pltpu.SemaphoreType.DMA((n // 2,)),
        ],
        compiler_params=pltpu.CompilerParams(collective_id=collective_id, has_side_effects=True),
    )(x)


def body(
    states, gap_mask, weights, leaf_order, exchanges, codon_freq, omega_ratio, lengths, classes
):
    site_count = lax.axis_size("site")
    site_pos = lax.axis_index("site")
    subtree = lax.axis_index("branch")
    site_span = states.shape[1]
    total_sites = site_span * site_count
    total_taxa = LEAF_DEV * lax.axis_size("branch")
    rate_matrix, stationary = build_rates(exchanges, codon_freq, omega_ratio)
    slot_len = jnp.concatenate([lengths, jnp.zeros((1,), lengths.dtype)])
    slot_cls = jnp.concatenate([classes, jnp.zeros((1,), jnp.int32)])
    class_pick = (slot_cls[:, None] == jnp.arange(CLASSES, dtype=jnp.int32)[None, :]).astype(
        jnp.float32
    )
    slot_rates = jnp.einsum("bc,cij->bij", class_pick, rate_matrix, precision=lax.Precision.HIGH)
    scaled = slot_rates * slot_len[:, None, None]
    per_dev = SLOTS // site_count
    own_start = site_pos * per_dev
    own_scaled = lax.dynamic_slice_in_dim(scaled, own_start, per_dev, 0)
    own_pull = None
    own_probs, own_pull = jax.vjp(expm_taylor, own_scaled)
    probs = lax.all_to_all(
        jnp.broadcast_to(own_probs[None], (site_count,) + own_probs.shape).reshape(
            (site_count * per_dev,) + own_probs.shape[1:]
        ),
        "site",
        0,
        0,
        tiled=True,
    )
    taxon_rows = lax.dynamic_slice_in_dim(leaf_order, subtree * LEAF_DEV, LEAF_DEV, 0)
    leaves = leaf_partials(
        jnp.take(states, taxon_rows, axis=0), jnp.take(gap_mask, taxon_rows, axis=0)
    )
    levels, messages, logscale = up_pass(probs, leaves)
    top_pack = jnp.concatenate([messages[-1][0], logscale[None, :]], axis=0)
    top_all = lax.all_gather(top_pack, "branch", axis=0, tiled=False)
    top_messages, top_logs = top_all[:, :64, :], top_all[:, 64, :]
    site_ll, above_all = root_terms(stationary, top_messages, top_logs)
    site_weight = weights.astype(jnp.float32)
    loglik_part = jnp.sum(site_weight * site_ll)
    above_top = lax.dynamic_slice_in_dim(above_all, subtree, 1, 0)
    a_list = down_pass(probs, levels, messages, above_top)
    weighted = weigh(a_list, messages, site_weight, total_sites)
    padding = jnp.zeros((1, 64, site_span), jnp.float32)
    weighted_all = jnp.concatenate(weighted + [padding], axis=0)
    partial_all = jnp.concatenate(levels + [padding], axis=0)
    part_above = lax.slice_in_dim(weighted_all, 0, lax.axis_size("site") * per_dev, axis=0)
    part_below = lax.slice_in_dim(partial_all, 0, lax.axis_size("site") * per_dev, axis=0)
    part_counts = jnp.einsum("bis,bjs->bij", part_above, part_below, precision=lax.Precision.HIGH)
    own_counts = pair_scatter(part_counts.reshape(site_count, -1, 128), 2).reshape((per_dev, 64, 64))
    d_scaled = own_pull(own_counts)[0]
    use_rates = lax.dynamic_slice_in_dim(slot_rates, own_start, per_dev, 0)
    use_len = lax.dynamic_slice_in_dim(slot_len, own_start, per_dev, 0)
    use_pick = lax.dynamic_slice_in_dim(class_pick, own_start, per_dev, 0)
    d_length = jnp.sum(d_scaled * use_rates, axis=(1, 2))
    d_rates = jnp.einsum(
        "bc,bij->cij", use_pick, d_scaled * use_len[:, None, None], precision=lax.Precision.HIGH
    )
    unused_rates, pull_rates = jax.vjp(
        lambda table, ratio: build_rates(table, codon_freq, ratio)[0], exchanges, omega_ratio
    )
    d_exch, d_omega = pull_rates(d_rates)
    n_branch = lax.axis_size("branch")
    length_slab = jnp.zeros((n_branch, SLOTS), jnp.float32)
    length_slab = lax.dynamic_update_slice(length_slab, d_length[None, :], (subtree, own_start))
    loglik_keep = jnp.where(subtree == 0, loglik_part, jnp.float32(0.0))
    packed = jnp.concatenate(
        [d_exch.reshape(-1), d_omega, length_slab.reshape(-1), loglik_keep[None]]
    )
    rows = -(-packed.shape[0] // (8 * 128)) * 8
    packed = jnp.pad(packed, (0, rows * 128 - packed.shape[0])).reshape(rows, 128)
    summed = allreduce_all(packed, site_count, n_branch).reshape(-1)
    grad_exch = summed[: 64 * 64].reshape(64, 64)
    grad_omega = summed[64 * 64 : 64 * 64 + CLASSES]
    length_all = summed[64 * 64 + CLASSES : 64 * 64 + CLASSES + n_branch * SLOTS].reshape(n_branch, SLOTS)
    log_total = summed[64 * 64 + CLASSES + n_branch * SLOTS]
    loglik = log_total / total_sites / total_taxa
    length_out = lax.dynamic_index_in_dim(length_all, subtree, 0, keepdims=False)[:EDGES]
    return (grad_exch, grad_omega, length_out, loglik)


def solution(mesh):
    return jax.shard_map(
        body,
        mesh=mesh,
        in_specs=(
            P(None, "site"),
            P(None, "site"),
            P("site"),
            P(),
            P(),
            P(),
            P(),
            P("branch"),
            P("branch"),
        ),
        out_specs=(P(), P(), P("branch"), P()),
        check_vma=False,
    )
```

```python
import jax
import jax.numpy as jnp
import numpy as np
from jax import lax
from jax.sharding import PartitionSpec as P
from jax.experimental import pallas as pl
from jax.experimental.pallas import tpu as pltpu
import functools

MESH_ID = pl.DeviceIdType.MESH

LEVELS = 6
LEAF_DEV = 64
EDGES = 127
SLOTS = 128
CLASSES = 8


CODE_TABLE = "FFLLSSSSYYXXCCXWLLLLPPPPHHQQRRRRIIIMTTTTNNKKSSRRVVVVAAAADDEEGGGG"


def codon_tables():
    amino_acid = np.array(list(CODE_TABLE))
    codon_index = np.arange(64)
    digits = np.stack([codon_index // 16, codon_index // 4 % 4, codon_index % 4], 1)
    differ = (digits[:, None, :] != digits[None, :, :]).sum(-1)
    is_sense = amino_acid != "X"
    single = (differ == 1) & is_sense[:, None] & is_sense[None, :]
    nonsyn = single & (amino_acid[:, None] != amino_acid[None, :])
    return (is_sense.astype(np.float32), single.astype(np.float32), nonsyn.astype(np.float32))


def build_rates(exchanges, codon_freq, omega_ratio):
    is_sense, single, nonsyn = codon_tables()
    stationary = codon_freq * is_sense / jnp.sum(codon_freq * is_sense)
    symmetric = 0.5 * (exchanges + exchanges.T)
    factor = 1.0 + nonsyn[None, :, :] * (omega_ratio[:, None, None] - 1.0)
    off_diag = symmetric[None, :, :] * stationary[None, None, :] * factor * single[None, :, :]
    row_total = jnp.sum(off_diag, axis=2)
    mean_rate = jnp.sum(stationary[None, :] * row_total, axis=1)
    identity = jnp.eye(64, dtype=exchanges.dtype)
    rate_matrix = (off_diag - row_total[:, :, None] * identity[None]) / mean_rate[:, None, None]
    return (rate_matrix, stationary)


def product(left, right):
    return jnp.einsum("bij,bjk->bik", left, right, precision=lax.Precision.HIGH)


def expm_taylor(scaled):
    reduced = scaled / 16.0
    identity = jnp.eye(64, dtype=scaled.dtype)
    series = jnp.broadcast_to(identity, scaled.shape)
    for degree in range(8, 0, -1):
        series = identity + product(reduced, series) / degree
    for square_step in range(4):
        series = product(series, series)
    return series


def forward(probs, vectors):
    return jnp.einsum("bij,bjs->bis", probs, vectors, precision=lax.Precision.HIGH)


def carried(probs, vectors):
    return jnp.einsum("bji,bjs->bis", probs, vectors, precision=lax.Precision.HIGH)


def leaf_partials(leaf_states, gap_rows):
    codon_axis = jnp.arange(64, dtype=jnp.int32)
    indicator = (leaf_states[:, None, :] == codon_axis[None, :, None]).astype(jnp.float32)
    return jnp.where(gap_rows[:, None, :] > 0, jnp.float32(1.0), indicator)


def up_pass(probs, leaves):
    levels = [leaves]
    messages = []
    logscale = jnp.zeros(leaves.shape[2:], jnp.float32)
    current = leaves
    for height in range(LEVELS):
        amount = current.shape[0]
        offset = 2 * LEAF_DEV - 2 * amount
        message = forward(probs[offset : offset + amount], current)
        messages.append(message)
        raw_parent = message[0::2] * message[1::2]
        scaling = jnp.sum(raw_parent, axis=1)
        current = raw_parent / scaling[:, None, :]
        logscale = logscale + jnp.sum(jnp.log(scaling), axis=0)
        levels.append(current)
    messages.append(forward(probs[EDGES - 1 : EDGES], current))
    return (levels, messages, logscale)


def root_terms(stationary, top_messages, top_logs):
    members = top_messages.shape[0]
    joint = stationary[:, None] * top_messages[0]
    for member in range(1, members):
        joint = joint * top_messages[member]
    site_ll = jnp.log(jnp.sum(joint, axis=0)) + jnp.sum(top_logs, axis=0)
    above_list = []
    for member in range(members):
        vector = jnp.broadcast_to(stationary[:, None], top_messages.shape[1:])
        for other in range(members):
            if other != member:
                vector = vector * top_messages[other]
        above_list.append(vector)
    return (site_ll, jnp.stack(above_list))


def down_pass(probs, levels, messages, above_top):
    a_list = [above_top]
    current = above_top
    for height in range(LEVELS, 0, -1):
        amount = levels[height].shape[0]
        offset = 2 * LEAF_DEV - 2 * amount
        down_part = carried(probs[offset : offset + amount], current)
        down_part = down_part / jnp.sum(down_part, axis=1, keepdims=True)
        message = messages[height - 1]
        current = jnp.stack([down_part * message[1::2], down_part * message[0::2]], axis=1).reshape(
            message.shape
        )
        a_list.append(current)
    return a_list[::-1]


def weigh(a_list, messages, site_weight, total_sites):
    weighted = []
    for vector, message in zip(a_list, messages):
        likelihood = jnp.sum(vector * message, axis=1)
        weighted.append(vector * (site_weight / (likelihood * total_sites))[:, None, :])
    return weighted


def sum_groups(n_site, n_branch):
    s = lax.axis_index("site")
    k = lax.axis_index("branch")
    core = s % 2
    y = (s // 2) % 4
    z = s // 8
    n_z = n_site // 8
    return [
        (2, core, lambda c: (s - core + c, k)),
        (n_branch, k, lambda c: (s, c)),
        (4, y, lambda c: (s - 2 * y + 2 * c, k)),
        (n_z, z, lambda c: (s - 8 * z + 8 * c, k)),
    ]


def allreduce_kernel(n_site, n_branch, x_ref, o_ref, held, send_sems, recv_sems):
    stages = sum_groups(n_site, n_branch)
    barrier = pltpu.get_barrier_semaphore()
    count = 0
    for size, mine, where in stages:
        for d in range(1, size):
            other = lax.rem(mine + d, size)
            pl.semaphore_signal(barrier, inc=1, device_id=where(other), device_id_type=MESH_ID)
            count += 1
    pl.semaphore_wait(barrier, count)
    total = x_ref[...]
    for st, (size, mine, where) in enumerate(stages):
        held[st, mine] = total
        sends = []
        for d in range(1, size):
            other = lax.rem(mine + d, size)
            copy = pltpu.make_async_remote_copy(
                src_ref=held.at[st, mine],
                dst_ref=held.at[st, mine],
                send_sem=send_sems.at[st, other],
                recv_sem=recv_sems.at[st, mine],
                device_id=where(other),
                device_id_type=MESH_ID,
            )
            copy.start()
            sends.append(copy)
        for d in range(1, size):
            other = lax.rem(mine + d, size)
            incoming = pltpu.make_async_remote_copy(
                src_ref=held.at[st, other],
                dst_ref=held.at[st, other],
                send_sem=send_sems.at[st, other],
                recv_sem=recv_sems.at[st, other],
                device_id=where(other),
                device_id_type=MESH_ID,
            )
            incoming.wait_recv()
        for copy in sends:
            copy.wait_send()
        total = held[st, 0]
        for c in range(1, size):
            total = total + held[st, c]
    o_ref[...] = total


def allreduce_all(x, n_site, n_branch):
    rows = x.shape[0]
    return pl.pallas_call(
        functools.partial(allreduce_kernel, n_site, n_branch),
        out_shape=jax.ShapeDtypeStruct(x.shape, jnp.float32),
        in_specs=[pl.BlockSpec(memory_space=pltpu.VMEM)],
        out_specs=pl.BlockSpec(memory_space=pltpu.VMEM),
        scratch_shapes=[
            pltpu.VMEM((4, 4, rows, 128), jnp.float32),
            pltpu.SemaphoreType.DMA((4, 4)),
            pltpu.SemaphoreType.DMA((4, 4)),
        ],
        compiler_params=pltpu.CompilerParams(collective_id=0, has_side_effects=True),
    )(x)


def exchange_kernel(axis, gather, x_ref, o_ref, held, send_sems, recv_sems):
    n = held.shape[0]
    me = lax.axis_index(axis)
    other_axis = "branch" if axis == "site" else "site"
    fixed = lax.axis_index(other_axis)

    def device(p):
        return (p, fixed) if axis == "site" else (fixed, p)

    barrier = pltpu.get_barrier_semaphore()

    def greet(d, carry):
        pl.semaphore_signal(
            barrier, inc=1, device_id=device(lax.rem(me + d, n)), device_id_type=MESH_ID
        )
        return carry

    lax.fori_loop(1, n, greet, 0)
    pl.semaphore_wait(barrier, n - 1)
    if gather:
        held[me] = x_ref[...]
    else:
        held[me] = x_ref[me]

    def outgoing(d):
        p = lax.rem(me + d, n)
        return pltpu.make_async_remote_copy(
            src_ref=x_ref if gather else x_ref.at[p],
            dst_ref=held.at[me],
            send_sem=send_sems.at[p],
            recv_sem=recv_sems.at[me],
            device_id=device(p),
            device_id_type=MESH_ID,
        )

    def send(d, carry):
        outgoing(d).start()
        return carry

    lax.fori_loop(1, n, send, 0)

    def receive(d, carry):
        p = lax.rem(me + n - d, n)
        pltpu.make_async_remote_copy(
            src_ref=held.at[p],
            dst_ref=held.at[p],
            send_sem=send_sems.at[p],
            recv_sem=recv_sems.at[p],
            device_id=device(p),
            device_id_type=MESH_ID,
        ).wait_recv()
        return carry

    lax.fori_loop(1, n, receive, 0)

    def sent(d, carry):
        outgoing(d).wait_send()
        return carry

    lax.fori_loop(1, n, sent, 0)
    if gather:
        o_ref[...] = held[...]
    else:
        o_ref[...] = lax.fori_loop(1, n, lambda j, acc: acc + held[j], held[0])


def exchange(x, axis, n, gather, collective_id):
    chunk = x.shape if gather else x.shape[1:]
    out_shape = (n,) + chunk if gather else chunk
    return pl.pallas_call(
        functools.partial(exchange_kernel, axis, gather),
        out_shape=jax.ShapeDtypeStruct(out_shape, jnp.float32),
        in_specs=[pl.BlockSpec(memory_space=pltpu.VMEM)],
        out_specs=pl.BlockSpec(memory_space=pltpu.VMEM),
        scratch_shapes=[
            pltpu.VMEM((n,) + chunk, jnp.float32),
            pltpu.SemaphoreType.DMA((n,)),
            pltpu.SemaphoreType.DMA((n,)),
        ],
        compiler_params=pltpu.CompilerParams(collective_id=collective_id, has_side_effects=True),
    )(x)


def pair_scatter_kernel(x_ref, o_ref, pair_buf, pair_sum, held, sems_a, sems_b, sems_c, sems_d):
    n = x_ref.shape[0]
    chips = n // 2
    s = lax.axis_index("site")
    k = lax.axis_index("branch")
    core = s % 2
    chip = s // 2
    partner = s - core + (1 - core)
    barrier = pltpu.get_barrier_semaphore()
    pl.semaphore_signal(barrier, inc=1, device_id=(partner, k), device_id_type=MESH_ID)

    def greet(d, carry):
        peer = 2 * lax.rem(chip + d, chips) + core
        pl.semaphore_signal(barrier, inc=1, device_id=(peer, k), device_id_type=MESH_ID)
        return carry

    lax.fori_loop(1, chips, greet, 0)
    pl.semaphore_wait(barrier, chips)

    def to_partner(m):
        return pltpu.make_async_remote_copy(
            src_ref=x_ref.at[2 * m + 1 - core],
            dst_ref=pair_buf.at[m],
            send_sem=sems_a.at[m],
            recv_sem=sems_b.at[m],
            device_id=(partner, k),
            device_id_type=MESH_ID,
        )

    def first_send(m, carry):
        to_partner(m).start()
        return carry

    lax.fori_loop(0, chips, first_send, 0)

    def first_recv(m, carry):
        to_partner(m).wait_recv()
        return carry

    lax.fori_loop(0, chips, first_recv, 0)

    def first_sent(m, carry):
        to_partner(m).wait_send()
        return carry

    lax.fori_loop(0, chips, first_sent, 0)

    def add_pair(m, carry):
        pair_sum[m] = x_ref[2 * m + core] + pair_buf[m]
        return carry

    lax.fori_loop(0, chips, add_pair, 0)
    held[chip] = pair_sum[chip]

    def to_chip(d):
        c = lax.rem(chip + d, chips)
        return pltpu.make_async_remote_copy(
            src_ref=pair_sum.at[c],
            dst_ref=held.at[chip],
            send_sem=sems_c.at[c],
            recv_sem=sems_d.at[chip],
            device_id=(2 * c + core, k),
            device_id_type=MESH_ID,
        )

    def second_send(d, carry):
        to_chip(d).start()
        return carry

    lax.fori_loop(1, chips, second_send, 0)

    def second_recv(d, carry):
        c = lax.rem(chip + chips - d, chips)
        pltpu.make_async_remote_copy(
            src_ref=held.at[c],
            dst_ref=held.at[c],
            send_sem=sems_c.at[c],
            recv_sem=sems_d.at[c],
            device_id=(2 * c + core, k),
            device_id_type=MESH_ID,
        ).wait_recv()
        return carry

    lax.fori_loop(1, chips, second_recv, 0)

    def second_sent(d, carry):
        to_chip(d).wait_send()
        return carry

    lax.fori_loop(1, chips, second_sent, 0)
    o_ref[...] = lax.fori_loop(1, chips, lambda j, acc: acc + held[j], held[0])


def pair_scatter(x, collective_id):
    n = x.shape[0]
    chunk = x.shape[1:]
    return pl.pallas_call(
        pair_scatter_kernel,
        out_shape=jax.ShapeDtypeStruct(chunk, jnp.float32),
        in_specs=[pl.BlockSpec(memory_space=pltpu.VMEM)],
        out_specs=pl.BlockSpec(memory_space=pltpu.VMEM),
        scratch_shapes=[
            pltpu.VMEM((n // 2,) + chunk, jnp.float32),
            pltpu.VMEM((n // 2,) + chunk, jnp.float32),
            pltpu.VMEM((n // 2,) + chunk, jnp.float32),
            pltpu.SemaphoreType.DMA((n // 2,)),
            pltpu.SemaphoreType.DMA((n // 2,)),
            pltpu.SemaphoreType.DMA((n // 2,)),
            pltpu.SemaphoreType.DMA((n // 2,)),
        ],
        compiler_params=pltpu.CompilerParams(collective_id=collective_id, has_side_effects=True),
    )(x)


def pair_gather_kernel(x_ref, o_ref, held, sems_a, sems_b, sems_c, sems_d):
    n = held.shape[0]
    chips = n // 2
    s = lax.axis_index("site")
    k = lax.axis_index("branch")
    core = s % 2
    chip = s // 2
    partner = s - core + (1 - core)
    barrier = pltpu.get_barrier_semaphore()
    pl.semaphore_signal(barrier, inc=1, device_id=(partner, k), device_id_type=MESH_ID)

    def greet(d, carry):
        peer = 2 * lax.rem(chip + d, chips) + core
        pl.semaphore_signal(barrier, inc=1, device_id=(peer, k), device_id_type=MESH_ID)
        return carry

    lax.fori_loop(1, chips, greet, 0)
    pl.semaphore_wait(barrier, chips)
    held[s] = x_ref[...]

    def to_chip(d):
        c = lax.rem(chip + d, chips)
        return pltpu.make_async_remote_copy(
            src_ref=x_ref,
            dst_ref=held.at[s],
            send_sem=sems_a.at[c],
            recv_sem=sems_b.at[chip],
            device_id=(2 * c + core, k),
            device_id_type=MESH_ID,
        )

    def first_send(d, carry):
        to_chip(d).start()
        return carry

    lax.fori_loop(1, chips, first_send, 0)

    def first_recv(d, carry):
        c = lax.rem(chip + chips - d, chips)
        pltpu.make_async_remote_copy(
            src_ref=held.at[2 * c + core],
            dst_ref=held.at[2 * c + core],
            send_sem=sems_a.at[c],
            recv_sem=sems_b.at[c],
            device_id=(2 * c + core, k),
            device_id_type=MESH_ID,
        ).wait_recv()
        return carry

    lax.fori_loop(1, chips, first_recv, 0)

    def to_partner(d):
        c = lax.rem(chip + d, chips)
        return pltpu.make_async_remote_copy(
            src_ref=held.at[2 * c + core],
            dst_ref=held.at[2 * c + core],
            send_sem=sems_c.at[c],
            recv_sem=sems_d.at[c],
            device_id=(partner, k),
            device_id_type=MESH_ID,
        )

    own = pltpu.make_async_remote_copy(
        src_ref=x_ref,
        dst_ref=held.at[s],
        send_sem=sems_c.at[chip],
        recv_sem=sems_d.at[chip],
        device_id=(partner, k),
        device_id_type=MESH_ID,
    )
    own.start()

    def second_send(d, carry):
        to_partner(d).start()
        return carry

    lax.fori_loop(1, chips, second_send, 0)

    def second_recv(c, carry):
        pltpu.make_async_remote_copy(
            src_ref=held.at[2 * c + 1 - core],
            dst_ref=held.at[2 * c + 1 - core],
            send_sem=sems_c.at[c],
            recv_sem=sems_d.at[c],
            device_id=(partner, k),
            device_id_type=MESH_ID,
        ).wait_recv()
        return carry

    lax.fori_loop(0, chips, second_recv, 0)

    def first_sent(d, carry):
        to_chip(d).wait_send()
        return carry

    lax.fori_loop(1, chips, first_sent, 0)
    own.wait_send()

    def second_sent(d, carry):
        to_partner(d).wait_send()
        return carry

    lax.fori_loop(1, chips, second_sent, 0)
    o_ref[...] = held[...]


def pair_gather(x, n, collective_id):
    return pl.pallas_call(
        pair_gather_kernel,
        out_shape=jax.ShapeDtypeStruct((n,) + x.shape, jnp.float32),
        in_specs=[pl.BlockSpec(memory_space=pltpu.VMEM)],
        out_specs=pl.BlockSpec(memory_space=pltpu.VMEM),
        scratch_shapes=[
            pltpu.VMEM((n,) + x.shape, jnp.float32),
            pltpu.SemaphoreType.DMA((n // 2,)),
            pltpu.SemaphoreType.DMA((n // 2,)),
            pltpu.SemaphoreType.DMA((n // 2,)),
            pltpu.SemaphoreType.DMA((n // 2,)),
        ],
        compiler_params=pltpu.CompilerParams(collective_id=collective_id, has_side_effects=True),
    )(x)


def body(
    states, gap_mask, weights, leaf_order, exchanges, codon_freq, omega_ratio, lengths, classes
):
    site_count = lax.axis_size("site")
    site_pos = lax.axis_index("site")
    subtree = lax.axis_index("branch")
    site_span = states.shape[1]
    total_sites = site_span * site_count
    total_taxa = LEAF_DEV * lax.axis_size("branch")
    rate_matrix, stationary = build_rates(exchanges, codon_freq, omega_ratio)
    slot_len = jnp.concatenate([lengths, jnp.zeros((1,), lengths.dtype)])
    slot_cls = jnp.concatenate([classes, jnp.zeros((1,), jnp.int32)])
    class_pick = (slot_cls[:, None] == jnp.arange(CLASSES, dtype=jnp.int32)[None, :]).astype(
        jnp.float32
    )
    slot_rates = jnp.einsum("bc,cij->bij", class_pick, rate_matrix, precision=lax.Precision.HIGH)
    scaled = slot_rates * slot_len[:, None, None]
    per_dev = SLOTS // site_count
    own_start = site_pos * per_dev
    own_scaled = lax.dynamic_slice_in_dim(scaled, own_start, per_dev, 0)
    own_pull = None
    own_probs, own_pull = jax.vjp(expm_taylor, own_scaled)
    dense = pair_gather(own_probs.reshape(-1, 128), site_count, 1)
    probs = dense.reshape((site_count * per_dev,) + own_probs.shape[1:])
    taxon_rows = lax.dynamic_slice_in_dim(leaf_order, subtree * LEAF_DEV, LEAF_DEV, 0)
    leaves = leaf_partials(
        jnp.take(states, taxon_rows, axis=0), jnp.take(gap_mask, taxon_rows, axis=0)
    )
    levels, messages, logscale = up_pass(probs, leaves)
    top_pack = jnp.concatenate([messages[-1][0], logscale[None, :]], axis=0)
    top_all = lax.all_gather(top_pack, "branch", axis=0, tiled=False)
    top_messages, top_logs = top_all[:, :64, :], top_all[:, 64, :]
    site_ll, above_all = root_terms(stationary, top_messages, top_logs)
    site_weight = weights.astype(jnp.float32)
    loglik_part = jnp.sum(site_weight * site_ll)
    above_top = lax.dynamic_slice_in_dim(above_all, subtree, 1, 0)
    a_list = down_pass(probs, levels, messages, above_top)
    weighted = weigh(a_list, messages, site_weight, total_sites)
    padding = jnp.zeros((1, 64, site_span), jnp.float32)
    weighted_all = jnp.concatenate(weighted + [padding], axis=0)
    partial_all = jnp.concatenate(levels + [padding], axis=0)
    part_above = lax.slice_in_dim(weighted_all, 0, lax.axis_size("site") * per_dev, axis=0)
    part_below = lax.slice_in_dim(partial_all, 0, lax.axis_size("site") * per_dev, axis=0)
    part_counts = jnp.einsum("bis,bjs->bij", part_above, part_below, precision=lax.Precision.HIGH)
    own_counts = pair_scatter(part_counts.reshape(site_count, -1, 128), 2).reshape((per_dev, 64, 64))
    d_scaled = own_pull(own_counts)[0]
    use_rates = lax.dynamic_slice_in_dim(slot_rates, own_start, per_dev, 0)
    use_len = lax.dynamic_slice_in_dim(slot_len, own_start, per_dev, 0)
    use_pick = lax.dynamic_slice_in_dim(class_pick, own_start, per_dev, 0)
    d_length = jnp.sum(d_scaled * use_rates, axis=(1, 2))
    d_rates = jnp.einsum(
        "bc,bij->cij", use_pick, d_scaled * use_len[:, None, None], precision=lax.Precision.HIGH
    )
    unused_rates, pull_rates = jax.vjp(
        lambda table, ratio: build_rates(table, codon_freq, ratio)[0], exchanges, omega_ratio
    )
    d_exch, d_omega = pull_rates(d_rates)
    n_branch = lax.axis_size("branch")
    length_slab = jnp.zeros((n_branch, SLOTS), jnp.float32)
    length_slab = lax.dynamic_update_slice(length_slab, d_length[None, :], (subtree, own_start))
    loglik_keep = jnp.where(subtree == 0, loglik_part, jnp.float32(0.0))
    packed = jnp.concatenate(
        [d_exch.reshape(-1), d_omega, length_slab.reshape(-1), loglik_keep[None]]
    )
    rows = -(-packed.shape[0] // (8 * 128)) * 8
    packed = jnp.pad(packed, (0, rows * 128 - packed.shape[0])).reshape(rows, 128)
    summed = allreduce_all(packed, site_count, n_branch).reshape(-1)
    grad_exch = summed[: 64 * 64].reshape(64, 64)
    grad_omega = summed[64 * 64 : 64 * 64 + CLASSES]
    length_all = summed[64 * 64 + CLASSES : 64 * 64 + CLASSES + n_branch * SLOTS].reshape(n_branch, SLOTS)
    log_total = summed[64 * 64 + CLASSES + n_branch * SLOTS]
    loglik = log_total / total_sites / total_taxa
    length_out = lax.dynamic_index_in_dim(length_all, subtree, 0, keepdims=False)[:EDGES]
    return (grad_exch, grad_omega, length_out, loglik)


def solution(mesh):
    return jax.shard_map(
        body,
        mesh=mesh,
        in_specs=(
            P(None, "site"),
            P(None, "site"),
            P("site"),
            P(),
            P(),
            P(),
            P(),
            P("branch"),
            P("branch"),
        ),
        out_specs=(P(), P(), P("branch"), P()),
        check_vma=False,
    )
```

```python
import jax
import jax.numpy as jnp
import numpy as np
from jax import lax
from jax.sharding import PartitionSpec as P
from jax.experimental import pallas as pl
from jax.experimental.pallas import tpu as pltpu
import functools

MESH_ID = pl.DeviceIdType.MESH

LEVELS = 6
LEAF_DEV = 64
EDGES = 127
SLOTS = 128
CLASSES = 8


CODE_TABLE = "FFLLSSSSYYXXCCXWLLLLPPPPHHQQRRRRIIIMTTTTNNKKSSRRVVVVAAAADDEEGGGG"


def codon_tables():
    amino_acid = np.array(list(CODE_TABLE))
    codon_index = np.arange(64)
    digits = np.stack([codon_index // 16, codon_index // 4 % 4, codon_index % 4], 1)
    differ = (digits[:, None, :] != digits[None, :, :]).sum(-1)
    is_sense = amino_acid != "X"
    single = (differ == 1) & is_sense[:, None] & is_sense[None, :]
    nonsyn = single & (amino_acid[:, None] != amino_acid[None, :])
    return (is_sense.astype(np.float32), single.astype(np.float32), nonsyn.astype(np.float32))


def build_rates(exchanges, codon_freq, omega_ratio):
    is_sense, single, nonsyn = codon_tables()
    stationary = codon_freq * is_sense / jnp.sum(codon_freq * is_sense)
    symmetric = 0.5 * (exchanges + exchanges.T)
    factor = 1.0 + nonsyn[None, :, :] * (omega_ratio[:, None, None] - 1.0)
    off_diag = symmetric[None, :, :] * stationary[None, None, :] * factor * single[None, :, :]
    row_total = jnp.sum(off_diag, axis=2)
    mean_rate = jnp.sum(stationary[None, :] * row_total, axis=1)
    identity = jnp.eye(64, dtype=exchanges.dtype)
    rate_matrix = (off_diag - row_total[:, :, None] * identity[None]) / mean_rate[:, None, None]
    return (rate_matrix, stationary)


def product(left, right):
    return jnp.einsum("bij,bjk->bik", left, right, precision=lax.Precision.HIGH)


def expm_taylor(scaled):
    reduced = scaled / 16.0
    identity = jnp.eye(64, dtype=scaled.dtype)
    series = jnp.broadcast_to(identity, scaled.shape)
    for degree in range(8, 0, -1):
        series = identity + product(reduced, series) / degree
    for square_step in range(4):
        series = product(series, series)
    return series


def forward(probs, vectors):
    return jnp.einsum("bij,bjs->bis", probs, vectors, precision=lax.Precision.HIGH)


def carried(probs, vectors):
    return jnp.einsum("bji,bjs->bis", probs, vectors, precision=lax.Precision.HIGH)


def leaf_partials(leaf_states, gap_rows):
    codon_axis = jnp.arange(64, dtype=jnp.int32)
    indicator = (leaf_states[:, None, :] == codon_axis[None, :, None]).astype(jnp.float32)
    return jnp.where(gap_rows[:, None, :] > 0, jnp.float32(1.0), indicator)


def up_pass(probs, leaves):
    levels = [leaves]
    messages = []
    logscale = jnp.zeros(leaves.shape[2:], jnp.float32)
    current = leaves
    for height in range(LEVELS):
        amount = current.shape[0]
        offset = 2 * LEAF_DEV - 2 * amount
        message = forward(probs[offset : offset + amount], current)
        messages.append(message)
        raw_parent = message[0::2] * message[1::2]
        scaling = jnp.sum(raw_parent, axis=1)
        current = raw_parent / scaling[:, None, :]
        logscale = logscale + jnp.sum(jnp.log(scaling), axis=0)
        levels.append(current)
    messages.append(forward(probs[EDGES - 1 : EDGES], current))
    return (levels, messages, logscale)


def root_terms(stationary, top_messages, top_logs):
    members = top_messages.shape[0]
    joint = stationary[:, None] * top_messages[0]
    for member in range(1, members):
        joint = joint * top_messages[member]
    site_ll = jnp.log(jnp.sum(joint, axis=0)) + jnp.sum(top_logs, axis=0)
    above_list = []
    for member in range(members):
        vector = jnp.broadcast_to(stationary[:, None], top_messages.shape[1:])
        for other in range(members):
            if other != member:
                vector = vector * top_messages[other]
        above_list.append(vector)
    return (site_ll, jnp.stack(above_list))


def down_pass(probs, levels, messages, above_top):
    a_list = [above_top]
    current = above_top
    for height in range(LEVELS, 0, -1):
        amount = levels[height].shape[0]
        offset = 2 * LEAF_DEV - 2 * amount
        down_part = carried(probs[offset : offset + amount], current)
        down_part = down_part / jnp.sum(down_part, axis=1, keepdims=True)
        message = messages[height - 1]
        current = jnp.stack([down_part * message[1::2], down_part * message[0::2]], axis=1).reshape(
            message.shape
        )
        a_list.append(current)
    return a_list[::-1]


def weigh(a_list, messages, site_weight, total_sites):
    weighted = []
    for vector, message in zip(a_list, messages):
        likelihood = jnp.sum(vector * message, axis=1)
        weighted.append(vector * (site_weight / (likelihood * total_sites))[:, None, :])
    return weighted


def sum_groups(n_site, n_branch):
    s = lax.axis_index("site")
    k = lax.axis_index("branch")
    core = s % 2
    y = (s // 2) % 4
    z = s // 8
    n_z = n_site // 8
    return [
        (2, core, lambda c: (s - core + c, k)),
        (n_branch, k, lambda c: (s, c)),
        (4, y, lambda c: (s - 2 * y + 2 * c, k)),
        (n_z, z, lambda c: (s - 8 * z + 8 * c, k)),
    ]


def allreduce_kernel(n_site, n_branch, x_ref, o_ref, held, send_sems, recv_sems):
    stages = sum_groups(n_site, n_branch)
    barrier = pltpu.get_barrier_semaphore()
    count = 0
    for size, mine, where in stages:
        for d in range(1, size):
            other = lax.rem(mine + d, size)
            pl.semaphore_signal(barrier, inc=1, device_id=where(other), device_id_type=MESH_ID)
            count += 1
    pl.semaphore_wait(barrier, count)
    total = x_ref[...]
    for st, (size, mine, where) in enumerate(stages):
        held[st, mine] = total
        sends = []
        for d in range(1, size):
            other = lax.rem(mine + d, size)
            copy = pltpu.make_async_remote_copy(
                src_ref=held.at[st, mine],
                dst_ref=held.at[st, mine],
                send_sem=send_sems.at[st, other],
                recv_sem=recv_sems.at[st, mine],
                device_id=where(other),
                device_id_type=MESH_ID,
            )
            copy.start()
            sends.append(copy)
        for d in range(1, size):
            other = lax.rem(mine + d, size)
            incoming = pltpu.make_async_remote_copy(
                src_ref=held.at[st, other],
                dst_ref=held.at[st, other],
                send_sem=send_sems.at[st, other],
                recv_sem=recv_sems.at[st, other],
                device_id=where(other),
                device_id_type=MESH_ID,
            )
            incoming.wait_recv()
        for copy in sends:
            copy.wait_send()
        total = held[st, 0]
        for c in range(1, size):
            total = total + held[st, c]
    o_ref[...] = total


def allreduce_all(x, n_site, n_branch):
    rows = x.shape[0]
    return pl.pallas_call(
        functools.partial(allreduce_kernel, n_site, n_branch),
        out_shape=jax.ShapeDtypeStruct(x.shape, jnp.float32),
        in_specs=[pl.BlockSpec(memory_space=pltpu.VMEM)],
        out_specs=pl.BlockSpec(memory_space=pltpu.VMEM),
        scratch_shapes=[
            pltpu.VMEM((4, 4, rows, 128), jnp.float32),
            pltpu.SemaphoreType.DMA((4, 4)),
            pltpu.SemaphoreType.DMA((4, 4)),
        ],
        compiler_params=pltpu.CompilerParams(collective_id=0, has_side_effects=True),
    )(x)


def exchange_kernel(axis, gather, x_ref, o_ref, held, send_sems, recv_sems):
    n = held.shape[0]
    me = lax.axis_index(axis)
    other_axis = "branch" if axis == "site" else "site"
    fixed = lax.axis_index(other_axis)

    def device(p):
        return (p, fixed) if axis == "site" else (fixed, p)

    barrier = pltpu.get_barrier_semaphore()

    def greet(d, carry):
        pl.semaphore_signal(
            barrier, inc=1, device_id=device(lax.rem(me + d, n)), device_id_type=MESH_ID
        )
        return carry

    lax.fori_loop(1, n, greet, 0)
    pl.semaphore_wait(barrier, n - 1)
    if gather:
        held[me] = x_ref[...]
    else:
        held[me] = x_ref[me]

    def outgoing(d):
        p = lax.rem(me + d, n)
        return pltpu.make_async_remote_copy(
            src_ref=x_ref if gather else x_ref.at[p],
            dst_ref=held.at[me],
            send_sem=send_sems.at[p],
            recv_sem=recv_sems.at[me],
            device_id=device(p),
            device_id_type=MESH_ID,
        )

    def send(d, carry):
        outgoing(d).start()
        return carry

    lax.fori_loop(1, n, send, 0)

    def receive(d, carry):
        p = lax.rem(me + n - d, n)
        pltpu.make_async_remote_copy(
            src_ref=held.at[p],
            dst_ref=held.at[p],
            send_sem=send_sems.at[p],
            recv_sem=recv_sems.at[p],
            device_id=device(p),
            device_id_type=MESH_ID,
        ).wait_recv()
        return carry

    lax.fori_loop(1, n, receive, 0)

    def sent(d, carry):
        outgoing(d).wait_send()
        return carry

    lax.fori_loop(1, n, sent, 0)
    if gather:
        o_ref[...] = held[...]
    else:
        o_ref[...] = lax.fori_loop(1, n, lambda j, acc: acc + held[j], held[0])


def exchange(x, axis, n, gather, collective_id):
    chunk = x.shape if gather else x.shape[1:]
    out_shape = (n,) + chunk if gather else chunk
    return pl.pallas_call(
        functools.partial(exchange_kernel, axis, gather),
        out_shape=jax.ShapeDtypeStruct(out_shape, jnp.float32),
        in_specs=[pl.BlockSpec(memory_space=pltpu.VMEM)],
        out_specs=pl.BlockSpec(memory_space=pltpu.VMEM),
        scratch_shapes=[
            pltpu.VMEM((n,) + chunk, jnp.float32),
            pltpu.SemaphoreType.DMA((n,)),
            pltpu.SemaphoreType.DMA((n,)),
        ],
        compiler_params=pltpu.CompilerParams(collective_id=collective_id, has_side_effects=True),
    )(x)


def pair_scatter_kernel(x_ref, o_ref, pair_buf, pair_sum, held, sems_a, sems_b, sems_c, sems_d):
    n = x_ref.shape[0]
    chips = n // 2
    s = lax.axis_index("site")
    k = lax.axis_index("branch")
    core = s % 2
    chip = s // 2
    partner = s - core + (1 - core)
    barrier = pltpu.get_barrier_semaphore()
    pl.semaphore_signal(barrier, inc=1, device_id=(partner, k), device_id_type=MESH_ID)

    def greet(d, carry):
        peer = 2 * lax.rem(chip + d, chips) + core
        pl.semaphore_signal(barrier, inc=1, device_id=(peer, k), device_id_type=MESH_ID)
        return carry

    lax.fori_loop(1, chips, greet, 0)
    pl.semaphore_wait(barrier, chips)

    def to_partner(m):
        return pltpu.make_async_remote_copy(
            src_ref=x_ref.at[2 * m + 1 - core],
            dst_ref=pair_buf.at[m],
            send_sem=sems_a.at[m],
            recv_sem=sems_b.at[m],
            device_id=(partner, k),
            device_id_type=MESH_ID,
        )

    def first_send(m, carry):
        to_partner(m).start()
        return carry

    lax.fori_loop(0, chips, first_send, 0)

    def to_chip(c):
        return pltpu.make_async_remote_copy(
            src_ref=pair_sum.at[c],
            dst_ref=held.at[chip],
            send_sem=sems_c.at[c],
            recv_sem=sems_d.at[chip],
            device_id=(2 * c + core, k),
            device_id_type=MESH_ID,
        )

    to_partner(chip).wait_recv()
    pair_sum[chip] = x_ref[2 * chip + core] + pair_buf[chip]
    held[chip] = pair_sum[chip]

    def add_and_send(d, carry):
        c = lax.rem(chip + d, chips)
        to_partner(c).wait_recv()
        pair_sum[c] = x_ref[2 * c + core] + pair_buf[c]
        to_chip(c).start()
        return carry

    lax.fori_loop(1, chips, add_and_send, 0)

    def second_recv(d, carry):
        c = lax.rem(chip + chips - d, chips)
        pltpu.make_async_remote_copy(
            src_ref=held.at[c],
            dst_ref=held.at[c],
            send_sem=sems_c.at[c],
            recv_sem=sems_d.at[c],
            device_id=(2 * c + core, k),
            device_id_type=MESH_ID,
        ).wait_recv()
        return carry

    lax.fori_loop(1, chips, second_recv, 0)

    def first_sent(m, carry):
        to_partner(m).wait_send()
        return carry

    lax.fori_loop(0, chips, first_sent, 0)

    def second_sent(d, carry):
        to_chip(lax.rem(chip + d, chips)).wait_send()
        return carry

    lax.fori_loop(1, chips, second_sent, 0)
    o_ref[...] = lax.fori_loop(1, chips, lambda j, acc: acc + held[j], held[0])


def pair_scatter(x, collective_id):
    n = x.shape[0]
    chunk = x.shape[1:]
    return pl.pallas_call(
        pair_scatter_kernel,
        out_shape=jax.ShapeDtypeStruct(chunk, jnp.float32),
        in_specs=[pl.BlockSpec(memory_space=pltpu.VMEM)],
        out_specs=pl.BlockSpec(memory_space=pltpu.VMEM),
        scratch_shapes=[
            pltpu.VMEM((n // 2,) + chunk, jnp.float32),
            pltpu.VMEM((n // 2,) + chunk, jnp.float32),
            pltpu.VMEM((n // 2,) + chunk, jnp.float32),
            pltpu.SemaphoreType.DMA((n // 2,)),
            pltpu.SemaphoreType.DMA((n // 2,)),
            pltpu.SemaphoreType.DMA((n // 2,)),
            pltpu.SemaphoreType.DMA((n // 2,)),
        ],
        compiler_params=pltpu.CompilerParams(collective_id=collective_id, has_side_effects=True),
    )(x)


def pair_gather_kernel(x_ref, o_ref, held, sems_a, sems_b, sems_c, sems_d):
    n = held.shape[0]
    chips = n // 2
    s = lax.axis_index("site")
    k = lax.axis_index("branch")
    core = s % 2
    chip = s // 2
    partner = s - core + (1 - core)
    barrier = pltpu.get_barrier_semaphore()
    pl.semaphore_signal(barrier, inc=1, device_id=(partner, k), device_id_type=MESH_ID)

    def greet(d, carry):
        peer = 2 * lax.rem(chip + d, chips) + core
        pl.semaphore_signal(barrier, inc=1, device_id=(peer, k), device_id_type=MESH_ID)
        return carry

    lax.fori_loop(1, chips, greet, 0)
    pl.semaphore_wait(barrier, chips)
    held[s] = x_ref[...]

    def to_chip(d):
        c = lax.rem(chip + d, chips)
        return pltpu.make_async_remote_copy(
            src_ref=x_ref,
            dst_ref=held.at[s],
            send_sem=sems_a.at[c],
            recv_sem=sems_b.at[chip],
            device_id=(2 * c + core, k),
            device_id_type=MESH_ID,
        )

    def first_send(d, carry):
        to_chip(d).start()
        return carry

    lax.fori_loop(1, chips, first_send, 0)

    def to_partner(c):
        return pltpu.make_async_remote_copy(
            src_ref=held.at[2 * c + core],
            dst_ref=held.at[2 * c + core],
            send_sem=sems_c.at[c],
            recv_sem=sems_d.at[c],
            device_id=(partner, k),
            device_id_type=MESH_ID,
        )

    own = pltpu.make_async_remote_copy(
        src_ref=x_ref,
        dst_ref=held.at[s],
        send_sem=sems_c.at[chip],
        recv_sem=sems_d.at[chip],
        device_id=(partner, k),
        device_id_type=MESH_ID,
    )
    own.start()

    def relay(d, carry):
        c = lax.rem(chip + chips - d, chips)
        pltpu.make_async_remote_copy(
            src_ref=held.at[2 * c + core],
            dst_ref=held.at[2 * c + core],
            send_sem=sems_a.at[c],
            recv_sem=sems_b.at[c],
            device_id=(2 * c + core, k),
            device_id_type=MESH_ID,
        ).wait_recv()
        to_partner(c).start()
        return carry

    lax.fori_loop(1, chips, relay, 0)

    def second_recv(c, carry):
        pltpu.make_async_remote_copy(
            src_ref=held.at[2 * c + 1 - core],
            dst_ref=held.at[2 * c + 1 - core],
            send_sem=sems_c.at[c],
            recv_sem=sems_d.at[c],
            device_id=(partner, k),
            device_id_type=MESH_ID,
        ).wait_recv()
        return carry

    lax.fori_loop(0, chips, second_recv, 0)

    def first_sent(d, carry):
        to_chip(d).wait_send()
        return carry

    lax.fori_loop(1, chips, first_sent, 0)
    own.wait_send()

    def second_sent(d, carry):
        to_partner(lax.rem(chip + d, chips)).wait_send()
        return carry

    lax.fori_loop(1, chips, second_sent, 0)
    o_ref[...] = held[...]


def pair_gather(x, n, collective_id):
    return pl.pallas_call(
        pair_gather_kernel,
        out_shape=jax.ShapeDtypeStruct((n,) + x.shape, jnp.float32),
        in_specs=[pl.BlockSpec(memory_space=pltpu.VMEM)],
        out_specs=pl.BlockSpec(memory_space=pltpu.VMEM),
        scratch_shapes=[
            pltpu.VMEM((n,) + x.shape, jnp.float32),
            pltpu.SemaphoreType.DMA((n // 2,)),
            pltpu.SemaphoreType.DMA((n // 2,)),
            pltpu.SemaphoreType.DMA((n // 2,)),
            pltpu.SemaphoreType.DMA((n // 2,)),
        ],
        compiler_params=pltpu.CompilerParams(collective_id=collective_id, has_side_effects=True),
    )(x)


def body(
    states, gap_mask, weights, leaf_order, exchanges, codon_freq, omega_ratio, lengths, classes
):
    site_count = lax.axis_size("site")
    site_pos = lax.axis_index("site")
    subtree = lax.axis_index("branch")
    site_span = states.shape[1]
    total_sites = site_span * site_count
    total_taxa = LEAF_DEV * lax.axis_size("branch")
    rate_matrix, stationary = build_rates(exchanges, codon_freq, omega_ratio)
    slot_len = jnp.concatenate([lengths, jnp.zeros((1,), lengths.dtype)])
    slot_cls = jnp.concatenate([classes, jnp.zeros((1,), jnp.int32)])
    class_pick = (slot_cls[:, None] == jnp.arange(CLASSES, dtype=jnp.int32)[None, :]).astype(
        jnp.float32
    )
    slot_rates = jnp.einsum("bc,cij->bij", class_pick, rate_matrix, precision=lax.Precision.HIGH)
    scaled = slot_rates * slot_len[:, None, None]
    per_dev = SLOTS // site_count
    own_start = site_pos * per_dev
    own_scaled = lax.dynamic_slice_in_dim(scaled, own_start, per_dev, 0)
    own_pull = None
    own_probs, own_pull = jax.vjp(expm_taylor, own_scaled)
    dense = pair_gather(own_probs.reshape(-1, 128), site_count, 1)
    probs = dense.reshape((site_count * per_dev,) + own_probs.shape[1:])
    taxon_rows = lax.dynamic_slice_in_dim(leaf_order, subtree * LEAF_DEV, LEAF_DEV, 0)
    leaves = leaf_partials(
        jnp.take(states, taxon_rows, axis=0), jnp.take(gap_mask, taxon_rows, axis=0)
    )
    levels, messages, logscale = up_pass(probs, leaves)
    top_pack = jnp.concatenate([messages[-1][0], logscale[None, :]], axis=0)
    top_all = lax.all_gather(top_pack, "branch", axis=0, tiled=False)
    top_messages, top_logs = top_all[:, :64, :], top_all[:, 64, :]
    site_ll, above_all = root_terms(stationary, top_messages, top_logs)
    site_weight = weights.astype(jnp.float32)
    loglik_part = jnp.sum(site_weight * site_ll)
    above_top = lax.dynamic_slice_in_dim(above_all, subtree, 1, 0)
    a_list = down_pass(probs, levels, messages, above_top)
    weighted = weigh(a_list, messages, site_weight, total_sites)
    padding = jnp.zeros((1, 64, site_span), jnp.float32)
    weighted_all = jnp.concatenate(weighted + [padding], axis=0)
    partial_all = jnp.concatenate(levels + [padding], axis=0)
    part_above = lax.slice_in_dim(weighted_all, 0, lax.axis_size("site") * per_dev, axis=0)
    part_below = lax.slice_in_dim(partial_all, 0, lax.axis_size("site") * per_dev, axis=0)
    part_counts = jnp.einsum("bis,bjs->bij", part_above, part_below, precision=lax.Precision.HIGH)
    own_counts = pair_scatter(part_counts.reshape(site_count, -1, 128), 2).reshape((per_dev, 64, 64))
    d_scaled = own_pull(own_counts)[0]
    use_rates = lax.dynamic_slice_in_dim(slot_rates, own_start, per_dev, 0)
    use_len = lax.dynamic_slice_in_dim(slot_len, own_start, per_dev, 0)
    use_pick = lax.dynamic_slice_in_dim(class_pick, own_start, per_dev, 0)
    d_length = jnp.sum(d_scaled * use_rates, axis=(1, 2))
    d_rates = jnp.einsum(
        "bc,bij->cij", use_pick, d_scaled * use_len[:, None, None], precision=lax.Precision.HIGH
    )
    unused_rates, pull_rates = jax.vjp(
        lambda table, ratio: build_rates(table, codon_freq, ratio)[0], exchanges, omega_ratio
    )
    d_exch, d_omega = pull_rates(d_rates)
    n_branch = lax.axis_size("branch")
    length_slab = jnp.zeros((n_branch, SLOTS), jnp.float32)
    length_slab = lax.dynamic_update_slice(length_slab, d_length[None, :], (subtree, own_start))
    loglik_keep = jnp.where(subtree == 0, loglik_part, jnp.float32(0.0))
    packed = jnp.concatenate(
        [d_exch.reshape(-1), d_omega, length_slab.reshape(-1), loglik_keep[None]]
    )
    rows = -(-packed.shape[0] // (8 * 128)) * 8
    packed = jnp.pad(packed, (0, rows * 128 - packed.shape[0])).reshape(rows, 128)
    summed = allreduce_all(packed, site_count, n_branch).reshape(-1)
    grad_exch = summed[: 64 * 64].reshape(64, 64)
    grad_omega = summed[64 * 64 : 64 * 64 + CLASSES]
    length_all = summed[64 * 64 + CLASSES : 64 * 64 + CLASSES + n_branch * SLOTS].reshape(n_branch, SLOTS)
    log_total = summed[64 * 64 + CLASSES + n_branch * SLOTS]
    loglik = log_total / total_sites / total_taxa
    length_out = lax.dynamic_index_in_dim(length_all, subtree, 0, keepdims=False)[:EDGES]
    return (grad_exch, grad_omega, length_out, loglik)


def solution(mesh):
    return jax.shard_map(
        body,
        mesh=mesh,
        in_specs=(
            P(None, "site"),
            P(None, "site"),
            P("site"),
            P(),
            P(),
            P(),
            P(),
            P("branch"),
            P("branch"),
        ),
        out_specs=(P(), P(), P("branch"), P()),
        check_vma=False,
    )
```

```python
import jax
import jax.numpy as jnp
import numpy as np
from jax import lax
from jax.sharding import PartitionSpec as P
from jax.experimental import pallas as pl
from jax.experimental.pallas import tpu as pltpu
import functools

MESH_ID = pl.DeviceIdType.MESH

LEVELS = 6
LEAF_DEV = 64
EDGES = 127
SLOTS = 128
CLASSES = 8


CODE_TABLE = "FFLLSSSSYYXXCCXWLLLLPPPPHHQQRRRRIIIMTTTTNNKKSSRRVVVVAAAADDEEGGGG"


def codon_tables():
    amino_acid = np.array(list(CODE_TABLE))
    codon_index = np.arange(64)
    digits = np.stack([codon_index // 16, codon_index // 4 % 4, codon_index % 4], 1)
    differ = (digits[:, None, :] != digits[None, :, :]).sum(-1)
    is_sense = amino_acid != "X"
    single = (differ == 1) & is_sense[:, None] & is_sense[None, :]
    nonsyn = single & (amino_acid[:, None] != amino_acid[None, :])
    return (is_sense.astype(np.float32), single.astype(np.float32), nonsyn.astype(np.float32))


def build_rates(exchanges, codon_freq, omega_ratio):
    is_sense, single, nonsyn = codon_tables()
    stationary = codon_freq * is_sense / jnp.sum(codon_freq * is_sense)
    symmetric = 0.5 * (exchanges + exchanges.T)
    factor = 1.0 + nonsyn[None, :, :] * (omega_ratio[:, None, None] - 1.0)
    off_diag = symmetric[None, :, :] * stationary[None, None, :] * factor * single[None, :, :]
    row_total = jnp.sum(off_diag, axis=2)
    mean_rate = jnp.sum(stationary[None, :] * row_total, axis=1)
    identity = jnp.eye(64, dtype=exchanges.dtype)
    rate_matrix = (off_diag - row_total[:, :, None] * identity[None]) / mean_rate[:, None, None]
    return (rate_matrix, stationary)


def product(left, right):
    return jnp.einsum("bij,bjk->bik", left, right, precision=lax.Precision.HIGH)


def expm_taylor(scaled):
    reduced = scaled / 16.0
    identity = jnp.eye(64, dtype=scaled.dtype)
    series = jnp.broadcast_to(identity, scaled.shape)
    for degree in range(8, 0, -1):
        series = identity + product(reduced, series) / degree
    for square_step in range(4):
        series = product(series, series)
    return series


def forward(probs, vectors):
    return jnp.einsum("bij,bjs->bis", probs, vectors, precision=lax.Precision.HIGH)


def carried(probs, vectors):
    return jnp.einsum("bji,bjs->bis", probs, vectors, precision=lax.Precision.HIGH)


def leaf_partials(leaf_states, gap_rows):
    codon_axis = jnp.arange(64, dtype=jnp.int32)
    indicator = (leaf_states[:, None, :] == codon_axis[None, :, None]).astype(jnp.float32)
    return jnp.where(gap_rows[:, None, :] > 0, jnp.float32(1.0), indicator)


def up_pass(probs, leaves):
    levels = [leaves]
    messages = []
    logscale = jnp.zeros(leaves.shape[2:], jnp.float32)
    current = leaves
    for height in range(LEVELS):
        amount = current.shape[0]
        offset = 2 * LEAF_DEV - 2 * amount
        message = forward(probs[offset : offset + amount], current)
        messages.append(message)
        raw_parent = message[0::2] * message[1::2]
        scaling = jnp.sum(raw_parent, axis=1)
        current = raw_parent / scaling[:, None, :]
        logscale = logscale + jnp.sum(jnp.log(scaling), axis=0)
        levels.append(current)
    messages.append(forward(probs[EDGES - 1 : EDGES], current))
    return (levels, messages, logscale)


def root_terms(stationary, top_messages, top_logs):
    members = top_messages.shape[0]
    joint = stationary[:, None] * top_messages[0]
    for member in range(1, members):
        joint = joint * top_messages[member]
    site_ll = jnp.log(jnp.sum(joint, axis=0)) + jnp.sum(top_logs, axis=0)
    above_list = []
    for member in range(members):
        vector = jnp.broadcast_to(stationary[:, None], top_messages.shape[1:])
        for other in range(members):
            if other != member:
                vector = vector * top_messages[other]
        above_list.append(vector)
    return (site_ll, jnp.stack(above_list))


def down_pass(probs, levels, messages, above_top):
    a_list = [above_top]
    current = above_top
    for height in range(LEVELS, 0, -1):
        amount = levels[height].shape[0]
        offset = 2 * LEAF_DEV - 2 * amount
        down_part = carried(probs[offset : offset + amount], current)
        down_part = down_part / jnp.sum(down_part, axis=1, keepdims=True)
        message = messages[height - 1]
        current = jnp.stack([down_part * message[1::2], down_part * message[0::2]], axis=1).reshape(
            message.shape
        )
        a_list.append(current)
    return a_list[::-1]


def weigh(a_list, messages, site_weight, total_sites):
    weighted = []
    for vector, message in zip(a_list, messages):
        likelihood = jnp.sum(vector * message, axis=1)
        weighted.append(vector * (site_weight / (likelihood * total_sites))[:, None, :])
    return weighted


def sum_groups(n_site, n_branch):
    s = lax.axis_index("site")
    k = lax.axis_index("branch")
    core = s % 2
    y = (s // 2) % 4
    z = s // 8
    n_z = n_site // 8
    return [
        (2, core, lambda c: (s - core + c, k)),
        (n_branch, k, lambda c: (s, c)),
        (4, y, lambda c: (s - 2 * y + 2 * c, k)),
        (n_z, z, lambda c: (s - 8 * z + 8 * c, k)),
    ]


def allreduce_kernel(n_site, n_branch, x_ref, o_ref, held, send_sems, recv_sems):
    stages = sum_groups(n_site, n_branch)
    barrier = pltpu.get_barrier_semaphore()
    count = 0
    for size, mine, where in stages:
        for d in range(1, size):
            other = lax.rem(mine + d, size)
            pl.semaphore_signal(barrier, inc=1, device_id=where(other), device_id_type=MESH_ID)
            count += 1
    pl.semaphore_wait(barrier, count)
    total = x_ref[...]
    for st, (size, mine, where) in enumerate(stages):
        held[st, mine] = total
        sends = []
        for d in range(1, size):
            other = lax.rem(mine + d, size)
            copy = pltpu.make_async_remote_copy(
                src_ref=held.at[st, mine],
                dst_ref=held.at[st, mine],
                send_sem=send_sems.at[st, other],
                recv_sem=recv_sems.at[st, mine],
                device_id=where(other),
                device_id_type=MESH_ID,
            )
            copy.start()
            sends.append(copy)
        for d in range(1, size):
            other = lax.rem(mine + d, size)
            incoming = pltpu.make_async_remote_copy(
                src_ref=held.at[st, other],
                dst_ref=held.at[st, other],
                send_sem=send_sems.at[st, other],
                recv_sem=recv_sems.at[st, other],
                device_id=where(other),
                device_id_type=MESH_ID,
            )
            incoming.wait_recv()
        for copy in sends:
            copy.wait_send()
        total = held[st, 0]
        for c in range(1, size):
            total = total + held[st, c]
    o_ref[...] = total


def allreduce_all(x, n_site, n_branch):
    rows = x.shape[0]
    return pl.pallas_call(
        functools.partial(allreduce_kernel, n_site, n_branch),
        out_shape=jax.ShapeDtypeStruct(x.shape, jnp.float32),
        in_specs=[pl.BlockSpec(memory_space=pltpu.VMEM)],
        out_specs=pl.BlockSpec(memory_space=pltpu.VMEM),
        scratch_shapes=[
            pltpu.VMEM((4, 4, rows, 128), jnp.float32),
            pltpu.SemaphoreType.DMA((4, 4)),
            pltpu.SemaphoreType.DMA((4, 4)),
        ],
        compiler_params=pltpu.CompilerParams(collective_id=0, has_side_effects=True),
    )(x)


def exchange_kernel(axis, gather, x_ref, o_ref, held, send_sems, recv_sems):
    n = held.shape[0]
    me = lax.axis_index(axis)
    other_axis = "branch" if axis == "site" else "site"
    fixed = lax.axis_index(other_axis)

    def device(p):
        return (p, fixed) if axis == "site" else (fixed, p)

    barrier = pltpu.get_barrier_semaphore()

    def greet(d, carry):
        pl.semaphore_signal(
            barrier, inc=1, device_id=device(lax.rem(me + d, n)), device_id_type=MESH_ID
        )
        return carry

    lax.fori_loop(1, n, greet, 0)
    pl.semaphore_wait(barrier, n - 1)
    if gather:
        held[me] = x_ref[...]
    else:
        held[me] = x_ref[me]

    def outgoing(d):
        p = lax.rem(me + d, n)
        return pltpu.make_async_remote_copy(
            src_ref=x_ref if gather else x_ref.at[p],
            dst_ref=held.at[me],
            send_sem=send_sems.at[p],
            recv_sem=recv_sems.at[me],
            device_id=device(p),
            device_id_type=MESH_ID,
        )

    def send(d, carry):
        outgoing(d).start()
        return carry

    lax.fori_loop(1, n, send, 0)

    def receive(d, carry):
        p = lax.rem(me + n - d, n)
        pltpu.make_async_remote_copy(
            src_ref=held.at[p],
            dst_ref=held.at[p],
            send_sem=send_sems.at[p],
            recv_sem=recv_sems.at[p],
            device_id=device(p),
            device_id_type=MESH_ID,
        ).wait_recv()
        return carry

    lax.fori_loop(1, n, receive, 0)

    def sent(d, carry):
        outgoing(d).wait_send()
        return carry

    lax.fori_loop(1, n, sent, 0)
    if gather:
        o_ref[...] = held[...]
    else:
        o_ref[...] = lax.fori_loop(1, n, lambda j, acc: acc + held[j], held[0])


def exchange(x, axis, n, gather, collective_id):
    chunk = x.shape if gather else x.shape[1:]
    out_shape = (n,) + chunk if gather else chunk
    return pl.pallas_call(
        functools.partial(exchange_kernel, axis, gather),
        out_shape=jax.ShapeDtypeStruct(out_shape, jnp.float32),
        in_specs=[pl.BlockSpec(memory_space=pltpu.VMEM)],
        out_specs=pl.BlockSpec(memory_space=pltpu.VMEM),
        scratch_shapes=[
            pltpu.VMEM((n,) + chunk, jnp.float32),
            pltpu.SemaphoreType.DMA((n,)),
            pltpu.SemaphoreType.DMA((n,)),
        ],
        compiler_params=pltpu.CompilerParams(collective_id=collective_id, has_side_effects=True),
    )(x)


def pair_scatter_kernel(x_ref, o_ref, pair_buf, pair_sum, held, sems_a, sems_b, sems_c, sems_d):
    n = x_ref.shape[0]
    chips = n // 2
    s = lax.axis_index("site")
    k = lax.axis_index("branch")
    core = s % 2
    chip = s // 2
    partner = s - core + (1 - core)
    barrier = pltpu.get_barrier_semaphore()
    pl.semaphore_signal(barrier, inc=1, device_id=(partner, k), device_id_type=MESH_ID)

    def greet(d, carry):
        peer = 2 * lax.rem(chip + d, chips) + core
        pl.semaphore_signal(barrier, inc=1, device_id=(peer, k), device_id_type=MESH_ID)
        return carry

    lax.fori_loop(1, chips, greet, 0)
    pl.semaphore_wait(barrier, chips)

    def to_partner(m):
        return pltpu.make_async_remote_copy(
            src_ref=x_ref.at[2 * m + 1 - core],
            dst_ref=pair_buf.at[m],
            send_sem=sems_a.at[m],
            recv_sem=sems_b.at[m],
            device_id=(partner, k),
            device_id_type=MESH_ID,
        )

    def first_send(m, carry):
        to_partner(m).start()
        return carry

    lax.fori_loop(0, chips, first_send, 0)

    def to_chip(c):
        return pltpu.make_async_remote_copy(
            src_ref=pair_sum.at[c],
            dst_ref=held.at[chip],
            send_sem=sems_c.at[c],
            recv_sem=sems_d.at[chip],
            device_id=(2 * c + core, k),
            device_id_type=MESH_ID,
        )

    to_partner(chip).wait_recv()
    pair_sum[chip] = x_ref[2 * chip + core] + pair_buf[chip]
    held[chip] = pair_sum[chip]

    def add_and_send(d, carry):
        c = lax.rem(chip + d, chips)
        to_partner(c).wait_recv()
        pair_sum[c] = x_ref[2 * c + core] + pair_buf[c]
        to_chip(c).start()
        return carry

    lax.fori_loop(1, chips, add_and_send, 0)

    def second_recv(d, carry):
        c = lax.rem(chip + chips - d, chips)
        pltpu.make_async_remote_copy(
            src_ref=held.at[c],
            dst_ref=held.at[c],
            send_sem=sems_c.at[c],
            recv_sem=sems_d.at[c],
            device_id=(2 * c + core, k),
            device_id_type=MESH_ID,
        ).wait_recv()
        return carry

    lax.fori_loop(1, chips, second_recv, 0)

    def first_sent(m, carry):
        to_partner(m).wait_send()
        return carry

    lax.fori_loop(0, chips, first_sent, 0)

    def second_sent(d, carry):
        to_chip(lax.rem(chip + d, chips)).wait_send()
        return carry

    lax.fori_loop(1, chips, second_sent, 0)
    o_ref[...] = lax.fori_loop(1, chips, lambda j, acc: acc + held[j], held[0])


def pair_scatter(x, collective_id):
    n = x.shape[0]
    chunk = x.shape[1:]
    return pl.pallas_call(
        pair_scatter_kernel,
        out_shape=jax.ShapeDtypeStruct(chunk, jnp.float32),
        in_specs=[pl.BlockSpec(memory_space=pltpu.VMEM)],
        out_specs=pl.BlockSpec(memory_space=pltpu.VMEM),
        scratch_shapes=[
            pltpu.VMEM((n // 2,) + chunk, jnp.float32),
            pltpu.VMEM((n // 2,) + chunk, jnp.float32),
            pltpu.VMEM((n // 2,) + chunk, jnp.float32),
            pltpu.SemaphoreType.DMA((n // 2,)),
            pltpu.SemaphoreType.DMA((n // 2,)),
            pltpu.SemaphoreType.DMA((n // 2,)),
            pltpu.SemaphoreType.DMA((n // 2,)),
        ],
        compiler_params=pltpu.CompilerParams(collective_id=collective_id, has_side_effects=True),
    )(x)


def pair_gather_kernel(x_ref, o_ref, held, sems_a, sems_b, sems_c, sems_d):
    n = held.shape[0]
    chips = n // 2
    s = lax.axis_index("site")
    k = lax.axis_index("branch")
    core = s % 2
    chip = s // 2
    partner = s - core + (1 - core)
    barrier = pltpu.get_barrier_semaphore()
    pl.semaphore_signal(barrier, inc=1, device_id=(partner, k), device_id_type=MESH_ID)

    def greet(d, carry):
        peer = 2 * lax.rem(chip + d, chips) + core
        pl.semaphore_signal(barrier, inc=1, device_id=(peer, k), device_id_type=MESH_ID)
        return carry

    lax.fori_loop(1, chips, greet, 0)
    pl.semaphore_wait(barrier, chips)
    held[s] = x_ref[...]

    def to_chip(d):
        c = lax.rem(chip + d, chips)
        return pltpu.make_async_remote_copy(
            src_ref=x_ref,
            dst_ref=held.at[s],
            send_sem=sems_a.at[c],
            recv_sem=sems_b.at[chip],
            device_id=(2 * c + core, k),
            device_id_type=MESH_ID,
        )

    def first_send(d, carry):
        to_chip(d).start()
        return carry

    lax.fori_loop(1, chips, first_send, 0)

    def to_partner(c):
        return pltpu.make_async_remote_copy(
            src_ref=held.at[2 * c + core],
            dst_ref=held.at[2 * c + core],
            send_sem=sems_c.at[c],
            recv_sem=sems_d.at[c],
            device_id=(partner, k),
            device_id_type=MESH_ID,
        )

    own = pltpu.make_async_remote_copy(
        src_ref=x_ref,
        dst_ref=held.at[s],
        send_sem=sems_c.at[chip],
        recv_sem=sems_d.at[chip],
        device_id=(partner, k),
        device_id_type=MESH_ID,
    )
    own.start()

    def relay(d, carry):
        c = lax.rem(chip + chips - d, chips)
        pltpu.make_async_remote_copy(
            src_ref=held.at[2 * c + core],
            dst_ref=held.at[2 * c + core],
            send_sem=sems_a.at[c],
            recv_sem=sems_b.at[c],
            device_id=(2 * c + core, k),
            device_id_type=MESH_ID,
        ).wait_recv()
        to_partner(c).start()
        return carry

    lax.fori_loop(1, chips, relay, 0)

    def second_recv(c, carry):
        pltpu.make_async_remote_copy(
            src_ref=held.at[2 * c + 1 - core],
            dst_ref=held.at[2 * c + 1 - core],
            send_sem=sems_c.at[c],
            recv_sem=sems_d.at[c],
            device_id=(partner, k),
            device_id_type=MESH_ID,
        ).wait_recv()
        return carry

    lax.fori_loop(0, chips, second_recv, 0)

    def first_sent(d, carry):
        to_chip(d).wait_send()
        return carry

    lax.fori_loop(1, chips, first_sent, 0)
    own.wait_send()

    def second_sent(d, carry):
        to_partner(lax.rem(chip + d, chips)).wait_send()
        return carry

    lax.fori_loop(1, chips, second_sent, 0)
    o_ref[...] = held[...]


def pair_gather(x, n, collective_id):
    return pl.pallas_call(
        pair_gather_kernel,
        out_shape=jax.ShapeDtypeStruct((n,) + x.shape, jnp.float32),
        in_specs=[pl.BlockSpec(memory_space=pltpu.VMEM)],
        out_specs=pl.BlockSpec(memory_space=pltpu.VMEM),
        scratch_shapes=[
            pltpu.VMEM((n,) + x.shape, jnp.float32),
            pltpu.SemaphoreType.DMA((n // 2,)),
            pltpu.SemaphoreType.DMA((n // 2,)),
            pltpu.SemaphoreType.DMA((n // 2,)),
            pltpu.SemaphoreType.DMA((n // 2,)),
        ],
        compiler_params=pltpu.CompilerParams(collective_id=collective_id, has_side_effects=True),
    )(x)


def body(
    states, gap_mask, weights, leaf_order, exchanges, codon_freq, omega_ratio, lengths, classes
):
    site_count = lax.axis_size("site")
    site_pos = lax.axis_index("site")
    subtree = lax.axis_index("branch")
    site_span = states.shape[1]
    total_sites = site_span * site_count
    total_taxa = LEAF_DEV * lax.axis_size("branch")
    rate_matrix, stationary = build_rates(exchanges, codon_freq, omega_ratio)
    slot_len = jnp.concatenate([lengths, jnp.zeros((1,), lengths.dtype)])
    slot_cls = jnp.concatenate([classes, jnp.zeros((1,), jnp.int32)])
    class_pick = (slot_cls[:, None] == jnp.arange(CLASSES, dtype=jnp.int32)[None, :]).astype(
        jnp.float32
    )
    slot_rates = jnp.einsum("bc,cij->bij", class_pick, rate_matrix, precision=lax.Precision.HIGH)
    scaled = slot_rates * slot_len[:, None, None]
    per_dev = SLOTS // site_count
    own_start = site_pos * per_dev
    own_scaled = lax.dynamic_slice_in_dim(scaled, own_start, per_dev, 0)
    own_pull = None
    own_probs, own_pull = jax.vjp(expm_taylor, own_scaled)
    dense = pair_gather(own_probs.reshape(-1, 128), site_count, 1)
    probs = dense.reshape((site_count * per_dev,) + own_probs.shape[1:])
    taxon_rows = lax.dynamic_slice_in_dim(leaf_order, subtree * LEAF_DEV, LEAF_DEV, 0)
    leaves = leaf_partials(
        jnp.take(states, taxon_rows, axis=0), jnp.take(gap_mask, taxon_rows, axis=0)
    )
    levels, messages, logscale = up_pass(probs, leaves)
    top_pack = jnp.concatenate([messages[-1][0], logscale[None, :]], axis=0)
    top_all = exchange(top_pack, "branch", lax.axis_size("branch"), True, 3)
    top_messages, top_logs = top_all[:, :64, :], top_all[:, 64, :]
    site_ll, above_all = root_terms(stationary, top_messages, top_logs)
    site_weight = weights.astype(jnp.float32)
    loglik_part = jnp.sum(site_weight * site_ll)
    above_top = lax.dynamic_slice_in_dim(above_all, subtree, 1, 0)
    a_list = down_pass(probs, levels, messages, above_top)
    weighted = weigh(a_list, messages, site_weight, total_sites)
    padding = jnp.zeros((1, 64, site_span), jnp.float32)
    weighted_all = jnp.concatenate(weighted + [padding], axis=0)
    partial_all = jnp.concatenate(levels + [padding], axis=0)
    part_above = lax.slice_in_dim(weighted_all, 0, lax.axis_size("site") * per_dev, axis=0)
    part_below = lax.slice_in_dim(partial_all, 0, lax.axis_size("site") * per_dev, axis=0)
    part_counts = jnp.einsum("bis,bjs->bij", part_above, part_below, precision=lax.Precision.HIGH)
    own_counts = pair_scatter(part_counts.reshape(site_count, -1, 128), 2).reshape((per_dev, 64, 64))
    d_scaled = own_pull(own_counts)[0]
    use_rates = lax.dynamic_slice_in_dim(slot_rates, own_start, per_dev, 0)
    use_len = lax.dynamic_slice_in_dim(slot_len, own_start, per_dev, 0)
    use_pick = lax.dynamic_slice_in_dim(class_pick, own_start, per_dev, 0)
    d_length = jnp.sum(d_scaled * use_rates, axis=(1, 2))
    d_rates = jnp.einsum(
        "bc,bij->cij", use_pick, d_scaled * use_len[:, None, None], precision=lax.Precision.HIGH
    )
    unused_rates, pull_rates = jax.vjp(
        lambda table, ratio: build_rates(table, codon_freq, ratio)[0], exchanges, omega_ratio
    )
    d_exch, d_omega = pull_rates(d_rates)
    n_branch = lax.axis_size("branch")
    length_slab = jnp.zeros((n_branch, SLOTS), jnp.float32)
    length_slab = lax.dynamic_update_slice(length_slab, d_length[None, :], (subtree, own_start))
    loglik_keep = jnp.where(subtree == 0, loglik_part, jnp.float32(0.0))
    packed = jnp.concatenate(
        [d_exch.reshape(-1), d_omega, length_slab.reshape(-1), loglik_keep[None]]
    )
    rows = -(-packed.shape[0] // (8 * 128)) * 8
    packed = jnp.pad(packed, (0, rows * 128 - packed.shape[0])).reshape(rows, 128)
    summed = allreduce_all(packed, site_count, n_branch).reshape(-1)
    grad_exch = summed[: 64 * 64].reshape(64, 64)
    grad_omega = summed[64 * 64 : 64 * 64 + CLASSES]
    length_all = summed[64 * 64 + CLASSES : 64 * 64 + CLASSES + n_branch * SLOTS].reshape(n_branch, SLOTS)
    log_total = summed[64 * 64 + CLASSES + n_branch * SLOTS]
    loglik = log_total / total_sites / total_taxa
    length_out = lax.dynamic_index_in_dim(length_all, subtree, 0, keepdims=False)[:EDGES]
    return (grad_exch, grad_omega, length_out, loglik)


def solution(mesh):
    return jax.shard_map(
        body,
        mesh=mesh,
        in_specs=(
            P(None, "site"),
            P(None, "site"),
            P("site"),
            P(),
            P(),
            P(),
            P(),
            P("branch"),
            P("branch"),
        ),
        out_specs=(P(), P(), P("branch"), P()),
        check_vma=False,
    )
```

```python
import jax
import jax.numpy as jnp
import numpy as np
from jax import lax
from jax.sharding import PartitionSpec as P
from jax.experimental import pallas as pl
from jax.experimental.pallas import tpu as pltpu
import functools

MESH_ID = pl.DeviceIdType.MESH

LEVELS = 6
LEAF_DEV = 64
EDGES = 127
SLOTS = 128
CLASSES = 8


CODE_TABLE = "FFLLSSSSYYXXCCXWLLLLPPPPHHQQRRRRIIIMTTTTNNKKSSRRVVVVAAAADDEEGGGG"


def codon_tables():
    amino_acid = np.array(list(CODE_TABLE))
    codon_index = np.arange(64)
    digits = np.stack([codon_index // 16, codon_index // 4 % 4, codon_index % 4], 1)
    differ = (digits[:, None, :] != digits[None, :, :]).sum(-1)
    is_sense = amino_acid != "X"
    single = (differ == 1) & is_sense[:, None] & is_sense[None, :]
    nonsyn = single & (amino_acid[:, None] != amino_acid[None, :])
    return (is_sense.astype(np.float32), single.astype(np.float32), nonsyn.astype(np.float32))


def build_rates(exchanges, codon_freq, omega_ratio):
    is_sense, single, nonsyn = codon_tables()
    stationary = codon_freq * is_sense / jnp.sum(codon_freq * is_sense)
    symmetric = 0.5 * (exchanges + exchanges.T)
    factor = 1.0 + nonsyn[None, :, :] * (omega_ratio[:, None, None] - 1.0)
    off_diag = symmetric[None, :, :] * stationary[None, None, :] * factor * single[None, :, :]
    row_total = jnp.sum(off_diag, axis=2)
    mean_rate = jnp.sum(stationary[None, :] * row_total, axis=1)
    identity = jnp.eye(64, dtype=exchanges.dtype)
    rate_matrix = (off_diag - row_total[:, :, None] * identity[None]) / mean_rate[:, None, None]
    return (rate_matrix, stationary)


def product(left, right):
    return jnp.einsum("bij,bjk->bik", left, right, precision=lax.Precision.HIGH)


def expm_taylor(scaled):
    reduced = scaled / 16.0
    identity = jnp.eye(64, dtype=scaled.dtype)
    series = jnp.broadcast_to(identity, scaled.shape)
    for degree in range(8, 0, -1):
        series = identity + product(reduced, series) / degree
    for square_step in range(4):
        series = product(series, series)
    return series


def forward(probs, vectors):
    return jnp.einsum("bij,bjs->bis", probs, vectors, precision=lax.Precision.HIGH)


def carried(probs, vectors):
    return jnp.einsum("bji,bjs->bis", probs, vectors, precision=lax.Precision.HIGH)


def leaf_partials(leaf_states, gap_rows):
    codon_axis = jnp.arange(64, dtype=jnp.int32)
    indicator = (leaf_states[:, None, :] == codon_axis[None, :, None]).astype(jnp.float32)
    return jnp.where(gap_rows[:, None, :] > 0, jnp.float32(1.0), indicator)


def up_pass(probs, leaves):
    levels = [leaves]
    messages = []
    logscale = jnp.zeros(leaves.shape[2:], jnp.float32)
    current = leaves
    for height in range(LEVELS):
        amount = current.shape[0]
        offset = 2 * LEAF_DEV - 2 * amount
        message = forward(probs[offset : offset + amount], current)
        messages.append(message)
        raw_parent = message[0::2] * message[1::2]
        scaling = jnp.sum(raw_parent, axis=1)
        current = raw_parent / scaling[:, None, :]
        logscale = logscale + jnp.sum(jnp.log(scaling), axis=0)
        levels.append(current)
    messages.append(forward(probs[EDGES - 1 : EDGES], current))
    return (levels, messages, logscale)


def root_terms(stationary, top_messages, top_logs):
    members = top_messages.shape[0]
    joint = stationary[:, None] * top_messages[0]
    for member in range(1, members):
        joint = joint * top_messages[member]
    site_ll = jnp.log(jnp.sum(joint, axis=0)) + jnp.sum(top_logs, axis=0)
    above_list = []
    for member in range(members):
        vector = jnp.broadcast_to(stationary[:, None], top_messages.shape[1:])
        for other in range(members):
            if other != member:
                vector = vector * top_messages[other]
        above_list.append(vector)
    return (site_ll, jnp.stack(above_list))


def down_pass(probs, levels, messages, above_top):
    a_list = [above_top]
    current = above_top
    for height in range(LEVELS, 0, -1):
        amount = levels[height].shape[0]
        offset = 2 * LEAF_DEV - 2 * amount
        down_part = carried(probs[offset : offset + amount], current)
        down_part = down_part / jnp.sum(down_part, axis=1, keepdims=True)
        message = messages[height - 1]
        current = jnp.stack([down_part * message[1::2], down_part * message[0::2]], axis=1).reshape(
            message.shape
        )
        a_list.append(current)
    return a_list[::-1]


def weigh(a_list, messages, site_weight, total_sites):
    weighted = []
    for vector, message in zip(a_list, messages):
        likelihood = jnp.sum(vector * message, axis=1)
        weighted.append(vector * (site_weight / (likelihood * total_sites))[:, None, :])
    return weighted


def sum_groups(n_site, n_branch):
    s = lax.axis_index("site")
    k = lax.axis_index("branch")
    core = s % 2
    plane = s // 2
    return [
        (2, core, lambda c: (s - core + c, k)),
        (n_branch, k, lambda c: (s, c)),
        (n_site // 2, plane, lambda c: (2 * c + core, k)),
    ]


def allreduce_kernel(n_site, n_branch, x_ref, o_ref, held, send_sems, recv_sems):
    stages = sum_groups(n_site, n_branch)
    barrier = pltpu.get_barrier_semaphore()
    count = 0
    for size, mine, where in stages:
        for d in range(1, size):
            other = lax.rem(mine + d, size)
            pl.semaphore_signal(barrier, inc=1, device_id=where(other), device_id_type=MESH_ID)
            count += 1
    pl.semaphore_wait(barrier, count)
    total = x_ref[...]
    for st, (size, mine, where) in enumerate(stages):
        held[st, mine] = total
        sends = []
        for d in range(1, size):
            other = lax.rem(mine + d, size)
            copy = pltpu.make_async_remote_copy(
                src_ref=held.at[st, mine],
                dst_ref=held.at[st, mine],
                send_sem=send_sems.at[st, other],
                recv_sem=recv_sems.at[st, mine],
                device_id=where(other),
                device_id_type=MESH_ID,
            )
            copy.start()
            sends.append(copy)
        for d in range(1, size):
            other = lax.rem(mine + d, size)
            incoming = pltpu.make_async_remote_copy(
                src_ref=held.at[st, other],
                dst_ref=held.at[st, other],
                send_sem=send_sems.at[st, other],
                recv_sem=recv_sems.at[st, other],
                device_id=where(other),
                device_id_type=MESH_ID,
            )
            incoming.wait_recv()
        for copy in sends:
            copy.wait_send()
        total = held[st, 0]
        for c in range(1, size):
            total = total + held[st, c]
    o_ref[...] = total


def allreduce_all(x, n_site, n_branch):
    rows = x.shape[0]
    return pl.pallas_call(
        functools.partial(allreduce_kernel, n_site, n_branch),
        out_shape=jax.ShapeDtypeStruct(x.shape, jnp.float32),
        in_specs=[pl.BlockSpec(memory_space=pltpu.VMEM)],
        out_specs=pl.BlockSpec(memory_space=pltpu.VMEM),
        scratch_shapes=[
            pltpu.VMEM((3, n_site // 2, rows, 128), jnp.float32),
            pltpu.SemaphoreType.DMA((3, n_site // 2)),
            pltpu.SemaphoreType.DMA((3, n_site // 2)),
        ],
        compiler_params=pltpu.CompilerParams(collective_id=0, has_side_effects=True),
    )(x)


def exchange_kernel(axis, gather, x_ref, o_ref, held, send_sems, recv_sems):
    n = held.shape[0]
    me = lax.axis_index(axis)
    other_axis = "branch" if axis == "site" else "site"
    fixed = lax.axis_index(other_axis)

    def device(p):
        return (p, fixed) if axis == "site" else (fixed, p)

    barrier = pltpu.get_barrier_semaphore()

    def greet(d, carry):
        pl.semaphore_signal(
            barrier, inc=1, device_id=device(lax.rem(me + d, n)), device_id_type=MESH_ID
        )
        return carry

    lax.fori_loop(1, n, greet, 0)
    pl.semaphore_wait(barrier, n - 1)
    if gather:
        held[me] = x_ref[...]
    else:
        held[me] = x_ref[me]

    def outgoing(d):
        p = lax.rem(me + d, n)
        return pltpu.make_async_remote_copy(
            src_ref=x_ref if gather else x_ref.at[p],
            dst_ref=held.at[me],
            send_sem=send_sems.at[p],
            recv_sem=recv_sems.at[me],
            device_id=device(p),
            device_id_type=MESH_ID,
        )

    def send(d, carry):
        outgoing(d).start()
        return carry

    lax.fori_loop(1, n, send, 0)

    def receive(d, carry):
        p = lax.rem(me + n - d, n)
        pltpu.make_async_remote_copy(
            src_ref=held.at[p],
            dst_ref=held.at[p],
            send_sem=send_sems.at[p],
            recv_sem=recv_sems.at[p],
            device_id=device(p),
            device_id_type=MESH_ID,
        ).wait_recv()
        return carry

    lax.fori_loop(1, n, receive, 0)

    def sent(d, carry):
        outgoing(d).wait_send()
        return carry

    lax.fori_loop(1, n, sent, 0)
    if gather:
        o_ref[...] = held[...]
    else:
        o_ref[...] = lax.fori_loop(1, n, lambda j, acc: acc + held[j], held[0])


def exchange(x, axis, n, gather, collective_id):
    chunk = x.shape if gather else x.shape[1:]
    out_shape = (n,) + chunk if gather else chunk
    return pl.pallas_call(
        functools.partial(exchange_kernel, axis, gather),
        out_shape=jax.ShapeDtypeStruct(out_shape, jnp.float32),
        in_specs=[pl.BlockSpec(memory_space=pltpu.VMEM)],
        out_specs=pl.BlockSpec(memory_space=pltpu.VMEM),
        scratch_shapes=[
            pltpu.VMEM((n,) + chunk, jnp.float32),
            pltpu.SemaphoreType.DMA((n,)),
            pltpu.SemaphoreType.DMA((n,)),
        ],
        compiler_params=pltpu.CompilerParams(collective_id=collective_id, has_side_effects=True),
    )(x)


def pair_scatter_kernel(x_ref, o_ref, pair_buf, pair_sum, held, sems_a, sems_b, sems_c, sems_d):
    n = x_ref.shape[0]
    chips = n // 2
    s = lax.axis_index("site")
    k = lax.axis_index("branch")
    core = s % 2
    chip = s // 2
    partner = s - core + (1 - core)
    barrier = pltpu.get_barrier_semaphore()
    pl.semaphore_signal(barrier, inc=1, device_id=(partner, k), device_id_type=MESH_ID)

    def greet(d, carry):
        peer = 2 * lax.rem(chip + d, chips) + core
        pl.semaphore_signal(barrier, inc=1, device_id=(peer, k), device_id_type=MESH_ID)
        return carry

    lax.fori_loop(1, chips, greet, 0)
    pl.semaphore_wait(barrier, chips)

    def to_partner(m):
        return pltpu.make_async_remote_copy(
            src_ref=x_ref.at[2 * m + 1 - core],
            dst_ref=pair_buf.at[m],
            send_sem=sems_a.at[m],
            recv_sem=sems_b.at[m],
            device_id=(partner, k),
            device_id_type=MESH_ID,
        )

    def first_send(m, carry):
        to_partner(m).start()
        return carry

    lax.fori_loop(0, chips, first_send, 0)

    def to_chip(c):
        return pltpu.make_async_remote_copy(
            src_ref=pair_sum.at[c],
            dst_ref=held.at[chip],
            send_sem=sems_c.at[c],
            recv_sem=sems_d.at[chip],
            device_id=(2 * c + core, k),
            device_id_type=MESH_ID,
        )

    to_partner(chip).wait_recv()
    pair_sum[chip] = x_ref[2 * chip + core] + pair_buf[chip]
    held[chip] = pair_sum[chip]

    def add_and_send(d, carry):
        c = lax.rem(chip + d, chips)
        to_partner(c).wait_recv()
        pair_sum[c] = x_ref[2 * c + core] + pair_buf[c]
        to_chip(c).start()
        return carry

    lax.fori_loop(1, chips, add_and_send, 0)

    def second_recv(d, carry):
        c = lax.rem(chip + chips - d, chips)
        pltpu.make_async_remote_copy(
            src_ref=held.at[c],
            dst_ref=held.at[c],
            send_sem=sems_c.at[c],
            recv_sem=sems_d.at[c],
            device_id=(2 * c + core, k),
            device_id_type=MESH_ID,
        ).wait_recv()
        return carry

    lax.fori_loop(1, chips, second_recv, 0)

    def first_sent(m, carry):
        to_partner(m).wait_send()
        return carry

    lax.fori_loop(0, chips, first_sent, 0)

    def second_sent(d, carry):
        to_chip(lax.rem(chip + d, chips)).wait_send()
        return carry

    lax.fori_loop(1, chips, second_sent, 0)
    o_ref[...] = lax.fori_loop(1, chips, lambda j, acc: acc + held[j], held[0])


def pair_scatter(x, collective_id):
    n = x.shape[0]
    chunk = x.shape[1:]
    return pl.pallas_call(
        pair_scatter_kernel,
        out_shape=jax.ShapeDtypeStruct(chunk, jnp.float32),
        in_specs=[pl.BlockSpec(memory_space=pltpu.VMEM)],
        out_specs=pl.BlockSpec(memory_space=pltpu.VMEM),
        scratch_shapes=[
            pltpu.VMEM((n // 2,) + chunk, jnp.float32),
            pltpu.VMEM((n // 2,) + chunk, jnp.float32),
            pltpu.VMEM((n // 2,) + chunk, jnp.float32),
            pltpu.SemaphoreType.DMA((n // 2,)),
            pltpu.SemaphoreType.DMA((n // 2,)),
            pltpu.SemaphoreType.DMA((n // 2,)),
            pltpu.SemaphoreType.DMA((n // 2,)),
        ],
        compiler_params=pltpu.CompilerParams(collective_id=collective_id, has_side_effects=True),
    )(x)


def pair_gather_kernel(x_ref, o_ref, held, sems_a, sems_b, sems_c, sems_d):
    n = held.shape[0]
    chips = n // 2
    s = lax.axis_index("site")
    k = lax.axis_index("branch")
    core = s % 2
    chip = s // 2
    partner = s - core + (1 - core)
    barrier = pltpu.get_barrier_semaphore()
    pl.semaphore_signal(barrier, inc=1, device_id=(partner, k), device_id_type=MESH_ID)

    def greet(d, carry):
        peer = 2 * lax.rem(chip + d, chips) + core
        pl.semaphore_signal(barrier, inc=1, device_id=(peer, k), device_id_type=MESH_ID)
        return carry

    lax.fori_loop(1, chips, greet, 0)
    pl.semaphore_wait(barrier, chips)
    held[s] = x_ref[...]

    def to_chip(d):
        c = lax.rem(chip + d, chips)
        return pltpu.make_async_remote_copy(
            src_ref=x_ref,
            dst_ref=held.at[s],
            send_sem=sems_a.at[c],
            recv_sem=sems_b.at[chip],
            device_id=(2 * c + core, k),
            device_id_type=MESH_ID,
        )

    def first_send(d, carry):
        to_chip(d).start()
        return carry

    lax.fori_loop(1, chips, first_send, 0)

    def to_partner(c):
        return pltpu.make_async_remote_copy(
            src_ref=held.at[2 * c + core],
            dst_ref=held.at[2 * c + core],
            send_sem=sems_c.at[c],
            recv_sem=sems_d.at[c],
            device_id=(partner, k),
            device_id_type=MESH_ID,
        )

    own = pltpu.make_async_remote_copy(
        src_ref=x_ref,
        dst_ref=held.at[s],
        send_sem=sems_c.at[chip],
        recv_sem=sems_d.at[chip],
        device_id=(partner, k),
        device_id_type=MESH_ID,
    )
    own.start()

    def relay(d, carry):
        c = lax.rem(chip + chips - d, chips)
        pltpu.make_async_remote_copy(
            src_ref=held.at[2 * c + core],
            dst_ref=held.at[2 * c + core],
            send_sem=sems_a.at[c],
            recv_sem=sems_b.at[c],
            device_id=(2 * c + core, k),
            device_id_type=MESH_ID,
        ).wait_recv()
        to_partner(c).start()
        return carry

    lax.fori_loop(1, chips, relay, 0)

    def second_recv(c, carry):
        pltpu.make_async_remote_copy(
            src_ref=held.at[2 * c + 1 - core],
            dst_ref=held.at[2 * c + 1 - core],
            send_sem=sems_c.at[c],
            recv_sem=sems_d.at[c],
            device_id=(partner, k),
            device_id_type=MESH_ID,
        ).wait_recv()
        return carry

    lax.fori_loop(0, chips, second_recv, 0)

    def first_sent(d, carry):
        to_chip(d).wait_send()
        return carry

    lax.fori_loop(1, chips, first_sent, 0)
    own.wait_send()

    def second_sent(d, carry):
        to_partner(lax.rem(chip + d, chips)).wait_send()
        return carry

    lax.fori_loop(1, chips, second_sent, 0)
    o_ref[...] = held[...]


def pair_gather(x, n, collective_id):
    return pl.pallas_call(
        pair_gather_kernel,
        out_shape=jax.ShapeDtypeStruct((n,) + x.shape, jnp.float32),
        in_specs=[pl.BlockSpec(memory_space=pltpu.VMEM)],
        out_specs=pl.BlockSpec(memory_space=pltpu.VMEM),
        scratch_shapes=[
            pltpu.VMEM((n,) + x.shape, jnp.float32),
            pltpu.SemaphoreType.DMA((n // 2,)),
            pltpu.SemaphoreType.DMA((n // 2,)),
            pltpu.SemaphoreType.DMA((n // 2,)),
            pltpu.SemaphoreType.DMA((n // 2,)),
        ],
        compiler_params=pltpu.CompilerParams(collective_id=collective_id, has_side_effects=True),
    )(x)


def body(
    states, gap_mask, weights, leaf_order, exchanges, codon_freq, omega_ratio, lengths, classes
):
    site_count = lax.axis_size("site")
    site_pos = lax.axis_index("site")
    subtree = lax.axis_index("branch")
    site_span = states.shape[1]
    total_sites = site_span * site_count
    total_taxa = LEAF_DEV * lax.axis_size("branch")
    rate_matrix, stationary = build_rates(exchanges, codon_freq, omega_ratio)
    slot_len = jnp.concatenate([lengths, jnp.zeros((1,), lengths.dtype)])
    slot_cls = jnp.concatenate([classes, jnp.zeros((1,), jnp.int32)])
    class_pick = (slot_cls[:, None] == jnp.arange(CLASSES, dtype=jnp.int32)[None, :]).astype(
        jnp.float32
    )
    slot_rates = jnp.einsum("bc,cij->bij", class_pick, rate_matrix, precision=lax.Precision.HIGH)
    scaled = slot_rates * slot_len[:, None, None]
    per_dev = SLOTS // site_count
    own_start = site_pos * per_dev
    own_scaled = lax.dynamic_slice_in_dim(scaled, own_start, per_dev, 0)
    own_pull = None
    own_probs, own_pull = jax.vjp(expm_taylor, own_scaled)
    dense = pair_gather(own_probs.reshape(-1, 128), site_count, 1)
    probs = dense.reshape((site_count * per_dev,) + own_probs.shape[1:])
    taxon_rows = lax.dynamic_slice_in_dim(leaf_order, subtree * LEAF_DEV, LEAF_DEV, 0)
    leaves = leaf_partials(
        jnp.take(states, taxon_rows, axis=0), jnp.take(gap_mask, taxon_rows, axis=0)
    )
    levels, messages, logscale = up_pass(probs, leaves)
    top_pack = jnp.concatenate([messages[-1][0], logscale[None, :]], axis=0)
    top_all = lax.all_gather(top_pack, "branch", axis=0, tiled=False)
    top_messages, top_logs = top_all[:, :64, :], top_all[:, 64, :]
    site_ll, above_all = root_terms(stationary, top_messages, top_logs)
    site_weight = weights.astype(jnp.float32)
    loglik_part = jnp.sum(site_weight * site_ll)
    above_top = lax.dynamic_slice_in_dim(above_all, subtree, 1, 0)
    a_list = down_pass(probs, levels, messages, above_top)
    weighted = weigh(a_list, messages, site_weight, total_sites)
    padding = jnp.zeros((1, 64, site_span), jnp.float32)
    weighted_all = jnp.concatenate(weighted + [padding], axis=0)
    partial_all = jnp.concatenate(levels + [padding], axis=0)
    part_above = lax.slice_in_dim(weighted_all, 0, lax.axis_size("site") * per_dev, axis=0)
    part_below = lax.slice_in_dim(partial_all, 0, lax.axis_size("site") * per_dev, axis=0)
    part_counts = jnp.einsum("bis,bjs->bij", part_above, part_below, precision=lax.Precision.HIGH)
    own_counts = pair_scatter(part_counts.reshape(site_count, -1, 128), 2).reshape((per_dev, 64, 64))
    d_scaled = own_pull(own_counts)[0]
    use_rates = lax.dynamic_slice_in_dim(slot_rates, own_start, per_dev, 0)
    use_len = lax.dynamic_slice_in_dim(slot_len, own_start, per_dev, 0)
    use_pick = lax.dynamic_slice_in_dim(class_pick, own_start, per_dev, 0)
    d_length = jnp.sum(d_scaled * use_rates, axis=(1, 2))
    d_rates = jnp.einsum(
        "bc,bij->cij", use_pick, d_scaled * use_len[:, None, None], precision=lax.Precision.HIGH
    )
    unused_rates, pull_rates = jax.vjp(
        lambda table, ratio: build_rates(table, codon_freq, ratio)[0], exchanges, omega_ratio
    )
    d_exch, d_omega = pull_rates(d_rates)
    n_branch = lax.axis_size("branch")
    length_slab = jnp.zeros((n_branch, SLOTS), jnp.float32)
    length_slab = lax.dynamic_update_slice(length_slab, d_length[None, :], (subtree, own_start))
    loglik_keep = jnp.where(subtree == 0, loglik_part, jnp.float32(0.0))
    packed = jnp.concatenate(
        [d_exch.reshape(-1), d_omega, length_slab.reshape(-1), loglik_keep[None]]
    )
    rows = -(-packed.shape[0] // (8 * 128)) * 8
    packed = jnp.pad(packed, (0, rows * 128 - packed.shape[0])).reshape(rows, 128)
    summed = allreduce_all(packed, site_count, n_branch).reshape(-1)
    grad_exch = summed[: 64 * 64].reshape(64, 64)
    grad_omega = summed[64 * 64 : 64 * 64 + CLASSES]
    length_all = summed[64 * 64 + CLASSES : 64 * 64 + CLASSES + n_branch * SLOTS].reshape(n_branch, SLOTS)
    log_total = summed[64 * 64 + CLASSES + n_branch * SLOTS]
    loglik = log_total / total_sites / total_taxa
    length_out = lax.dynamic_index_in_dim(length_all, subtree, 0, keepdims=False)[:EDGES]
    return (grad_exch, grad_omega, length_out, loglik)


def solution(mesh):
    return jax.shard_map(
        body,
        mesh=mesh,
        in_specs=(
            P(None, "site"),
            P(None, "site"),
            P("site"),
            P(),
            P(),
            P(),
            P(),
            P("branch"),
            P("branch"),
        ),
        out_specs=(P(), P(), P("branch"), P()),
        check_vma=False,
    )
```

```python
import jax
import jax.numpy as jnp
import numpy as np
from jax import lax
from jax.sharding import PartitionSpec as P
from jax.experimental import pallas as pl
from jax.experimental.pallas import tpu as pltpu
import functools

MESH_ID = pl.DeviceIdType.MESH

LEVELS = 6
LEAF_DEV = 64
EDGES = 127
SLOTS = 128
CLASSES = 8


CODE_TABLE = "FFLLSSSSYYXXCCXWLLLLPPPPHHQQRRRRIIIMTTTTNNKKSSRRVVVVAAAADDEEGGGG"


def codon_tables():
    amino_acid = np.array(list(CODE_TABLE))
    codon_index = np.arange(64)
    digits = np.stack([codon_index // 16, codon_index // 4 % 4, codon_index % 4], 1)
    differ = (digits[:, None, :] != digits[None, :, :]).sum(-1)
    is_sense = amino_acid != "X"
    single = (differ == 1) & is_sense[:, None] & is_sense[None, :]
    nonsyn = single & (amino_acid[:, None] != amino_acid[None, :])
    return (is_sense.astype(np.float32), single.astype(np.float32), nonsyn.astype(np.float32))


def build_rates(exchanges, codon_freq, omega_ratio):
    is_sense, single, nonsyn = codon_tables()
    stationary = codon_freq * is_sense / jnp.sum(codon_freq * is_sense)
    symmetric = 0.5 * (exchanges + exchanges.T)
    factor = 1.0 + nonsyn[None, :, :] * (omega_ratio[:, None, None] - 1.0)
    off_diag = symmetric[None, :, :] * stationary[None, None, :] * factor * single[None, :, :]
    row_total = jnp.sum(off_diag, axis=2)
    mean_rate = jnp.sum(stationary[None, :] * row_total, axis=1)
    identity = jnp.eye(64, dtype=exchanges.dtype)
    rate_matrix = (off_diag - row_total[:, :, None] * identity[None]) / mean_rate[:, None, None]
    return (rate_matrix, stationary)


def product(left, right):
    return jnp.einsum("bij,bjk->bik", left, right, precision=lax.Precision.HIGH)


def expm_taylor(scaled):
    reduced = scaled / 16.0
    identity = jnp.eye(64, dtype=scaled.dtype)
    series = jnp.broadcast_to(identity, scaled.shape)
    for degree in range(8, 0, -1):
        series = identity + product(reduced, series) / degree
    for square_step in range(4):
        series = product(series, series)
    return series


def forward(probs, vectors):
    return jnp.einsum("bij,bjs->bis", probs, vectors, precision=lax.Precision.HIGH)


def carried(probs, vectors):
    return jnp.einsum("bji,bjs->bis", probs, vectors, precision=lax.Precision.HIGH)


def leaf_partials(leaf_states, gap_rows):
    codon_axis = jnp.arange(64, dtype=jnp.int32)
    indicator = (leaf_states[:, None, :] == codon_axis[None, :, None]).astype(jnp.float32)
    return jnp.where(gap_rows[:, None, :] > 0, jnp.float32(1.0), indicator)


def up_pass(probs, leaves):
    levels = [leaves]
    messages = []
    logscale = jnp.zeros(leaves.shape[2:], jnp.float32)
    current = leaves
    for height in range(LEVELS):
        amount = current.shape[0]
        offset = 2 * LEAF_DEV - 2 * amount
        message = forward(probs[offset : offset + amount], current)
        messages.append(message)
        raw_parent = message[0::2] * message[1::2]
        scaling = jnp.sum(raw_parent, axis=1)
        current = raw_parent / scaling[:, None, :]
        logscale = logscale + jnp.sum(jnp.log(scaling), axis=0)
        levels.append(current)
    messages.append(forward(probs[EDGES - 1 : EDGES], current))
    return (levels, messages, logscale)


def root_terms(stationary, top_messages, top_logs):
    members = top_messages.shape[0]
    joint = stationary[:, None] * top_messages[0]
    for member in range(1, members):
        joint = joint * top_messages[member]
    site_ll = jnp.log(jnp.sum(joint, axis=0)) + jnp.sum(top_logs, axis=0)
    above_list = []
    for member in range(members):
        vector = jnp.broadcast_to(stationary[:, None], top_messages.shape[1:])
        for other in range(members):
            if other != member:
                vector = vector * top_messages[other]
        above_list.append(vector)
    return (site_ll, jnp.stack(above_list))


def down_pass(probs, levels, messages, above_top):
    a_list = [above_top]
    current = above_top
    for height in range(LEVELS, 0, -1):
        amount = levels[height].shape[0]
        offset = 2 * LEAF_DEV - 2 * amount
        down_part = carried(probs[offset : offset + amount], current)
        down_part = down_part / jnp.sum(down_part, axis=1, keepdims=True)
        message = messages[height - 1]
        current = jnp.stack([down_part * message[1::2], down_part * message[0::2]], axis=1).reshape(
            message.shape
        )
        a_list.append(current)
    return a_list[::-1]


def weigh(a_list, messages, site_weight, total_sites):
    weighted = []
    for vector, message in zip(a_list, messages):
        likelihood = jnp.sum(vector * message, axis=1)
        weighted.append(vector * (site_weight / (likelihood * total_sites))[:, None, :])
    return weighted


def sum_groups(n_site, n_branch):
    s = lax.axis_index("site")
    k = lax.axis_index("branch")
    core = s % 2
    plane = s // 2
    return [
        (2, core, lambda c: (s - core + c, k)),
        (n_branch, k, lambda c: (s, c)),
        (n_site // 2, plane, lambda c: (2 * c + core, k)),
    ]


def allreduce_kernel(n_site, n_branch, x_ref, o_ref, held, send_sems, recv_sems):
    stages = sum_groups(n_site, n_branch)
    barrier = pltpu.get_barrier_semaphore()
    count = 0
    for size, mine, where in stages:
        for d in range(1, size):
            other = lax.rem(mine + d, size)
            pl.semaphore_signal(barrier, inc=1, device_id=where(other), device_id_type=MESH_ID)
            count += 1
    pl.semaphore_wait(barrier, count)
    total = x_ref[...]
    for st, (size, mine, where) in enumerate(stages):
        held[st, mine] = total
        sends = []
        for d in range(1, size):
            other = lax.rem(mine + d, size)
            copy = pltpu.make_async_remote_copy(
                src_ref=held.at[st, mine],
                dst_ref=held.at[st, mine],
                send_sem=send_sems.at[st, other],
                recv_sem=recv_sems.at[st, mine],
                device_id=where(other),
                device_id_type=MESH_ID,
            )
            copy.start()
            sends.append(copy)
        for d in range(1, size):
            other = lax.rem(mine + d, size)
            incoming = pltpu.make_async_remote_copy(
                src_ref=held.at[st, other],
                dst_ref=held.at[st, other],
                send_sem=send_sems.at[st, other],
                recv_sem=recv_sems.at[st, other],
                device_id=where(other),
                device_id_type=MESH_ID,
            )
            incoming.wait_recv()
        for copy in sends:
            copy.wait_send()
        total = held[st, 0]
        for c in range(1, size):
            total = total + held[st, c]
    o_ref[...] = total


def allreduce_all(x, n_site, n_branch):
    rows = x.shape[0]
    return pl.pallas_call(
        functools.partial(allreduce_kernel, n_site, n_branch),
        out_shape=jax.ShapeDtypeStruct(x.shape, jnp.float32),
        in_specs=[pl.BlockSpec(memory_space=pltpu.VMEM)],
        out_specs=pl.BlockSpec(memory_space=pltpu.VMEM),
        scratch_shapes=[
            pltpu.VMEM((3, n_site // 2, rows, 128), jnp.float32),
            pltpu.SemaphoreType.DMA((3, n_site // 2)),
            pltpu.SemaphoreType.DMA((3, n_site // 2)),
        ],
        compiler_params=pltpu.CompilerParams(collective_id=0, has_side_effects=True),
    )(x)


def exchange_kernel(axis, gather, x_ref, o_ref, held, send_sems, recv_sems):
    n = held.shape[0]
    me = lax.axis_index(axis)
    other_axis = "branch" if axis == "site" else "site"
    fixed = lax.axis_index(other_axis)

    def device(p):
        return (p, fixed) if axis == "site" else (fixed, p)

    barrier = pltpu.get_barrier_semaphore()

    def greet(d, carry):
        pl.semaphore_signal(
            barrier, inc=1, device_id=device(lax.rem(me + d, n)), device_id_type=MESH_ID
        )
        return carry

    lax.fori_loop(1, n, greet, 0)
    pl.semaphore_wait(barrier, n - 1)
    if gather:
        held[me] = x_ref[...]
    else:
        held[me] = x_ref[me]

    def outgoing(d):
        p = lax.rem(me + d, n)
        return pltpu.make_async_remote_copy(
            src_ref=x_ref if gather else x_ref.at[p],
            dst_ref=held.at[me],
            send_sem=send_sems.at[p],
            recv_sem=recv_sems.at[me],
            device_id=device(p),
            device_id_type=MESH_ID,
        )

    def send(d, carry):
        outgoing(d).start()
        return carry

    lax.fori_loop(1, n, send, 0)

    def receive(d, carry):
        p = lax.rem(me + n - d, n)
        pltpu.make_async_remote_copy(
            src_ref=held.at[p],
            dst_ref=held.at[p],
            send_sem=send_sems.at[p],
            recv_sem=recv_sems.at[p],
            device_id=device(p),
            device_id_type=MESH_ID,
        ).wait_recv()
        return carry

    lax.fori_loop(1, n, receive, 0)

    def sent(d, carry):
        outgoing(d).wait_send()
        return carry

    lax.fori_loop(1, n, sent, 0)
    if gather:
        o_ref[...] = held[...]
    else:
        o_ref[...] = lax.fori_loop(1, n, lambda j, acc: acc + held[j], held[0])


def exchange(x, axis, n, gather, collective_id):
    chunk = x.shape if gather else x.shape[1:]
    out_shape = (n,) + chunk if gather else chunk
    return pl.pallas_call(
        functools.partial(exchange_kernel, axis, gather),
        out_shape=jax.ShapeDtypeStruct(out_shape, jnp.float32),
        in_specs=[pl.BlockSpec(memory_space=pltpu.VMEM)],
        out_specs=pl.BlockSpec(memory_space=pltpu.VMEM),
        scratch_shapes=[
            pltpu.VMEM((n,) + chunk, jnp.float32),
            pltpu.SemaphoreType.DMA((n,)),
            pltpu.SemaphoreType.DMA((n,)),
        ],
        compiler_params=pltpu.CompilerParams(collective_id=collective_id, has_side_effects=True),
    )(x)


def pair_scatter_kernel(x_ref, o_ref, pair_buf, pair_sum, held, sems_a, sems_b, sems_c, sems_d):
    n = x_ref.shape[0]
    chips = n // 2
    s = lax.axis_index("site")
    k = lax.axis_index("branch")
    core = s % 2
    chip = s // 2
    partner = s - core + (1 - core)
    barrier = pltpu.get_barrier_semaphore()
    pl.semaphore_signal(barrier, inc=1, device_id=(partner, k), device_id_type=MESH_ID)

    def greet(d, carry):
        peer = 2 * lax.rem(chip + d, chips) + core
        pl.semaphore_signal(barrier, inc=1, device_id=(peer, k), device_id_type=MESH_ID)
        return carry

    lax.fori_loop(1, chips, greet, 0)
    pl.semaphore_wait(barrier, chips)

    def to_partner(m):
        return pltpu.make_async_remote_copy(
            src_ref=x_ref.at[2 * m + 1 - core],
            dst_ref=pair_buf.at[m],
            send_sem=sems_a.at[m],
            recv_sem=sems_b.at[m],
            device_id=(partner, k),
            device_id_type=MESH_ID,
        )

    def first_send(d, carry):
        to_partner(lax.rem(chip + d, chips)).start()
        return carry

    lax.fori_loop(0, chips, first_send, 0)

    def to_chip(c):
        return pltpu.make_async_remote_copy(
            src_ref=pair_sum.at[c],
            dst_ref=held.at[chip],
            send_sem=sems_c.at[c],
            recv_sem=sems_d.at[chip],
            device_id=(2 * c + core, k),
            device_id_type=MESH_ID,
        )

    to_partner(chip).wait_recv()
    pair_sum[chip] = x_ref[2 * chip + core] + pair_buf[chip]
    held[chip] = pair_sum[chip]

    def add_and_send(d, carry):
        c = lax.rem(chip + d, chips)
        to_partner(c).wait_recv()
        pair_sum[c] = x_ref[2 * c + core] + pair_buf[c]
        to_chip(c).start()
        return carry

    lax.fori_loop(1, chips, add_and_send, 0)

    def second_recv(d, carry):
        c = lax.rem(chip + chips - d, chips)
        pltpu.make_async_remote_copy(
            src_ref=held.at[c],
            dst_ref=held.at[c],
            send_sem=sems_c.at[c],
            recv_sem=sems_d.at[c],
            device_id=(2 * c + core, k),
            device_id_type=MESH_ID,
        ).wait_recv()
        return carry

    lax.fori_loop(1, chips, second_recv, 0)

    def first_sent(m, carry):
        to_partner(m).wait_send()
        return carry

    lax.fori_loop(0, chips, first_sent, 0)

    def second_sent(d, carry):
        to_chip(lax.rem(chip + d, chips)).wait_send()
        return carry

    lax.fori_loop(1, chips, second_sent, 0)
    o_ref[...] = lax.fori_loop(1, chips, lambda j, acc: acc + held[j], held[0])


def pair_scatter(x, collective_id):
    n = x.shape[0]
    chunk = x.shape[1:]
    return pl.pallas_call(
        pair_scatter_kernel,
        out_shape=jax.ShapeDtypeStruct(chunk, jnp.float32),
        in_specs=[pl.BlockSpec(memory_space=pltpu.VMEM)],
        out_specs=pl.BlockSpec(memory_space=pltpu.VMEM),
        scratch_shapes=[
            pltpu.VMEM((n // 2,) + chunk, jnp.float32),
            pltpu.VMEM((n // 2,) + chunk, jnp.float32),
            pltpu.VMEM((n // 2,) + chunk, jnp.float32),
            pltpu.SemaphoreType.DMA((n // 2,)),
            pltpu.SemaphoreType.DMA((n // 2,)),
            pltpu.SemaphoreType.DMA((n // 2,)),
            pltpu.SemaphoreType.DMA((n // 2,)),
        ],
        compiler_params=pltpu.CompilerParams(collective_id=collective_id, has_side_effects=True),
    )(x)


def pair_gather_kernel(x_ref, o_ref, held, sems_a, sems_b, sems_c, sems_d):
    n = held.shape[0]
    chips = n // 2
    s = lax.axis_index("site")
    k = lax.axis_index("branch")
    core = s % 2
    chip = s // 2
    partner = s - core + (1 - core)
    barrier = pltpu.get_barrier_semaphore()
    pl.semaphore_signal(barrier, inc=1, device_id=(partner, k), device_id_type=MESH_ID)

    def greet(d, carry):
        peer = 2 * lax.rem(chip + d, chips) + core
        pl.semaphore_signal(barrier, inc=1, device_id=(peer, k), device_id_type=MESH_ID)
        return carry

    lax.fori_loop(1, chips, greet, 0)
    pl.semaphore_wait(barrier, chips)
    held[s] = x_ref[...]

    def to_chip(d):
        c = lax.rem(chip + d, chips)
        return pltpu.make_async_remote_copy(
            src_ref=x_ref,
            dst_ref=held.at[s],
            send_sem=sems_a.at[c],
            recv_sem=sems_b.at[chip],
            device_id=(2 * c + core, k),
            device_id_type=MESH_ID,
        )

    def first_send(d, carry):
        to_chip(d).start()
        return carry

    lax.fori_loop(1, chips, first_send, 0)

    def to_partner(c):
        return pltpu.make_async_remote_copy(
            src_ref=held.at[2 * c + core],
            dst_ref=held.at[2 * c + core],
            send_sem=sems_c.at[c],
            recv_sem=sems_d.at[c],
            device_id=(partner, k),
            device_id_type=MESH_ID,
        )

    own = pltpu.make_async_remote_copy(
        src_ref=x_ref,
        dst_ref=held.at[s],
        send_sem=sems_c.at[chip],
        recv_sem=sems_d.at[chip],
        device_id=(partner, k),
        device_id_type=MESH_ID,
    )
    own.start()

    def relay(d, carry):
        c = lax.rem(chip + chips - d, chips)
        pltpu.make_async_remote_copy(
            src_ref=held.at[2 * c + core],
            dst_ref=held.at[2 * c + core],
            send_sem=sems_a.at[c],
            recv_sem=sems_b.at[c],
            device_id=(2 * c + core, k),
            device_id_type=MESH_ID,
        ).wait_recv()
        to_partner(c).start()
        return carry

    lax.fori_loop(1, chips, relay, 0)

    def second_recv(c, carry):
        pltpu.make_async_remote_copy(
            src_ref=held.at[2 * c + 1 - core],
            dst_ref=held.at[2 * c + 1 - core],
            send_sem=sems_c.at[c],
            recv_sem=sems_d.at[c],
            device_id=(partner, k),
            device_id_type=MESH_ID,
        ).wait_recv()
        return carry

    lax.fori_loop(0, chips, second_recv, 0)

    def first_sent(d, carry):
        to_chip(d).wait_send()
        return carry

    lax.fori_loop(1, chips, first_sent, 0)
    own.wait_send()

    def second_sent(d, carry):
        to_partner(lax.rem(chip + d, chips)).wait_send()
        return carry

    lax.fori_loop(1, chips, second_sent, 0)
    o_ref[...] = held[...]


def pair_gather(x, n, collective_id):
    return pl.pallas_call(
        pair_gather_kernel,
        out_shape=jax.ShapeDtypeStruct((n,) + x.shape, jnp.float32),
        in_specs=[pl.BlockSpec(memory_space=pltpu.VMEM)],
        out_specs=pl.BlockSpec(memory_space=pltpu.VMEM),
        scratch_shapes=[
            pltpu.VMEM((n,) + x.shape, jnp.float32),
            pltpu.SemaphoreType.DMA((n // 2,)),
            pltpu.SemaphoreType.DMA((n // 2,)),
            pltpu.SemaphoreType.DMA((n // 2,)),
            pltpu.SemaphoreType.DMA((n // 2,)),
        ],
        compiler_params=pltpu.CompilerParams(collective_id=collective_id, has_side_effects=True),
    )(x)


def body(
    states, gap_mask, weights, leaf_order, exchanges, codon_freq, omega_ratio, lengths, classes
):
    site_count = lax.axis_size("site")
    site_pos = lax.axis_index("site")
    subtree = lax.axis_index("branch")
    site_span = states.shape[1]
    total_sites = site_span * site_count
    total_taxa = LEAF_DEV * lax.axis_size("branch")
    rate_matrix, stationary = build_rates(exchanges, codon_freq, omega_ratio)
    slot_len = jnp.concatenate([lengths, jnp.zeros((1,), lengths.dtype)])
    slot_cls = jnp.concatenate([classes, jnp.zeros((1,), jnp.int32)])
    class_pick = (slot_cls[:, None] == jnp.arange(CLASSES, dtype=jnp.int32)[None, :]).astype(
        jnp.float32
    )
    slot_rates = jnp.einsum("bc,cij->bij", class_pick, rate_matrix, precision=lax.Precision.HIGH)
    scaled = slot_rates * slot_len[:, None, None]
    per_dev = SLOTS // site_count
    own_start = site_pos * per_dev
    own_scaled = lax.dynamic_slice_in_dim(scaled, own_start, per_dev, 0)
    own_pull = None
    own_probs, own_pull = jax.vjp(expm_taylor, own_scaled)
    dense = pair_gather(own_probs.reshape(-1, 128), site_count, 1)
    probs = dense.reshape((site_count * per_dev,) + own_probs.shape[1:])
    taxon_rows = lax.dynamic_slice_in_dim(leaf_order, subtree * LEAF_DEV, LEAF_DEV, 0)
    leaves = leaf_partials(
        jnp.take(states, taxon_rows, axis=0), jnp.take(gap_mask, taxon_rows, axis=0)
    )
    levels, messages, logscale = up_pass(probs, leaves)
    top_pack = jnp.concatenate([messages[-1][0], logscale[None, :]], axis=0)
    top_all = lax.all_gather(top_pack, "branch", axis=0, tiled=False)
    top_messages, top_logs = top_all[:, :64, :], top_all[:, 64, :]
    site_ll, above_all = root_terms(stationary, top_messages, top_logs)
    site_weight = weights.astype(jnp.float32)
    loglik_part = jnp.sum(site_weight * site_ll)
    above_top = lax.dynamic_slice_in_dim(above_all, subtree, 1, 0)
    a_list = down_pass(probs, levels, messages, above_top)
    weighted = weigh(a_list, messages, site_weight, total_sites)
    padding = jnp.zeros((1, 64, site_span), jnp.float32)
    weighted_all = jnp.concatenate(weighted + [padding], axis=0)
    partial_all = jnp.concatenate(levels + [padding], axis=0)
    part_above = lax.slice_in_dim(weighted_all, 0, lax.axis_size("site") * per_dev, axis=0)
    part_below = lax.slice_in_dim(partial_all, 0, lax.axis_size("site") * per_dev, axis=0)
    part_counts = jnp.einsum("bis,bjs->bij", part_above, part_below, precision=lax.Precision.HIGH)
    own_counts = pair_scatter(part_counts.reshape(site_count, -1, 128), 2).reshape((per_dev, 64, 64))
    d_scaled = own_pull(own_counts)[0]
    use_rates = lax.dynamic_slice_in_dim(slot_rates, own_start, per_dev, 0)
    use_len = lax.dynamic_slice_in_dim(slot_len, own_start, per_dev, 0)
    use_pick = lax.dynamic_slice_in_dim(class_pick, own_start, per_dev, 0)
    d_length = jnp.sum(d_scaled * use_rates, axis=(1, 2))
    d_rates = jnp.einsum(
        "bc,bij->cij", use_pick, d_scaled * use_len[:, None, None], precision=lax.Precision.HIGH
    )
    unused_rates, pull_rates = jax.vjp(
        lambda table, ratio: build_rates(table, codon_freq, ratio)[0], exchanges, omega_ratio
    )
    d_exch, d_omega = pull_rates(d_rates)
    n_branch = lax.axis_size("branch")
    length_slab = jnp.zeros((n_branch, SLOTS), jnp.float32)
    length_slab = lax.dynamic_update_slice(length_slab, d_length[None, :], (subtree, own_start))
    loglik_keep = jnp.where(subtree == 0, loglik_part, jnp.float32(0.0))
    packed = jnp.concatenate(
        [d_exch.reshape(-1), d_omega, length_slab.reshape(-1), loglik_keep[None]]
    )
    rows = -(-packed.shape[0] // (8 * 128)) * 8
    packed = jnp.pad(packed, (0, rows * 128 - packed.shape[0])).reshape(rows, 128)
    summed = allreduce_all(packed, site_count, n_branch).reshape(-1)
    grad_exch = summed[: 64 * 64].reshape(64, 64)
    grad_omega = summed[64 * 64 : 64 * 64 + CLASSES]
    length_all = summed[64 * 64 + CLASSES : 64 * 64 + CLASSES + n_branch * SLOTS].reshape(n_branch, SLOTS)
    log_total = summed[64 * 64 + CLASSES + n_branch * SLOTS]
    loglik = log_total / total_sites / total_taxa
    length_out = lax.dynamic_index_in_dim(length_all, subtree, 0, keepdims=False)[:EDGES]
    return (grad_exch, grad_omega, length_out, loglik)


def solution(mesh):
    return jax.shard_map(
        body,
        mesh=mesh,
        in_specs=(
            P(None, "site"),
            P(None, "site"),
            P("site"),
            P(),
            P(),
            P(),
            P(),
            P("branch"),
            P("branch"),
        ),
        out_specs=(P(), P(), P("branch"), P()),
        check_vma=False,
    )
```

```python
import jax
import jax.numpy as jnp
import numpy as np
from jax import lax
from jax.sharding import PartitionSpec as P
from jax.experimental import pallas as pl
from jax.experimental.pallas import tpu as pltpu
import functools

MESH_ID = pl.DeviceIdType.MESH

LEVELS = 6
LEAF_DEV = 64
EDGES = 127
SLOTS = 128
CLASSES = 8


CODE_TABLE = "FFLLSSSSYYXXCCXWLLLLPPPPHHQQRRRRIIIMTTTTNNKKSSRRVVVVAAAADDEEGGGG"


def codon_tables():
    amino_acid = np.array(list(CODE_TABLE))
    codon_index = np.arange(64)
    digits = np.stack([codon_index // 16, codon_index // 4 % 4, codon_index % 4], 1)
    differ = (digits[:, None, :] != digits[None, :, :]).sum(-1)
    is_sense = amino_acid != "X"
    single = (differ == 1) & is_sense[:, None] & is_sense[None, :]
    nonsyn = single & (amino_acid[:, None] != amino_acid[None, :])
    return (is_sense.astype(np.float32), single.astype(np.float32), nonsyn.astype(np.float32))


def build_rates(exchanges, codon_freq, omega_ratio):
    is_sense, single, nonsyn = codon_tables()
    stationary = codon_freq * is_sense / jnp.sum(codon_freq * is_sense)
    symmetric = 0.5 * (exchanges + exchanges.T)
    factor = 1.0 + nonsyn[None, :, :] * (omega_ratio[:, None, None] - 1.0)
    off_diag = symmetric[None, :, :] * stationary[None, None, :] * factor * single[None, :, :]
    row_total = jnp.sum(off_diag, axis=2)
    mean_rate = jnp.sum(stationary[None, :] * row_total, axis=1)
    identity = jnp.eye(64, dtype=exchanges.dtype)
    rate_matrix = (off_diag - row_total[:, :, None] * identity[None]) / mean_rate[:, None, None]
    return (rate_matrix, stationary)


def product(left, right):
    return jnp.einsum("bij,bjk->bik", left, right, precision=lax.Precision.HIGH)


def expm_taylor(scaled):
    reduced = scaled / 16.0
    identity = jnp.eye(64, dtype=scaled.dtype)
    series = jnp.broadcast_to(identity, scaled.shape)
    for degree in range(8, 0, -1):
        series = identity + product(reduced, series) / degree
    for square_step in range(4):
        series = product(series, series)
    return series


def forward(probs, vectors):
    return jnp.einsum("bij,bjs->bis", probs, vectors, precision=lax.Precision.HIGH)


def carried(probs, vectors):
    return jnp.einsum("bji,bjs->bis", probs, vectors, precision=lax.Precision.HIGH)


def leaf_partials(leaf_states, gap_rows):
    codon_axis = jnp.arange(64, dtype=jnp.int32)
    indicator = (leaf_states[:, None, :] == codon_axis[None, :, None]).astype(jnp.float32)
    return jnp.where(gap_rows[:, None, :] > 0, jnp.float32(1.0), indicator)


def up_pass(probs, leaves):
    levels = [leaves]
    messages = []
    logscale = jnp.zeros(leaves.shape[2:], jnp.float32)
    current = leaves
    for height in range(LEVELS):
        amount = current.shape[0]
        offset = 2 * LEAF_DEV - 2 * amount
        message = forward(probs[offset : offset + amount], current)
        messages.append(message)
        raw_parent = message[0::2] * message[1::2]
        scaling = jnp.sum(raw_parent, axis=1)
        current = raw_parent / scaling[:, None, :]
        logscale = logscale + jnp.sum(jnp.log(scaling), axis=0)
        levels.append(current)
    messages.append(forward(probs[EDGES - 1 : EDGES], current))
    return (levels, messages, logscale)


def root_terms(stationary, top_messages, top_logs):
    members = top_messages.shape[0]
    joint = stationary[:, None] * top_messages[0]
    for member in range(1, members):
        joint = joint * top_messages[member]
    site_ll = jnp.log(jnp.sum(joint, axis=0)) + jnp.sum(top_logs, axis=0)
    above_list = []
    for member in range(members):
        vector = jnp.broadcast_to(stationary[:, None], top_messages.shape[1:])
        for other in range(members):
            if other != member:
                vector = vector * top_messages[other]
        above_list.append(vector)
    return (site_ll, jnp.stack(above_list))


def down_pass(probs, levels, messages, above_top):
    a_list = [above_top]
    current = above_top
    for height in range(LEVELS, 0, -1):
        amount = levels[height].shape[0]
        offset = 2 * LEAF_DEV - 2 * amount
        down_part = carried(probs[offset : offset + amount], current)
        down_part = down_part / jnp.sum(down_part, axis=1, keepdims=True)
        message = messages[height - 1]
        current = jnp.stack([down_part * message[1::2], down_part * message[0::2]], axis=1).reshape(
            message.shape
        )
        a_list.append(current)
    return a_list[::-1]


def weigh(a_list, messages, site_weight, total_sites):
    weighted = []
    for vector, message in zip(a_list, messages):
        likelihood = jnp.sum(vector * message, axis=1)
        weighted.append(vector * (site_weight / (likelihood * total_sites))[:, None, :])
    return weighted


def sum_groups(n_site, n_branch):
    s = lax.axis_index("site")
    k = lax.axis_index("branch")
    core = s % 2
    plane = s // 2
    return [
        (2 * n_branch, 2 * k + core, lambda c: (s - core + c % 2, c // 2)),
        (n_site // 2, plane, lambda c: (2 * c + core, k)),
    ]


def allreduce_kernel(n_site, n_branch, x_ref, o_ref, held, send_sems, recv_sems):
    stages = sum_groups(n_site, n_branch)
    barrier = pltpu.get_barrier_semaphore()
    count = 0
    for size, mine, where in stages:
        for d in range(1, size):
            other = lax.rem(mine + d, size)
            pl.semaphore_signal(barrier, inc=1, device_id=where(other), device_id_type=MESH_ID)
            count += 1
    pl.semaphore_wait(barrier, count)
    total = x_ref[...]
    for st, (size, mine, where) in enumerate(stages):
        held[st, mine] = total
        sends = []
        for d in range(1, size):
            other = lax.rem(mine + d, size)
            copy = pltpu.make_async_remote_copy(
                src_ref=held.at[st, mine],
                dst_ref=held.at[st, mine],
                send_sem=send_sems.at[st, other],
                recv_sem=recv_sems.at[st, mine],
                device_id=where(other),
                device_id_type=MESH_ID,
            )
            copy.start()
            sends.append(copy)
        for d in range(1, size):
            other = lax.rem(mine + d, size)
            incoming = pltpu.make_async_remote_copy(
                src_ref=held.at[st, other],
                dst_ref=held.at[st, other],
                send_sem=send_sems.at[st, other],
                recv_sem=recv_sems.at[st, other],
                device_id=where(other),
                device_id_type=MESH_ID,
            )
            incoming.wait_recv()
        for copy in sends:
            copy.wait_send()
        total = held[st, 0]
        for c in range(1, size):
            total = total + held[st, c]
    o_ref[...] = total


def allreduce_all(x, n_site, n_branch):
    rows = x.shape[0]
    return pl.pallas_call(
        functools.partial(allreduce_kernel, n_site, n_branch),
        out_shape=jax.ShapeDtypeStruct(x.shape, jnp.float32),
        in_specs=[pl.BlockSpec(memory_space=pltpu.VMEM)],
        out_specs=pl.BlockSpec(memory_space=pltpu.VMEM),
        scratch_shapes=[
            pltpu.VMEM((2, n_site // 2, rows, 128), jnp.float32),
            pltpu.SemaphoreType.DMA((2, n_site // 2)),
            pltpu.SemaphoreType.DMA((2, n_site // 2)),
        ],
        compiler_params=pltpu.CompilerParams(collective_id=0, has_side_effects=True),
    )(x)


def exchange_kernel(axis, gather, x_ref, o_ref, held, send_sems, recv_sems):
    n = held.shape[0]
    me = lax.axis_index(axis)
    other_axis = "branch" if axis == "site" else "site"
    fixed = lax.axis_index(other_axis)

    def device(p):
        return (p, fixed) if axis == "site" else (fixed, p)

    barrier = pltpu.get_barrier_semaphore()

    def greet(d, carry):
        pl.semaphore_signal(
            barrier, inc=1, device_id=device(lax.rem(me + d, n)), device_id_type=MESH_ID
        )
        return carry

    lax.fori_loop(1, n, greet, 0)
    pl.semaphore_wait(barrier, n - 1)
    if gather:
        held[me] = x_ref[...]
    else:
        held[me] = x_ref[me]

    def outgoing(d):
        p = lax.rem(me + d, n)
        return pltpu.make_async_remote_copy(
            src_ref=x_ref if gather else x_ref.at[p],
            dst_ref=held.at[me],
            send_sem=send_sems.at[p],
            recv_sem=recv_sems.at[me],
            device_id=device(p),
            device_id_type=MESH_ID,
        )

    def send(d, carry):
        outgoing(d).start()
        return carry

    lax.fori_loop(1, n, send, 0)

    def receive(d, carry):
        p = lax.rem(me + n - d, n)
        pltpu.make_async_remote_copy(
            src_ref=held.at[p],
            dst_ref=held.at[p],
            send_sem=send_sems.at[p],
            recv_sem=recv_sems.at[p],
            device_id=device(p),
            device_id_type=MESH_ID,
        ).wait_recv()
        return carry

    lax.fori_loop(1, n, receive, 0)

    def sent(d, carry):
        outgoing(d).wait_send()
        return carry

    lax.fori_loop(1, n, sent, 0)
    if gather:
        o_ref[...] = held[...]
    else:
        o_ref[...] = lax.fori_loop(1, n, lambda j, acc: acc + held[j], held[0])


def exchange(x, axis, n, gather, collective_id):
    chunk = x.shape if gather else x.shape[1:]
    out_shape = (n,) + chunk if gather else chunk
    return pl.pallas_call(
        functools.partial(exchange_kernel, axis, gather),
        out_shape=jax.ShapeDtypeStruct(out_shape, jnp.float32),
        in_specs=[pl.BlockSpec(memory_space=pltpu.VMEM)],
        out_specs=pl.BlockSpec(memory_space=pltpu.VMEM),
        scratch_shapes=[
            pltpu.VMEM((n,) + chunk, jnp.float32),
            pltpu.SemaphoreType.DMA((n,)),
            pltpu.SemaphoreType.DMA((n,)),
        ],
        compiler_params=pltpu.CompilerParams(collective_id=collective_id, has_side_effects=True),
    )(x)


def pair_scatter_kernel(x_ref, o_ref, pair_buf, pair_sum, held, sems_a, sems_b, sems_c, sems_d):
    n = x_ref.shape[0]
    chips = n // 2
    s = lax.axis_index("site")
    k = lax.axis_index("branch")
    core = s % 2
    chip = s // 2
    partner = s - core + (1 - core)
    barrier = pltpu.get_barrier_semaphore()
    pl.semaphore_signal(barrier, inc=1, device_id=(partner, k), device_id_type=MESH_ID)

    def greet(d, carry):
        peer = 2 * lax.rem(chip + d, chips) + core
        pl.semaphore_signal(barrier, inc=1, device_id=(peer, k), device_id_type=MESH_ID)
        return carry

    lax.fori_loop(1, chips, greet, 0)
    pl.semaphore_wait(barrier, chips)

    def to_partner(m):
        return pltpu.make_async_remote_copy(
            src_ref=x_ref.at[2 * m + 1 - core],
            dst_ref=pair_buf.at[m],
            send_sem=sems_a.at[m],
            recv_sem=sems_b.at[m],
            device_id=(partner, k),
            device_id_type=MESH_ID,
        )

    def first_send(m, carry):
        to_partner(m).start()
        return carry

    lax.fori_loop(0, chips, first_send, 0)

    def to_chip(c):
        return pltpu.make_async_remote_copy(
            src_ref=pair_sum.at[c],
            dst_ref=held.at[chip],
            send_sem=sems_c.at[c],
            recv_sem=sems_d.at[chip],
            device_id=(2 * c + core, k),
            device_id_type=MESH_ID,
        )

    to_partner(chip).wait_recv()
    pair_sum[chip] = x_ref[2 * chip + core] + pair_buf[chip]
    held[chip] = pair_sum[chip]

    def add_and_send(d, carry):
        c = lax.rem(chip + d, chips)
        to_partner(c).wait_recv()
        pair_sum[c] = x_ref[2 * c + core] + pair_buf[c]
        to_chip(c).start()
        return carry

    lax.fori_loop(1, chips, add_and_send, 0)

    def second_recv(d, carry):
        c = lax.rem(chip + chips - d, chips)
        pltpu.make_async_remote_copy(
            src_ref=held.at[c],
            dst_ref=held.at[c],
            send_sem=sems_c.at[c],
            recv_sem=sems_d.at[c],
            device_id=(2 * c + core, k),
            device_id_type=MESH_ID,
        ).wait_recv()
        return carry

    lax.fori_loop(1, chips, second_recv, 0)

    def first_sent(m, carry):
        to_partner(m).wait_send()
        return carry

    lax.fori_loop(0, chips, first_sent, 0)

    def second_sent(d, carry):
        to_chip(lax.rem(chip + d, chips)).wait_send()
        return carry

    lax.fori_loop(1, chips, second_sent, 0)
    o_ref[...] = lax.fori_loop(1, chips, lambda j, acc: acc + held[j], held[0])


def pair_scatter(x, collective_id):
    n = x.shape[0]
    chunk = x.shape[1:]
    return pl.pallas_call(
        pair_scatter_kernel,
        out_shape=jax.ShapeDtypeStruct(chunk, jnp.float32),
        in_specs=[pl.BlockSpec(memory_space=pltpu.VMEM)],
        out_specs=pl.BlockSpec(memory_space=pltpu.VMEM),
        scratch_shapes=[
            pltpu.VMEM((n // 2,) + chunk, jnp.float32),
            pltpu.VMEM((n // 2,) + chunk, jnp.float32),
            pltpu.VMEM((n // 2,) + chunk, jnp.float32),
            pltpu.SemaphoreType.DMA((n // 2,)),
            pltpu.SemaphoreType.DMA((n // 2,)),
            pltpu.SemaphoreType.DMA((n // 2,)),
            pltpu.SemaphoreType.DMA((n // 2,)),
        ],
        compiler_params=pltpu.CompilerParams(collective_id=collective_id, has_side_effects=True),
    )(x)


def pair_gather_kernel(x_ref, o_ref, held, sems_a, sems_b, sems_c, sems_d):
    n = held.shape[0]
    chips = n // 2
    s = lax.axis_index("site")
    k = lax.axis_index("branch")
    core = s % 2
    chip = s // 2
    partner = s - core + (1 - core)
    barrier = pltpu.get_barrier_semaphore()
    pl.semaphore_signal(barrier, inc=1, device_id=(partner, k), device_id_type=MESH_ID)

    def greet(d, carry):
        peer = 2 * lax.rem(chip + d, chips) + core
        pl.semaphore_signal(barrier, inc=1, device_id=(peer, k), device_id_type=MESH_ID)
        return carry

    lax.fori_loop(1, chips, greet, 0)
    pl.semaphore_wait(barrier, chips)
    held[s] = x_ref[...]

    def to_chip(d):
        c = lax.rem(chip + d, chips)
        return pltpu.make_async_remote_copy(
            src_ref=x_ref,
            dst_ref=held.at[s],
            send_sem=sems_a.at[c],
            recv_sem=sems_b.at[chip],
            device_id=(2 * c + core, k),
            device_id_type=MESH_ID,
        )

    def first_send(d, carry):
        to_chip(d).start()
        return carry

    lax.fori_loop(1, chips, first_send, 0)

    def to_partner(c):
        return pltpu.make_async_remote_copy(
            src_ref=held.at[2 * c + core],
            dst_ref=held.at[2 * c + core],
            send_sem=sems_c.at[c],
            recv_sem=sems_d.at[c],
            device_id=(partner, k),
            device_id_type=MESH_ID,
        )

    own = pltpu.make_async_remote_copy(
        src_ref=x_ref,
        dst_ref=held.at[s],
        send_sem=sems_c.at[chip],
        recv_sem=sems_d.at[chip],
        device_id=(partner, k),
        device_id_type=MESH_ID,
    )
    own.start()

    def relay(d, carry):
        c = lax.rem(chip + chips - d, chips)
        pltpu.make_async_remote_copy(
            src_ref=held.at[2 * c + core],
            dst_ref=held.at[2 * c + core],
            send_sem=sems_a.at[c],
            recv_sem=sems_b.at[c],
            device_id=(2 * c + core, k),
            device_id_type=MESH_ID,
        ).wait_recv()
        to_partner(c).start()
        return carry

    lax.fori_loop(1, chips, relay, 0)

    def second_recv(c, carry):
        pltpu.make_async_remote_copy(
            src_ref=held.at[2 * c + 1 - core],
            dst_ref=held.at[2 * c + 1 - core],
            send_sem=sems_c.at[c],
            recv_sem=sems_d.at[c],
            device_id=(partner, k),
            device_id_type=MESH_ID,
        ).wait_recv()
        return carry

    lax.fori_loop(0, chips, second_recv, 0)

    def first_sent(d, carry):
        to_chip(d).wait_send()
        return carry

    lax.fori_loop(1, chips, first_sent, 0)
    own.wait_send()

    def second_sent(d, carry):
        to_partner(lax.rem(chip + d, chips)).wait_send()
        return carry

    lax.fori_loop(1, chips, second_sent, 0)
    o_ref[...] = held[...]


def pair_gather(x, n, collective_id):
    return pl.pallas_call(
        pair_gather_kernel,
        out_shape=jax.ShapeDtypeStruct((n,) + x.shape, jnp.float32),
        in_specs=[pl.BlockSpec(memory_space=pltpu.VMEM)],
        out_specs=pl.BlockSpec(memory_space=pltpu.VMEM),
        scratch_shapes=[
            pltpu.VMEM((n,) + x.shape, jnp.float32),
            pltpu.SemaphoreType.DMA((n // 2,)),
            pltpu.SemaphoreType.DMA((n // 2,)),
            pltpu.SemaphoreType.DMA((n // 2,)),
            pltpu.SemaphoreType.DMA((n // 2,)),
        ],
        compiler_params=pltpu.CompilerParams(collective_id=collective_id, has_side_effects=True),
    )(x)


def body(
    states, gap_mask, weights, leaf_order, exchanges, codon_freq, omega_ratio, lengths, classes
):
    site_count = lax.axis_size("site")
    site_pos = lax.axis_index("site")
    subtree = lax.axis_index("branch")
    site_span = states.shape[1]
    total_sites = site_span * site_count
    total_taxa = LEAF_DEV * lax.axis_size("branch")
    rate_matrix, stationary = build_rates(exchanges, codon_freq, omega_ratio)
    slot_len = jnp.concatenate([lengths, jnp.zeros((1,), lengths.dtype)])
    slot_cls = jnp.concatenate([classes, jnp.zeros((1,), jnp.int32)])
    class_pick = (slot_cls[:, None] == jnp.arange(CLASSES, dtype=jnp.int32)[None, :]).astype(
        jnp.float32
    )
    slot_rates = jnp.einsum("bc,cij->bij", class_pick, rate_matrix, precision=lax.Precision.HIGH)
    scaled = slot_rates * slot_len[:, None, None]
    per_dev = SLOTS // site_count
    own_start = site_pos * per_dev
    own_scaled = lax.dynamic_slice_in_dim(scaled, own_start, per_dev, 0)
    own_pull = None
    own_probs, own_pull = jax.vjp(expm_taylor, own_scaled)
    dense = pair_gather(own_probs.reshape(-1, 128), site_count, 1)
    probs = dense.reshape((site_count * per_dev,) + own_probs.shape[1:])
    taxon_rows = lax.dynamic_slice_in_dim(leaf_order, subtree * LEAF_DEV, LEAF_DEV, 0)
    leaves = leaf_partials(
        jnp.take(states, taxon_rows, axis=0), jnp.take(gap_mask, taxon_rows, axis=0)
    )
    levels, messages, logscale = up_pass(probs, leaves)
    top_pack = jnp.concatenate([messages[-1][0], logscale[None, :]], axis=0)
    top_all = lax.all_gather(top_pack, "branch", axis=0, tiled=False)
    top_messages, top_logs = top_all[:, :64, :], top_all[:, 64, :]
    site_ll, above_all = root_terms(stationary, top_messages, top_logs)
    site_weight = weights.astype(jnp.float32)
    loglik_part = jnp.sum(site_weight * site_ll)
    above_top = lax.dynamic_slice_in_dim(above_all, subtree, 1, 0)
    a_list = down_pass(probs, levels, messages, above_top)
    weighted = weigh(a_list, messages, site_weight, total_sites)
    padding = jnp.zeros((1, 64, site_span), jnp.float32)
    weighted_all = jnp.concatenate(weighted + [padding], axis=0)
    partial_all = jnp.concatenate(levels + [padding], axis=0)
    part_above = lax.slice_in_dim(weighted_all, 0, lax.axis_size("site") * per_dev, axis=0)
    part_below = lax.slice_in_dim(partial_all, 0, lax.axis_size("site") * per_dev, axis=0)
    part_counts = jnp.einsum("bis,bjs->bij", part_above, part_below, precision=lax.Precision.HIGH)
    own_counts = pair_scatter(part_counts.reshape(site_count, -1, 128), 2).reshape((per_dev, 64, 64))
    d_scaled = own_pull(own_counts)[0]
    use_rates = lax.dynamic_slice_in_dim(slot_rates, own_start, per_dev, 0)
    use_len = lax.dynamic_slice_in_dim(slot_len, own_start, per_dev, 0)
    use_pick = lax.dynamic_slice_in_dim(class_pick, own_start, per_dev, 0)
    d_length = jnp.sum(d_scaled * use_rates, axis=(1, 2))
    d_rates = jnp.einsum(
        "bc,bij->cij", use_pick, d_scaled * use_len[:, None, None], precision=lax.Precision.HIGH
    )
    unused_rates, pull_rates = jax.vjp(
        lambda table, ratio: build_rates(table, codon_freq, ratio)[0], exchanges, omega_ratio
    )
    d_exch, d_omega = pull_rates(d_rates)
    n_branch = lax.axis_size("branch")
    length_slab = jnp.zeros((n_branch, SLOTS), jnp.float32)
    length_slab = lax.dynamic_update_slice(length_slab, d_length[None, :], (subtree, own_start))
    loglik_keep = jnp.where(subtree == 0, loglik_part, jnp.float32(0.0))
    packed = jnp.concatenate(
        [d_exch.reshape(-1), d_omega, length_slab.reshape(-1), loglik_keep[None]]
    )
    rows = -(-packed.shape[0] // (8 * 128)) * 8
    packed = jnp.pad(packed, (0, rows * 128 - packed.shape[0])).reshape(rows, 128)
    summed = allreduce_all(packed, site_count, n_branch).reshape(-1)
    grad_exch = summed[: 64 * 64].reshape(64, 64)
    grad_omega = summed[64 * 64 : 64 * 64 + CLASSES]
    length_all = summed[64 * 64 + CLASSES : 64 * 64 + CLASSES + n_branch * SLOTS].reshape(n_branch, SLOTS)
    log_total = summed[64 * 64 + CLASSES + n_branch * SLOTS]
    loglik = log_total / total_sites / total_taxa
    length_out = lax.dynamic_index_in_dim(length_all, subtree, 0, keepdims=False)[:EDGES]
    return (grad_exch, grad_omega, length_out, loglik)


def solution(mesh):
    return jax.shard_map(
        body,
        mesh=mesh,
        in_specs=(
            P(None, "site"),
            P(None, "site"),
            P("site"),
            P(),
            P(),
            P(),
            P(),
            P("branch"),
            P("branch"),
        ),
        out_specs=(P(), P(), P("branch"), P()),
        check_vma=False,
    )
```

```python
import jax
import jax.numpy as jnp
import numpy as np
from jax import lax
from jax.sharding import PartitionSpec as P
from jax.experimental import pallas as pl
from jax.experimental.pallas import tpu as pltpu
import functools

MESH_ID = pl.DeviceIdType.MESH

LEVELS = 6
LEAF_DEV = 64
EDGES = 127
SLOTS = 128
CLASSES = 8


CODE_TABLE = "FFLLSSSSYYXXCCXWLLLLPPPPHHQQRRRRIIIMTTTTNNKKSSRRVVVVAAAADDEEGGGG"


def codon_tables():
    amino_acid = np.array(list(CODE_TABLE))
    codon_index = np.arange(64)
    digits = np.stack([codon_index // 16, codon_index // 4 % 4, codon_index % 4], 1)
    differ = (digits[:, None, :] != digits[None, :, :]).sum(-1)
    is_sense = amino_acid != "X"
    single = (differ == 1) & is_sense[:, None] & is_sense[None, :]
    nonsyn = single & (amino_acid[:, None] != amino_acid[None, :])
    return (is_sense.astype(np.float32), single.astype(np.float32), nonsyn.astype(np.float32))


def build_rates(exchanges, codon_freq, omega_ratio):
    is_sense, single, nonsyn = codon_tables()
    stationary = codon_freq * is_sense / jnp.sum(codon_freq * is_sense)
    symmetric = 0.5 * (exchanges + exchanges.T)
    factor = 1.0 + nonsyn[None, :, :] * (omega_ratio[:, None, None] - 1.0)
    off_diag = symmetric[None, :, :] * stationary[None, None, :] * factor * single[None, :, :]
    row_total = jnp.sum(off_diag, axis=2)
    mean_rate = jnp.sum(stationary[None, :] * row_total, axis=1)
    identity = jnp.eye(64, dtype=exchanges.dtype)
    rate_matrix = (off_diag - row_total[:, :, None] * identity[None]) / mean_rate[:, None, None]
    return (rate_matrix, stationary)


def product(left, right):
    return jnp.einsum("bij,bjk->bik", left, right, precision=lax.Precision.HIGH)


def expm_taylor(scaled):
    reduced = scaled / 16.0
    identity = jnp.eye(64, dtype=scaled.dtype)
    series = jnp.broadcast_to(identity, scaled.shape)
    for degree in range(8, 0, -1):
        series = identity + product(reduced, series) / degree
    for square_step in range(4):
        series = product(series, series)
    return series


def forward(probs, vectors):
    return jnp.einsum("bij,bjs->bis", probs, vectors, precision=lax.Precision.HIGH)


def carried(probs, vectors):
    return jnp.einsum("bji,bjs->bis", probs, vectors, precision=lax.Precision.HIGH)


def leaf_partials(leaf_states, gap_rows):
    codon_axis = jnp.arange(64, dtype=jnp.int32)
    indicator = (leaf_states[:, None, :] == codon_axis[None, :, None]).astype(jnp.float32)
    return jnp.where(gap_rows[:, None, :] > 0, jnp.float32(1.0), indicator)


def up_pass(probs, leaves):
    levels = [leaves]
    messages = []
    logscale = jnp.zeros(leaves.shape[2:], jnp.float32)
    current = leaves
    for height in range(LEVELS):
        amount = current.shape[0]
        offset = 2 * LEAF_DEV - 2 * amount
        message = forward(probs[offset : offset + amount], current)
        messages.append(message)
        raw_parent = message[0::2] * message[1::2]
        scaling = jnp.sum(raw_parent, axis=1)
        current = raw_parent / scaling[:, None, :]
        logscale = logscale + jnp.sum(jnp.log(scaling), axis=0)
        levels.append(current)
    messages.append(forward(probs[EDGES - 1 : EDGES], current))
    return (levels, messages, logscale)


def root_terms(stationary, top_messages, top_logs):
    members = top_messages.shape[0]
    joint = stationary[:, None] * top_messages[0]
    for member in range(1, members):
        joint = joint * top_messages[member]
    site_ll = jnp.log(jnp.sum(joint, axis=0)) + jnp.sum(top_logs, axis=0)
    above_list = []
    for member in range(members):
        vector = jnp.broadcast_to(stationary[:, None], top_messages.shape[1:])
        for other in range(members):
            if other != member:
                vector = vector * top_messages[other]
        above_list.append(vector)
    return (site_ll, jnp.stack(above_list))


def down_pass(probs, levels, messages, above_top):
    a_list = [above_top]
    current = above_top
    for height in range(LEVELS, 0, -1):
        amount = levels[height].shape[0]
        offset = 2 * LEAF_DEV - 2 * amount
        down_part = carried(probs[offset : offset + amount], current)
        down_part = down_part / jnp.sum(down_part, axis=1, keepdims=True)
        message = messages[height - 1]
        current = jnp.stack([down_part * message[1::2], down_part * message[0::2]], axis=1).reshape(
            message.shape
        )
        a_list.append(current)
    return a_list[::-1]


def weigh(a_list, messages, site_weight, total_sites):
    weighted = []
    for vector, message in zip(a_list, messages):
        likelihood = jnp.sum(vector * message, axis=1)
        weighted.append(vector * (site_weight / (likelihood * total_sites))[:, None, :])
    return weighted


def sum_groups(n_site, n_branch):
    s = lax.axis_index("site")
    k = lax.axis_index("branch")
    core = s % 2
    plane = s // 2
    return [
        (2, core, lambda c: (s - core + c, k)),
        (n_branch, k, lambda c: (s, c)),
        (n_site // 2, plane, lambda c: (2 * c + core, k)),
    ]


def allreduce_kernel(n_site, n_branch, x_ref, o_ref, held, send_sems, recv_sems):
    stages = sum_groups(n_site, n_branch)
    barrier = pltpu.get_barrier_semaphore()
    count = 0
    for size, mine, where in stages:
        for d in range(1, size):
            other = lax.rem(mine + d, size)
            pl.semaphore_signal(barrier, inc=1, device_id=where(other), device_id_type=MESH_ID)
            count += 1
    pl.semaphore_wait(barrier, count)
    total = x_ref[...]
    for st, (size, mine, where) in enumerate(stages):
        held[st, mine] = total
        sends = []
        for d in range(1, size):
            other = lax.rem(mine + d, size)
            copy = pltpu.make_async_remote_copy(
                src_ref=held.at[st, mine],
                dst_ref=held.at[st, mine],
                send_sem=send_sems.at[st, other],
                recv_sem=recv_sems.at[st, mine],
                device_id=where(other),
                device_id_type=MESH_ID,
            )
            copy.start()
            sends.append(copy)
        for d in range(1, size):
            other = lax.rem(mine + d, size)
            incoming = pltpu.make_async_remote_copy(
                src_ref=held.at[st, other],
                dst_ref=held.at[st, other],
                send_sem=send_sems.at[st, other],
                recv_sem=recv_sems.at[st, other],
                device_id=where(other),
                device_id_type=MESH_ID,
            )
            incoming.wait_recv()
        for copy in sends:
            copy.wait_send()
        total = held[st, 0]
        for c in range(1, size):
            total = total + held[st, c]
    o_ref[...] = total


def allreduce_all(x, n_site, n_branch):
    rows = x.shape[0]
    return pl.pallas_call(
        functools.partial(allreduce_kernel, n_site, n_branch),
        out_shape=jax.ShapeDtypeStruct(x.shape, jnp.float32),
        in_specs=[pl.BlockSpec(memory_space=pltpu.VMEM)],
        out_specs=pl.BlockSpec(memory_space=pltpu.VMEM),
        scratch_shapes=[
            pltpu.VMEM((3, n_site // 2, rows, 128), jnp.float32),
            pltpu.SemaphoreType.DMA((3, n_site // 2)),
            pltpu.SemaphoreType.DMA((3, n_site // 2)),
        ],
        compiler_params=pltpu.CompilerParams(collective_id=0, has_side_effects=True),
    )(x)


def exchange_kernel(axis, gather, x_ref, o_ref, held, send_sems, recv_sems):
    n = held.shape[0]
    me = lax.axis_index(axis)
    other_axis = "branch" if axis == "site" else "site"
    fixed = lax.axis_index(other_axis)

    def device(p):
        return (p, fixed) if axis == "site" else (fixed, p)

    barrier = pltpu.get_barrier_semaphore()

    def greet(d, carry):
        pl.semaphore_signal(
            barrier, inc=1, device_id=device(lax.rem(me + d, n)), device_id_type=MESH_ID
        )
        return carry

    lax.fori_loop(1, n, greet, 0)
    pl.semaphore_wait(barrier, n - 1)
    if gather:
        held[me] = x_ref[...]
    else:
        held[me] = x_ref[me]

    def outgoing(d):
        p = lax.rem(me + d, n)
        return pltpu.make_async_remote_copy(
            src_ref=x_ref if gather else x_ref.at[p],
            dst_ref=held.at[me],
            send_sem=send_sems.at[p],
            recv_sem=recv_sems.at[me],
            device_id=device(p),
            device_id_type=MESH_ID,
        )

    def send(d, carry):
        outgoing(d).start()
        return carry

    lax.fori_loop(1, n, send, 0)

    def receive(d, carry):
        p = lax.rem(me + n - d, n)
        pltpu.make_async_remote_copy(
            src_ref=held.at[p],
            dst_ref=held.at[p],
            send_sem=send_sems.at[p],
            recv_sem=recv_sems.at[p],
            device_id=device(p),
            device_id_type=MESH_ID,
        ).wait_recv()
        return carry

    lax.fori_loop(1, n, receive, 0)

    def sent(d, carry):
        outgoing(d).wait_send()
        return carry

    lax.fori_loop(1, n, sent, 0)
    if gather:
        o_ref[...] = held[...]
    else:
        o_ref[...] = lax.fori_loop(1, n, lambda j, acc: acc + held[j], held[0])


def exchange(x, axis, n, gather, collective_id):
    chunk = x.shape if gather else x.shape[1:]
    out_shape = (n,) + chunk if gather else chunk
    return pl.pallas_call(
        functools.partial(exchange_kernel, axis, gather),
        out_shape=jax.ShapeDtypeStruct(out_shape, jnp.float32),
        in_specs=[pl.BlockSpec(memory_space=pltpu.VMEM)],
        out_specs=pl.BlockSpec(memory_space=pltpu.VMEM),
        scratch_shapes=[
            pltpu.VMEM((n,) + chunk, jnp.float32),
            pltpu.SemaphoreType.DMA((n,)),
            pltpu.SemaphoreType.DMA((n,)),
        ],
        compiler_params=pltpu.CompilerParams(collective_id=collective_id, has_side_effects=True),
    )(x)


def pair_scatter_kernel(x_ref, o_ref, pair_buf, pair_sum, held, sems_a, sems_b, sems_c, sems_d):
    n = x_ref.shape[0]
    chips = n // 2
    s = lax.axis_index("site")
    k = lax.axis_index("branch")
    core = s % 2
    chip = s // 2
    partner = s - core + (1 - core)
    barrier = pltpu.get_barrier_semaphore()
    pl.semaphore_signal(barrier, inc=1, device_id=(partner, k), device_id_type=MESH_ID)

    def greet(d, carry):
        peer = 2 * lax.rem(chip + d, chips) + core
        pl.semaphore_signal(barrier, inc=1, device_id=(peer, k), device_id_type=MESH_ID)
        return carry

    lax.fori_loop(1, chips, greet, 0)
    pl.semaphore_wait(barrier, chips)

    def to_partner(m):
        return pltpu.make_async_remote_copy(
            src_ref=x_ref.at[2 * m + 1 - core],
            dst_ref=pair_buf.at[m],
            send_sem=sems_a.at[m],
            recv_sem=sems_b.at[m],
            device_id=(partner, k),
            device_id_type=MESH_ID,
        )

    def first_send(m, carry):
        to_partner(m).start()
        return carry

    lax.fori_loop(0, chips, first_send, 0)

    def to_chip(c):
        return pltpu.make_async_remote_copy(
            src_ref=pair_sum.at[c],
            dst_ref=held.at[chip],
            send_sem=sems_c.at[c],
            recv_sem=sems_d.at[chip],
            device_id=(2 * c + core, k),
            device_id_type=MESH_ID,
        )

    to_partner(chip).wait_recv()
    pair_sum[chip] = x_ref[2 * chip + core] + pair_buf[chip]
    held[chip] = pair_sum[chip]

    def add_and_send(d, carry):
        c = lax.rem(chip + d, chips)
        to_partner(c).wait_recv()
        pair_sum[c] = x_ref[2 * c + core] + pair_buf[c]
        to_chip(c).start()
        return carry

    lax.fori_loop(1, chips, add_and_send, 0)

    def second_recv(d, carry):
        c = lax.rem(chip + chips - d, chips)
        pltpu.make_async_remote_copy(
            src_ref=held.at[c],
            dst_ref=held.at[c],
            send_sem=sems_c.at[c],
            recv_sem=sems_d.at[c],
            device_id=(2 * c + core, k),
            device_id_type=MESH_ID,
        ).wait_recv()
        return carry

    lax.fori_loop(1, chips, second_recv, 0)

    def first_sent(m, carry):
        to_partner(m).wait_send()
        return carry

    lax.fori_loop(0, chips, first_sent, 0)

    def second_sent(d, carry):
        to_chip(lax.rem(chip + d, chips)).wait_send()
        return carry

    lax.fori_loop(1, chips, second_sent, 0)
    o_ref[...] = lax.fori_loop(1, chips, lambda j, acc: acc + held[j], held[0])


def pair_scatter(x, collective_id):
    n = x.shape[0]
    chunk = x.shape[1:]
    return pl.pallas_call(
        pair_scatter_kernel,
        out_shape=jax.ShapeDtypeStruct(chunk, jnp.float32),
        in_specs=[pl.BlockSpec(memory_space=pltpu.VMEM)],
        out_specs=pl.BlockSpec(memory_space=pltpu.VMEM),
        scratch_shapes=[
            pltpu.VMEM((n // 2,) + chunk, jnp.float32),
            pltpu.VMEM((n // 2,) + chunk, jnp.float32),
            pltpu.VMEM((n // 2,) + chunk, jnp.float32),
            pltpu.SemaphoreType.DMA((n // 2,)),
            pltpu.SemaphoreType.DMA((n // 2,)),
            pltpu.SemaphoreType.DMA((n // 2,)),
            pltpu.SemaphoreType.DMA((n // 2,)),
        ],
        compiler_params=pltpu.CompilerParams(collective_id=collective_id, has_side_effects=True),
    )(x)


def pair_gather_kernel(x_ref, o_ref, held, sems_a, sems_b, sems_c, sems_d):
    n = held.shape[0]
    chips = n // 2
    s = lax.axis_index("site")
    k = lax.axis_index("branch")
    core = s % 2
    chip = s // 2
    partner = s - core + (1 - core)
    barrier = pltpu.get_barrier_semaphore()
    pl.semaphore_signal(barrier, inc=1, device_id=(partner, k), device_id_type=MESH_ID)

    def greet(d, carry):
        peer = 2 * lax.rem(chip + d, chips) + core
        pl.semaphore_signal(barrier, inc=1, device_id=(peer, k), device_id_type=MESH_ID)
        return carry

    lax.fori_loop(1, chips, greet, 0)
    pl.semaphore_wait(barrier, chips)
    held[s] = x_ref[...]

    def to_chip(d):
        c = lax.rem(chip + d, chips)
        return pltpu.make_async_remote_copy(
            src_ref=x_ref,
            dst_ref=held.at[s],
            send_sem=sems_a.at[c],
            recv_sem=sems_b.at[chip],
            device_id=(2 * c + core, k),
            device_id_type=MESH_ID,
        )

    def first_send(d, carry):
        to_chip(d).start()
        return carry

    lax.fori_loop(1, chips, first_send, 0)

    def to_partner(c):
        return pltpu.make_async_remote_copy(
            src_ref=held.at[2 * c + core],
            dst_ref=held.at[2 * c + core],
            send_sem=sems_c.at[c],
            recv_sem=sems_d.at[c],
            device_id=(partner, k),
            device_id_type=MESH_ID,
        )

    own = pltpu.make_async_remote_copy(
        src_ref=x_ref,
        dst_ref=held.at[s],
        send_sem=sems_c.at[chip],
        recv_sem=sems_d.at[chip],
        device_id=(partner, k),
        device_id_type=MESH_ID,
    )
    own.start()

    def relay(d, carry):
        c = lax.rem(chip + chips - d, chips)
        pltpu.make_async_remote_copy(
            src_ref=held.at[2 * c + core],
            dst_ref=held.at[2 * c + core],
            send_sem=sems_a.at[c],
            recv_sem=sems_b.at[c],
            device_id=(2 * c + core, k),
            device_id_type=MESH_ID,
        ).wait_recv()
        to_partner(c).start()
        return carry

    lax.fori_loop(1, chips, relay, 0)

    def second_recv(c, carry):
        pltpu.make_async_remote_copy(
            src_ref=held.at[2 * c + 1 - core],
            dst_ref=held.at[2 * c + 1 - core],
            send_sem=sems_c.at[c],
            recv_sem=sems_d.at[c],
            device_id=(partner, k),
            device_id_type=MESH_ID,
        ).wait_recv()
        return carry

    lax.fori_loop(0, chips, second_recv, 0)

    def first_sent(d, carry):
        to_chip(d).wait_send()
        return carry

    lax.fori_loop(1, chips, first_sent, 0)
    own.wait_send()

    def second_sent(d, carry):
        to_partner(lax.rem(chip + d, chips)).wait_send()
        return carry

    lax.fori_loop(1, chips, second_sent, 0)
    per = o_ref.shape[0] // n
    width = o_ref.shape[2]

    def unpack(p, carry):
        for q in range(per):
            o_ref[per * p + q] = held[p, :, q * width : (q + 1) * width]
        return carry

    lax.fori_loop(0, n, unpack, 0)


def pair_gather(x, n, collective_id):
    per = x.shape[1] // x.shape[0]
    return pl.pallas_call(
        pair_gather_kernel,
        out_shape=jax.ShapeDtypeStruct((n * per, x.shape[0], x.shape[0]), jnp.float32),
        in_specs=[pl.BlockSpec(memory_space=pltpu.VMEM)],
        out_specs=pl.BlockSpec(memory_space=pltpu.VMEM),
        scratch_shapes=[
            pltpu.VMEM((n,) + x.shape, jnp.float32),
            pltpu.SemaphoreType.DMA((n // 2,)),
            pltpu.SemaphoreType.DMA((n // 2,)),
            pltpu.SemaphoreType.DMA((n // 2,)),
            pltpu.SemaphoreType.DMA((n // 2,)),
        ],
        compiler_params=pltpu.CompilerParams(collective_id=collective_id, has_side_effects=True),
    )(x)


def body(
    states, gap_mask, weights, leaf_order, exchanges, codon_freq, omega_ratio, lengths, classes
):
    site_count = lax.axis_size("site")
    site_pos = lax.axis_index("site")
    subtree = lax.axis_index("branch")
    site_span = states.shape[1]
    total_sites = site_span * site_count
    total_taxa = LEAF_DEV * lax.axis_size("branch")
    rate_matrix, stationary = build_rates(exchanges, codon_freq, omega_ratio)
    slot_len = jnp.concatenate([lengths, jnp.zeros((1,), lengths.dtype)])
    slot_cls = jnp.concatenate([classes, jnp.zeros((1,), jnp.int32)])
    class_pick = (slot_cls[:, None] == jnp.arange(CLASSES, dtype=jnp.int32)[None, :]).astype(
        jnp.float32
    )
    slot_rates = jnp.einsum("bc,cij->bij", class_pick, rate_matrix, precision=lax.Precision.HIGH)
    scaled = slot_rates * slot_len[:, None, None]
    per_dev = SLOTS // site_count
    own_start = site_pos * per_dev
    own_scaled = lax.dynamic_slice_in_dim(scaled, own_start, per_dev, 0)
    own_pull = None
    own_probs, own_pull = jax.vjp(expm_taylor, own_scaled)
    packed_probs = own_probs.transpose(1, 0, 2).reshape(own_probs.shape[1], -1)
    probs = pair_gather(packed_probs, site_count, 1)
    taxon_rows = lax.dynamic_slice_in_dim(leaf_order, subtree * LEAF_DEV, LEAF_DEV, 0)
    leaves = leaf_partials(
        jnp.take(states, taxon_rows, axis=0), jnp.take(gap_mask, taxon_rows, axis=0)
    )
    levels, messages, logscale = up_pass(probs, leaves)
    top_pack = jnp.concatenate([messages[-1][0], logscale[None, :]], axis=0)
    top_all = lax.all_gather(top_pack, "branch", axis=0, tiled=False)
    top_messages, top_logs = top_all[:, :64, :], top_all[:, 64, :]
    site_ll, above_all = root_terms(stationary, top_messages, top_logs)
    site_weight = weights.astype(jnp.float32)
    loglik_part = jnp.sum(site_weight * site_ll)
    above_top = lax.dynamic_slice_in_dim(above_all, subtree, 1, 0)
    a_list = down_pass(probs, levels, messages, above_top)
    weighted = weigh(a_list, messages, site_weight, total_sites)
    padding = jnp.zeros((1, 64, site_span), jnp.float32)
    weighted_all = jnp.concatenate(weighted + [padding], axis=0)
    partial_all = jnp.concatenate(levels + [padding], axis=0)
    part_above = lax.slice_in_dim(weighted_all, 0, lax.axis_size("site") * per_dev, axis=0)
    part_below = lax.slice_in_dim(partial_all, 0, lax.axis_size("site") * per_dev, axis=0)
    part_counts = jnp.einsum("bis,bjs->bij", part_above, part_below, precision=lax.Precision.HIGH)
    own_counts = pair_scatter(part_counts.reshape(site_count, -1, 128), 2).reshape((per_dev, 64, 64))
    d_scaled = own_pull(own_counts)[0]
    use_rates = lax.dynamic_slice_in_dim(slot_rates, own_start, per_dev, 0)
    use_len = lax.dynamic_slice_in_dim(slot_len, own_start, per_dev, 0)
    use_pick = lax.dynamic_slice_in_dim(class_pick, own_start, per_dev, 0)
    d_length = jnp.sum(d_scaled * use_rates, axis=(1, 2))
    d_rates = jnp.einsum(
        "bc,bij->cij", use_pick, d_scaled * use_len[:, None, None], precision=lax.Precision.HIGH
    )
    unused_rates, pull_rates = jax.vjp(
        lambda table, ratio: build_rates(table, codon_freq, ratio)[0], exchanges, omega_ratio
    )
    d_exch, d_omega = pull_rates(d_rates)
    n_branch = lax.axis_size("branch")
    length_slab = jnp.zeros((n_branch, SLOTS), jnp.float32)
    length_slab = lax.dynamic_update_slice(length_slab, d_length[None, :], (subtree, own_start))
    loglik_keep = jnp.where(subtree == 0, loglik_part, jnp.float32(0.0))
    packed = jnp.concatenate(
        [d_exch.reshape(-1), d_omega, length_slab.reshape(-1), loglik_keep[None]]
    )
    rows = -(-packed.shape[0] // (8 * 128)) * 8
    packed = jnp.pad(packed, (0, rows * 128 - packed.shape[0])).reshape(rows, 128)
    summed = allreduce_all(packed, site_count, n_branch).reshape(-1)
    grad_exch = summed[: 64 * 64].reshape(64, 64)
    grad_omega = summed[64 * 64 : 64 * 64 + CLASSES]
    length_all = summed[64 * 64 + CLASSES : 64 * 64 + CLASSES + n_branch * SLOTS].reshape(n_branch, SLOTS)
    log_total = summed[64 * 64 + CLASSES + n_branch * SLOTS]
    loglik = log_total / total_sites / total_taxa
    length_out = lax.dynamic_index_in_dim(length_all, subtree, 0, keepdims=False)[:EDGES]
    return (grad_exch, grad_omega, length_out, loglik)


def solution(mesh):
    return jax.shard_map(
        body,
        mesh=mesh,
        in_specs=(
            P(None, "site"),
            P(None, "site"),
            P("site"),
            P(),
            P(),
            P(),
            P(),
            P("branch"),
            P("branch"),
        ),
        out_specs=(P(), P(), P("branch"), P()),
        check_vma=False,
    )
```

```python
import jax
import jax.numpy as jnp
import numpy as np
from jax import lax
from jax.sharding import PartitionSpec as P
from jax.experimental import pallas as pl
from jax.experimental.pallas import tpu as pltpu
import functools

MESH_ID = pl.DeviceIdType.MESH

LEVELS = 6
LEAF_DEV = 64
EDGES = 127
SLOTS = 128
CLASSES = 8


CODE_TABLE = "FFLLSSSSYYXXCCXWLLLLPPPPHHQQRRRRIIIMTTTTNNKKSSRRVVVVAAAADDEEGGGG"


def codon_tables():
    amino_acid = np.array(list(CODE_TABLE))
    codon_index = np.arange(64)
    digits = np.stack([codon_index // 16, codon_index // 4 % 4, codon_index % 4], 1)
    differ = (digits[:, None, :] != digits[None, :, :]).sum(-1)
    is_sense = amino_acid != "X"
    single = (differ == 1) & is_sense[:, None] & is_sense[None, :]
    nonsyn = single & (amino_acid[:, None] != amino_acid[None, :])
    return (is_sense.astype(np.float32), single.astype(np.float32), nonsyn.astype(np.float32))


def build_rates(exchanges, codon_freq, omega_ratio):
    is_sense, single, nonsyn = codon_tables()
    stationary = codon_freq * is_sense / jnp.sum(codon_freq * is_sense)
    symmetric = 0.5 * (exchanges + exchanges.T)
    factor = 1.0 + nonsyn[None, :, :] * (omega_ratio[:, None, None] - 1.0)
    off_diag = symmetric[None, :, :] * stationary[None, None, :] * factor * single[None, :, :]
    row_total = jnp.sum(off_diag, axis=2)
    mean_rate = jnp.sum(stationary[None, :] * row_total, axis=1)
    identity = jnp.eye(64, dtype=exchanges.dtype)
    rate_matrix = (off_diag - row_total[:, :, None] * identity[None]) / mean_rate[:, None, None]
    return (rate_matrix, stationary)


def product(left, right):
    return jnp.einsum("bij,bjk->bik", left, right, precision=lax.Precision.HIGH)


def expm_taylor(scaled):
    reduced = scaled / 16.0
    identity = jnp.eye(64, dtype=scaled.dtype)
    series = jnp.broadcast_to(identity, scaled.shape)
    for degree in range(8, 0, -1):
        series = identity + product(reduced, series) / degree
    for square_step in range(4):
        series = product(series, series)
    return series


def forward(probs, vectors):
    return jnp.einsum("bij,bjs->bis", probs, vectors, precision=lax.Precision.HIGH)


def carried(probs, vectors):
    return jnp.einsum("bji,bjs->bis", probs, vectors, precision=lax.Precision.HIGH)


def leaf_partials(leaf_states, gap_rows):
    codon_axis = jnp.arange(64, dtype=jnp.int32)
    indicator = (leaf_states[:, None, :] == codon_axis[None, :, None]).astype(jnp.float32)
    return jnp.where(gap_rows[:, None, :] > 0, jnp.float32(1.0), indicator)


def up_pass(probs, leaves):
    levels = [leaves]
    messages = []
    logscale = jnp.zeros(leaves.shape[2:], jnp.float32)
    current = leaves
    for height in range(LEVELS):
        amount = current.shape[0]
        offset = 2 * LEAF_DEV - 2 * amount
        message = forward(probs[offset : offset + amount], current)
        messages.append(message)
        raw_parent = message[0::2] * message[1::2]
        scaling = jnp.sum(raw_parent, axis=1)
        current = raw_parent / scaling[:, None, :]
        logscale = logscale + jnp.sum(jnp.log(scaling), axis=0)
        levels.append(current)
    messages.append(forward(probs[EDGES - 1 : EDGES], current))
    return (levels, messages, logscale)


def root_terms(stationary, top_messages, top_logs):
    members = top_messages.shape[0]
    joint = stationary[:, None] * top_messages[0]
    for member in range(1, members):
        joint = joint * top_messages[member]
    site_ll = jnp.log(jnp.sum(joint, axis=0)) + jnp.sum(top_logs, axis=0)
    above_list = []
    for member in range(members):
        vector = jnp.broadcast_to(stationary[:, None], top_messages.shape[1:])
        for other in range(members):
            if other != member:
                vector = vector * top_messages[other]
        above_list.append(vector)
    return (site_ll, jnp.stack(above_list))


def down_pass(probs, levels, messages, above_top):
    a_list = [above_top]
    current = above_top
    for height in range(LEVELS, 0, -1):
        amount = levels[height].shape[0]
        offset = 2 * LEAF_DEV - 2 * amount
        down_part = carried(probs[offset : offset + amount], current)
        down_part = down_part / jnp.sum(down_part, axis=1, keepdims=True)
        message = messages[height - 1]
        current = jnp.stack([down_part * message[1::2], down_part * message[0::2]], axis=1).reshape(
            message.shape
        )
        a_list.append(current)
    return a_list[::-1]


def weigh(a_list, messages, site_weight, total_sites):
    weighted = []
    for vector, message in zip(a_list, messages):
        likelihood = jnp.sum(vector * message, axis=1)
        weighted.append(vector * (site_weight / (likelihood * total_sites))[:, None, :])
    return weighted


def sum_groups(n_site, n_branch):
    s = lax.axis_index("site")
    k = lax.axis_index("branch")
    core = s % 2
    plane = s // 2
    return [
        (2, core, lambda c: (s - core + c, k)),
        (n_branch, k, lambda c: (s, c)),
        (n_site // 2, plane, lambda c: (2 * c + core, k)),
    ]


def allreduce_kernel(n_site, n_branch, x_ref, o_ref, held, send_sems, recv_sems):
    stages = sum_groups(n_site, n_branch)
    barrier = pltpu.get_barrier_semaphore()
    count = 0
    for size, mine, where in stages:
        for d in range(1, size):
            other = lax.rem(mine + d, size)
            pl.semaphore_signal(barrier, inc=1, device_id=where(other), device_id_type=MESH_ID)
            count += 1
    pl.semaphore_wait(barrier, count)
    total = x_ref[...]
    for st, (size, mine, where) in enumerate(stages):
        held[st, mine] = total
        sends = []
        for d in range(1, size):
            other = lax.rem(mine + d, size)
            copy = pltpu.make_async_remote_copy(
                src_ref=held.at[st, mine],
                dst_ref=held.at[st, mine],
                send_sem=send_sems.at[st, other],
                recv_sem=recv_sems.at[st, mine],
                device_id=where(other),
                device_id_type=MESH_ID,
            )
            copy.start()
            sends.append(copy)
        for d in range(1, size):
            other = lax.rem(mine + d, size)
            incoming = pltpu.make_async_remote_copy(
                src_ref=held.at[st, other],
                dst_ref=held.at[st, other],
                send_sem=send_sems.at[st, other],
                recv_sem=recv_sems.at[st, other],
                device_id=where(other),
                device_id_type=MESH_ID,
            )
            incoming.wait_recv()
        for copy in sends:
            copy.wait_send()
        total = held[st, 0]
        for c in range(1, size):
            total = total + held[st, c]
    o_ref[...] = total


def allreduce_all(x, n_site, n_branch):
    rows = x.shape[0]
    return pl.pallas_call(
        functools.partial(allreduce_kernel, n_site, n_branch),
        out_shape=jax.ShapeDtypeStruct(x.shape, jnp.float32),
        in_specs=[pl.BlockSpec(memory_space=pltpu.VMEM)],
        out_specs=pl.BlockSpec(memory_space=pltpu.VMEM),
        scratch_shapes=[
            pltpu.VMEM((3, n_site // 2, rows, 128), jnp.float32),
            pltpu.SemaphoreType.DMA((3, n_site // 2)),
            pltpu.SemaphoreType.DMA((3, n_site // 2)),
        ],
        compiler_params=pltpu.CompilerParams(collective_id=0, has_side_effects=True),
    )(x)


def exchange_kernel(axis, gather, x_ref, o_ref, held, send_sems, recv_sems):
    n = held.shape[0]
    me = lax.axis_index(axis)
    other_axis = "branch" if axis == "site" else "site"
    fixed = lax.axis_index(other_axis)

    def device(p):
        return (p, fixed) if axis == "site" else (fixed, p)

    barrier = pltpu.get_barrier_semaphore()

    def greet(d, carry):
        pl.semaphore_signal(
            barrier, inc=1, device_id=device(lax.rem(me + d, n)), device_id_type=MESH_ID
        )
        return carry

    lax.fori_loop(1, n, greet, 0)
    pl.semaphore_wait(barrier, n - 1)
    if gather:
        held[me] = x_ref[...]
    else:
        held[me] = x_ref[me]

    def outgoing(d):
        p = lax.rem(me + d, n)
        return pltpu.make_async_remote_copy(
            src_ref=x_ref if gather else x_ref.at[p],
            dst_ref=held.at[me],
            send_sem=send_sems.at[p],
            recv_sem=recv_sems.at[me],
            device_id=device(p),
            device_id_type=MESH_ID,
        )

    def send(d, carry):
        outgoing(d).start()
        return carry

    lax.fori_loop(1, n, send, 0)

    def receive(d, carry):
        p = lax.rem(me + n - d, n)
        pltpu.make_async_remote_copy(
            src_ref=held.at[p],
            dst_ref=held.at[p],
            send_sem=send_sems.at[p],
            recv_sem=recv_sems.at[p],
            device_id=device(p),
            device_id_type=MESH_ID,
        ).wait_recv()
        return carry

    lax.fori_loop(1, n, receive, 0)

    def sent(d, carry):
        outgoing(d).wait_send()
        return carry

    lax.fori_loop(1, n, sent, 0)
    if gather:
        o_ref[...] = held[...]
    else:
        o_ref[...] = lax.fori_loop(1, n, lambda j, acc: acc + held[j], held[0])


def exchange(x, axis, n, gather, collective_id):
    chunk = x.shape if gather else x.shape[1:]
    out_shape = (n,) + chunk if gather else chunk
    return pl.pallas_call(
        functools.partial(exchange_kernel, axis, gather),
        out_shape=jax.ShapeDtypeStruct(out_shape, jnp.float32),
        in_specs=[pl.BlockSpec(memory_space=pltpu.VMEM)],
        out_specs=pl.BlockSpec(memory_space=pltpu.VMEM),
        scratch_shapes=[
            pltpu.VMEM((n,) + chunk, jnp.float32),
            pltpu.SemaphoreType.DMA((n,)),
            pltpu.SemaphoreType.DMA((n,)),
        ],
        compiler_params=pltpu.CompilerParams(collective_id=collective_id, has_side_effects=True),
    )(x)


def pair_scatter_kernel(x_ref, o_ref, packed, pair_buf, pair_sum, held, sems_a, sems_b, sems_c, sems_d):
    n = packed.shape[0]
    per = o_ref.shape[0]
    width = o_ref.shape[2]

    def pack(p, carry):
        for q in range(per):
            packed[p, :, q * width : (q + 1) * width] = x_ref[per * p + q]
        return carry

    lax.fori_loop(0, n, pack, 0)
    chips = n // 2
    s = lax.axis_index("site")
    k = lax.axis_index("branch")
    core = s % 2
    chip = s // 2
    partner = s - core + (1 - core)
    barrier = pltpu.get_barrier_semaphore()
    pl.semaphore_signal(barrier, inc=1, device_id=(partner, k), device_id_type=MESH_ID)

    def greet(d, carry):
        peer = 2 * lax.rem(chip + d, chips) + core
        pl.semaphore_signal(barrier, inc=1, device_id=(peer, k), device_id_type=MESH_ID)
        return carry

    lax.fori_loop(1, chips, greet, 0)
    pl.semaphore_wait(barrier, chips)

    def to_partner(m):
        return pltpu.make_async_remote_copy(
            src_ref=packed.at[2 * m + 1 - core],
            dst_ref=pair_buf.at[m],
            send_sem=sems_a.at[m],
            recv_sem=sems_b.at[m],
            device_id=(partner, k),
            device_id_type=MESH_ID,
        )

    def first_send(m, carry):
        to_partner(m).start()
        return carry

    lax.fori_loop(0, chips, first_send, 0)

    def to_chip(c):
        return pltpu.make_async_remote_copy(
            src_ref=pair_sum.at[c],
            dst_ref=held.at[chip],
            send_sem=sems_c.at[c],
            recv_sem=sems_d.at[chip],
            device_id=(2 * c + core, k),
            device_id_type=MESH_ID,
        )

    to_partner(chip).wait_recv()
    pair_sum[chip] = packed[2 * chip + core] + pair_buf[chip]
    held[chip] = pair_sum[chip]

    def add_and_send(d, carry):
        c = lax.rem(chip + d, chips)
        to_partner(c).wait_recv()
        pair_sum[c] = packed[2 * c + core] + pair_buf[c]
        to_chip(c).start()
        return carry

    lax.fori_loop(1, chips, add_and_send, 0)

    def second_recv(d, carry):
        c = lax.rem(chip + chips - d, chips)
        pltpu.make_async_remote_copy(
            src_ref=held.at[c],
            dst_ref=held.at[c],
            send_sem=sems_c.at[c],
            recv_sem=sems_d.at[c],
            device_id=(2 * c + core, k),
            device_id_type=MESH_ID,
        ).wait_recv()
        return carry

    lax.fori_loop(1, chips, second_recv, 0)

    def first_sent(m, carry):
        to_partner(m).wait_send()
        return carry

    lax.fori_loop(0, chips, first_sent, 0)

    def second_sent(d, carry):
        to_chip(lax.rem(chip + d, chips)).wait_send()
        return carry

    lax.fori_loop(1, chips, second_sent, 0)
    total = lax.fori_loop(1, chips, lambda j, acc: acc + held[j], held[0])
    for q in range(per):
        o_ref[q] = total[:, q * width : (q + 1) * width]


def pair_scatter(x, n, collective_id):
    per = x.shape[0] // n
    chunk = (x.shape[1], per * x.shape[2])
    return pl.pallas_call(
        pair_scatter_kernel,
        out_shape=jax.ShapeDtypeStruct((per,) + x.shape[1:], jnp.float32),
        in_specs=[pl.BlockSpec(memory_space=pltpu.VMEM)],
        out_specs=pl.BlockSpec(memory_space=pltpu.VMEM),
        scratch_shapes=[
            pltpu.VMEM((n,) + chunk, jnp.float32),
            pltpu.VMEM((n // 2,) + chunk, jnp.float32),
            pltpu.VMEM((n // 2,) + chunk, jnp.float32),
            pltpu.VMEM((n // 2,) + chunk, jnp.float32),
            pltpu.SemaphoreType.DMA((n // 2,)),
            pltpu.SemaphoreType.DMA((n // 2,)),
            pltpu.SemaphoreType.DMA((n // 2,)),
            pltpu.SemaphoreType.DMA((n // 2,)),
        ],
        compiler_params=pltpu.CompilerParams(collective_id=collective_id, has_side_effects=True),
    )(x)


def pair_gather_kernel(x_ref, o_ref, held, sems_a, sems_b, sems_c, sems_d):
    n = held.shape[0]
    chips = n // 2
    s = lax.axis_index("site")
    k = lax.axis_index("branch")
    core = s % 2
    chip = s // 2
    partner = s - core + (1 - core)
    barrier = pltpu.get_barrier_semaphore()
    pl.semaphore_signal(barrier, inc=1, device_id=(partner, k), device_id_type=MESH_ID)

    def greet(d, carry):
        peer = 2 * lax.rem(chip + d, chips) + core
        pl.semaphore_signal(barrier, inc=1, device_id=(peer, k), device_id_type=MESH_ID)
        return carry

    lax.fori_loop(1, chips, greet, 0)
    pl.semaphore_wait(barrier, chips)
    held[s] = x_ref[...]

    def to_chip(d):
        c = lax.rem(chip + d, chips)
        return pltpu.make_async_remote_copy(
            src_ref=x_ref,
            dst_ref=held.at[s],
            send_sem=sems_a.at[c],
            recv_sem=sems_b.at[chip],
            device_id=(2 * c + core, k),
            device_id_type=MESH_ID,
        )

    def first_send(d, carry):
        to_chip(d).start()
        return carry

    lax.fori_loop(1, chips, first_send, 0)

    def to_partner(c):
        return pltpu.make_async_remote_copy(
            src_ref=held.at[2 * c + core],
            dst_ref=held.at[2 * c + core],
            send_sem=sems_c.at[c],
            recv_sem=sems_d.at[c],
            device_id=(partner, k),
            device_id_type=MESH_ID,
        )

    own = pltpu.make_async_remote_copy(
        src_ref=x_ref,
        dst_ref=held.at[s],
        send_sem=sems_c.at[chip],
        recv_sem=sems_d.at[chip],
        device_id=(partner, k),
        device_id_type=MESH_ID,
    )
    own.start()

    def relay(d, carry):
        c = lax.rem(chip + chips - d, chips)
        pltpu.make_async_remote_copy(
            src_ref=held.at[2 * c + core],
            dst_ref=held.at[2 * c + core],
            send_sem=sems_a.at[c],
            recv_sem=sems_b.at[c],
            device_id=(2 * c + core, k),
            device_id_type=MESH_ID,
        ).wait_recv()
        to_partner(c).start()
        return carry

    lax.fori_loop(1, chips, relay, 0)

    def second_recv(c, carry):
        pltpu.make_async_remote_copy(
            src_ref=held.at[2 * c + 1 - core],
            dst_ref=held.at[2 * c + 1 - core],
            send_sem=sems_c.at[c],
            recv_sem=sems_d.at[c],
            device_id=(partner, k),
            device_id_type=MESH_ID,
        ).wait_recv()
        return carry

    lax.fori_loop(0, chips, second_recv, 0)

    def first_sent(d, carry):
        to_chip(d).wait_send()
        return carry

    lax.fori_loop(1, chips, first_sent, 0)
    own.wait_send()

    def second_sent(d, carry):
        to_partner(lax.rem(chip + d, chips)).wait_send()
        return carry

    lax.fori_loop(1, chips, second_sent, 0)
    per = o_ref.shape[0] // n
    width = o_ref.shape[2]

    def unpack(p, carry):
        for q in range(per):
            o_ref[per * p + q] = held[p, :, q * width : (q + 1) * width]
        return carry

    lax.fori_loop(0, n, unpack, 0)


def pair_gather(x, n, collective_id):
    per = x.shape[1] // x.shape[0]
    return pl.pallas_call(
        pair_gather_kernel,
        out_shape=jax.ShapeDtypeStruct((n * per, x.shape[0], x.shape[0]), jnp.float32),
        in_specs=[pl.BlockSpec(memory_space=pltpu.VMEM)],
        out_specs=pl.BlockSpec(memory_space=pltpu.VMEM),
        scratch_shapes=[
            pltpu.VMEM((n,) + x.shape, jnp.float32),
            pltpu.SemaphoreType.DMA((n // 2,)),
            pltpu.SemaphoreType.DMA((n // 2,)),
            pltpu.SemaphoreType.DMA((n // 2,)),
            pltpu.SemaphoreType.DMA((n // 2,)),
        ],
        compiler_params=pltpu.CompilerParams(collective_id=collective_id, has_side_effects=True),
    )(x)


def body(
    states, gap_mask, weights, leaf_order, exchanges, codon_freq, omega_ratio, lengths, classes
):
    site_count = lax.axis_size("site")
    site_pos = lax.axis_index("site")
    subtree = lax.axis_index("branch")
    site_span = states.shape[1]
    total_sites = site_span * site_count
    total_taxa = LEAF_DEV * lax.axis_size("branch")
    rate_matrix, stationary = build_rates(exchanges, codon_freq, omega_ratio)
    slot_len = jnp.concatenate([lengths, jnp.zeros((1,), lengths.dtype)])
    slot_cls = jnp.concatenate([classes, jnp.zeros((1,), jnp.int32)])
    class_pick = (slot_cls[:, None] == jnp.arange(CLASSES, dtype=jnp.int32)[None, :]).astype(
        jnp.float32
    )
    slot_rates = jnp.einsum("bc,cij->bij", class_pick, rate_matrix, precision=lax.Precision.HIGH)
    scaled = slot_rates * slot_len[:, None, None]
    per_dev = SLOTS // site_count
    own_start = site_pos * per_dev
    own_scaled = lax.dynamic_slice_in_dim(scaled, own_start, per_dev, 0)
    own_pull = None
    own_probs, own_pull = jax.vjp(expm_taylor, own_scaled)
    packed_probs = own_probs.transpose(1, 0, 2).reshape(own_probs.shape[1], -1)
    probs = pair_gather(packed_probs, site_count, 1)
    taxon_rows = lax.dynamic_slice_in_dim(leaf_order, subtree * LEAF_DEV, LEAF_DEV, 0)
    leaves = leaf_partials(
        jnp.take(states, taxon_rows, axis=0), jnp.take(gap_mask, taxon_rows, axis=0)
    )
    levels, messages, logscale = up_pass(probs, leaves)
    top_pack = jnp.concatenate([messages[-1][0], logscale[None, :]], axis=0)
    top_all = lax.all_gather(top_pack, "branch", axis=0, tiled=False)
    top_messages, top_logs = top_all[:, :64, :], top_all[:, 64, :]
    site_ll, above_all = root_terms(stationary, top_messages, top_logs)
    site_weight = weights.astype(jnp.float32)
    loglik_part = jnp.sum(site_weight * site_ll)
    above_top = lax.dynamic_slice_in_dim(above_all, subtree, 1, 0)
    a_list = down_pass(probs, levels, messages, above_top)
    weighted = weigh(a_list, messages, site_weight, total_sites)
    padding = jnp.zeros((1, 64, site_span), jnp.float32)
    weighted_all = jnp.concatenate(weighted + [padding], axis=0)
    partial_all = jnp.concatenate(levels + [padding], axis=0)
    part_above = lax.slice_in_dim(weighted_all, 0, lax.axis_size("site") * per_dev, axis=0)
    part_below = lax.slice_in_dim(partial_all, 0, lax.axis_size("site") * per_dev, axis=0)
    part_counts = jnp.einsum("bis,bjs->bij", part_above, part_below, precision=lax.Precision.HIGH)
    own_counts = pair_scatter(part_counts, site_count, 2)
    d_scaled = own_pull(own_counts)[0]
    use_rates = lax.dynamic_slice_in_dim(slot_rates, own_start, per_dev, 0)
    use_len = lax.dynamic_slice_in_dim(slot_len, own_start, per_dev, 0)
    use_pick = lax.dynamic_slice_in_dim(class_pick, own_start, per_dev, 0)
    d_length = jnp.sum(d_scaled * use_rates, axis=(1, 2))
    d_rates = jnp.einsum(
        "bc,bij->cij", use_pick, d_scaled * use_len[:, None, None], precision=lax.Precision.HIGH
    )
    unused_rates, pull_rates = jax.vjp(
        lambda table, ratio: build_rates(table, codon_freq, ratio)[0], exchanges, omega_ratio
    )
    d_exch, d_omega = pull_rates(d_rates)
    n_branch = lax.axis_size("branch")
    length_slab = jnp.zeros((n_branch, SLOTS), jnp.float32)
    length_slab = lax.dynamic_update_slice(length_slab, d_length[None, :], (subtree, own_start))
    loglik_keep = jnp.where(subtree == 0, loglik_part, jnp.float32(0.0))
    packed = jnp.concatenate(
        [d_exch.reshape(-1), d_omega, length_slab.reshape(-1), loglik_keep[None]]
    )
    rows = -(-packed.shape[0] // (8 * 128)) * 8
    packed = jnp.pad(packed, (0, rows * 128 - packed.shape[0])).reshape(rows, 128)
    summed = allreduce_all(packed, site_count, n_branch).reshape(-1)
    grad_exch = summed[: 64 * 64].reshape(64, 64)
    grad_omega = summed[64 * 64 : 64 * 64 + CLASSES]
    length_all = summed[64 * 64 + CLASSES : 64 * 64 + CLASSES + n_branch * SLOTS].reshape(n_branch, SLOTS)
    log_total = summed[64 * 64 + CLASSES + n_branch * SLOTS]
    loglik = log_total / total_sites / total_taxa
    length_out = lax.dynamic_index_in_dim(length_all, subtree, 0, keepdims=False)[:EDGES]
    return (grad_exch, grad_omega, length_out, loglik)


def solution(mesh):
    return jax.shard_map(
        body,
        mesh=mesh,
        in_specs=(
            P(None, "site"),
            P(None, "site"),
            P("site"),
            P(),
            P(),
            P(),
            P(),
            P("branch"),
            P("branch"),
        ),
        out_specs=(P(), P(), P("branch"), P()),
        check_vma=False,
    )
```

```python
import jax
import jax.numpy as jnp
import numpy as np
from jax import lax
from jax.sharding import PartitionSpec as P
from jax.experimental import pallas as pl
from jax.experimental.pallas import tpu as pltpu
import functools

MESH_ID = pl.DeviceIdType.MESH

LEVELS = 6
LEAF_DEV = 64
EDGES = 127
SLOTS = 128
CLASSES = 8


CODE_TABLE = "FFLLSSSSYYXXCCXWLLLLPPPPHHQQRRRRIIIMTTTTNNKKSSRRVVVVAAAADDEEGGGG"


def codon_tables():
    amino_acid = np.array(list(CODE_TABLE))
    codon_index = np.arange(64)
    digits = np.stack([codon_index // 16, codon_index // 4 % 4, codon_index % 4], 1)
    differ = (digits[:, None, :] != digits[None, :, :]).sum(-1)
    is_sense = amino_acid != "X"
    single = (differ == 1) & is_sense[:, None] & is_sense[None, :]
    nonsyn = single & (amino_acid[:, None] != amino_acid[None, :])
    return (is_sense.astype(np.float32), single.astype(np.float32), nonsyn.astype(np.float32))


def build_rates(exchanges, codon_freq, omega_ratio):
    is_sense, single, nonsyn = codon_tables()
    stationary = codon_freq * is_sense / jnp.sum(codon_freq * is_sense)
    symmetric = 0.5 * (exchanges + exchanges.T)
    factor = 1.0 + nonsyn[None, :, :] * (omega_ratio[:, None, None] - 1.0)
    off_diag = symmetric[None, :, :] * stationary[None, None, :] * factor * single[None, :, :]
    row_total = jnp.sum(off_diag, axis=2)
    mean_rate = jnp.sum(stationary[None, :] * row_total, axis=1)
    identity = jnp.eye(64, dtype=exchanges.dtype)
    rate_matrix = (off_diag - row_total[:, :, None] * identity[None]) / mean_rate[:, None, None]
    return (rate_matrix, stationary)


def product(left, right):
    return jnp.einsum("bij,bjk->bik", left, right, precision=lax.Precision.HIGH)


def expm_taylor(scaled):
    reduced = scaled / 16.0
    identity = jnp.eye(64, dtype=scaled.dtype)
    series = jnp.broadcast_to(identity, scaled.shape)
    for degree in range(8, 0, -1):
        series = identity + product(reduced, series) / degree
    for square_step in range(4):
        series = product(series, series)
    return series


def forward(probs, vectors):
    return jnp.einsum("bij,bjs->bis", probs, vectors, precision=lax.Precision.HIGH)


def carried(probs, vectors):
    return jnp.einsum("bji,bjs->bis", probs, vectors, precision=lax.Precision.HIGH)


def leaf_partials(leaf_states, gap_rows):
    codon_axis = jnp.arange(64, dtype=jnp.int32)
    indicator = (leaf_states[:, None, :] == codon_axis[None, :, None]).astype(jnp.float32)
    return jnp.where(gap_rows[:, None, :] > 0, jnp.float32(1.0), indicator)


def up_pass(probs, leaves):
    levels = [leaves]
    messages = []
    logscale = jnp.zeros(leaves.shape[2:], jnp.float32)
    current = leaves
    for height in range(LEVELS):
        amount = current.shape[0]
        offset = 2 * LEAF_DEV - 2 * amount
        message = forward(probs[offset : offset + amount], current)
        messages.append(message)
        raw_parent = message[0::2] * message[1::2]
        scaling = jnp.sum(raw_parent, axis=1)
        current = raw_parent / scaling[:, None, :]
        logscale = logscale + jnp.sum(jnp.log(scaling), axis=0)
        levels.append(current)
    messages.append(forward(probs[EDGES - 1 : EDGES], current))
    return (levels, messages, logscale)


def root_terms(stationary, top_messages, top_logs):
    members = top_messages.shape[0]
    joint = stationary[:, None] * top_messages[0]
    for member in range(1, members):
        joint = joint * top_messages[member]
    site_ll = jnp.log(jnp.sum(joint, axis=0)) + jnp.sum(top_logs, axis=0)
    above_list = []
    for member in range(members):
        vector = jnp.broadcast_to(stationary[:, None], top_messages.shape[1:])
        for other in range(members):
            if other != member:
                vector = vector * top_messages[other]
        above_list.append(vector)
    return (site_ll, jnp.stack(above_list))


def down_pass(probs, levels, messages, above_top):
    a_list = [above_top]
    current = above_top
    for height in range(LEVELS, 0, -1):
        amount = levels[height].shape[0]
        offset = 2 * LEAF_DEV - 2 * amount
        down_part = carried(probs[offset : offset + amount], current)
        down_part = down_part / jnp.sum(down_part, axis=1, keepdims=True)
        message = messages[height - 1]
        current = jnp.stack([down_part * message[1::2], down_part * message[0::2]], axis=1).reshape(
            message.shape
        )
        a_list.append(current)
    return a_list[::-1]


def weigh(a_list, messages, site_weight, total_sites):
    weighted = []
    for vector, message in zip(a_list, messages):
        likelihood = jnp.sum(vector * message, axis=1)
        weighted.append(vector * (site_weight / (likelihood * total_sites))[:, None, :])
    return weighted


def sum_groups(n_site, n_branch):
    s = lax.axis_index("site")
    k = lax.axis_index("branch")
    core = s % 2
    plane = s // 2
    return [
        (2, core, lambda c: (s - core + c, k)),
        (n_branch, k, lambda c: (s, c)),
        (n_site // 2, plane, lambda c: (2 * c + core, k)),
    ]


def allreduce_kernel(n_site, n_branch, x_ref, o_ref, held, send_sems, recv_sems):
    stages = sum_groups(n_site, n_branch)
    barrier = pltpu.get_barrier_semaphore()
    count = 0
    for size, mine, where in stages:
        for d in range(1, size):
            other = lax.rem(mine + d, size)
            pl.semaphore_signal(barrier, inc=1, device_id=where(other), device_id_type=MESH_ID)
            count += 1
    pl.semaphore_wait(barrier, count)
    total = x_ref[...]
    for st, (size, mine, where) in enumerate(stages):
        held[st, mine] = total
        sends = []
        for d in range(1, size):
            other = lax.rem(mine + d, size)
            copy = pltpu.make_async_remote_copy(
                src_ref=held.at[st, mine],
                dst_ref=held.at[st, mine],
                send_sem=send_sems.at[st, other],
                recv_sem=recv_sems.at[st, mine],
                device_id=where(other),
                device_id_type=MESH_ID,
            )
            copy.start()
            sends.append(copy)
        for d in range(1, size):
            other = lax.rem(mine + d, size)
            incoming = pltpu.make_async_remote_copy(
                src_ref=held.at[st, other],
                dst_ref=held.at[st, other],
                send_sem=send_sems.at[st, other],
                recv_sem=recv_sems.at[st, other],
                device_id=where(other),
                device_id_type=MESH_ID,
            )
            incoming.wait_recv()
        for copy in sends:
            copy.wait_send()
        total = held[st, 0]
        for c in range(1, size):
            total = total + held[st, c]
    o_ref[...] = total


def allreduce_all(x, n_site, n_branch):
    rows = x.shape[0]
    return pl.pallas_call(
        functools.partial(allreduce_kernel, n_site, n_branch),
        out_shape=jax.ShapeDtypeStruct(x.shape, jnp.float32),
        in_specs=[pl.BlockSpec(memory_space=pltpu.VMEM)],
        out_specs=pl.BlockSpec(memory_space=pltpu.VMEM),
        scratch_shapes=[
            pltpu.VMEM((3, n_site // 2, rows, 128), jnp.float32),
            pltpu.SemaphoreType.DMA((3, n_site // 2)),
            pltpu.SemaphoreType.DMA((3, n_site // 2)),
        ],
        compiler_params=pltpu.CompilerParams(collective_id=0, has_side_effects=True),
    )(x)


def exchange_kernel(axis, gather, x_ref, o_ref, held, send_sems, recv_sems):
    n = held.shape[0]
    me = lax.axis_index(axis)
    other_axis = "branch" if axis == "site" else "site"
    fixed = lax.axis_index(other_axis)

    def device(p):
        return (p, fixed) if axis == "site" else (fixed, p)

    barrier = pltpu.get_barrier_semaphore()

    def greet(d, carry):
        pl.semaphore_signal(
            barrier, inc=1, device_id=device(lax.rem(me + d, n)), device_id_type=MESH_ID
        )
        return carry

    lax.fori_loop(1, n, greet, 0)
    pl.semaphore_wait(barrier, n - 1)
    if gather:
        held[me] = x_ref[...]
    else:
        held[me] = x_ref[me]

    def outgoing(d):
        p = lax.rem(me + d, n)
        return pltpu.make_async_remote_copy(
            src_ref=x_ref if gather else x_ref.at[p],
            dst_ref=held.at[me],
            send_sem=send_sems.at[p],
            recv_sem=recv_sems.at[me],
            device_id=device(p),
            device_id_type=MESH_ID,
        )

    def send(d, carry):
        outgoing(d).start()
        return carry

    lax.fori_loop(1, n, send, 0)

    def receive(d, carry):
        p = lax.rem(me + n - d, n)
        pltpu.make_async_remote_copy(
            src_ref=held.at[p],
            dst_ref=held.at[p],
            send_sem=send_sems.at[p],
            recv_sem=recv_sems.at[p],
            device_id=device(p),
            device_id_type=MESH_ID,
        ).wait_recv()
        return carry

    lax.fori_loop(1, n, receive, 0)

    def sent(d, carry):
        outgoing(d).wait_send()
        return carry

    lax.fori_loop(1, n, sent, 0)
    if gather:
        o_ref[...] = held[...]
    else:
        o_ref[...] = lax.fori_loop(1, n, lambda j, acc: acc + held[j], held[0])


def exchange(x, axis, n, gather, collective_id):
    chunk = x.shape if gather else x.shape[1:]
    out_shape = (n,) + chunk if gather else chunk
    return pl.pallas_call(
        functools.partial(exchange_kernel, axis, gather),
        out_shape=jax.ShapeDtypeStruct(out_shape, jnp.float32),
        in_specs=[pl.BlockSpec(memory_space=pltpu.VMEM)],
        out_specs=pl.BlockSpec(memory_space=pltpu.VMEM),
        scratch_shapes=[
            pltpu.VMEM((n,) + chunk, jnp.float32),
            pltpu.SemaphoreType.DMA((n,)),
            pltpu.SemaphoreType.DMA((n,)),
        ],
        compiler_params=pltpu.CompilerParams(collective_id=collective_id, has_side_effects=True),
    )(x)


def pair_scatter_kernel(x_ref, o_ref, packed, pair_buf, pair_sum, held, sems_a, sems_b, sems_c, sems_d):
    n = packed.shape[0]
    per = o_ref.shape[0]
    width = o_ref.shape[2]

    def pack(p, carry):
        for q in range(per):
            packed[p, :, q * width : (q + 1) * width] = x_ref[per * p + q]
        return carry

    lax.fori_loop(0, n, pack, 0)
    chips = n // 2
    s = lax.axis_index("site")
    k = lax.axis_index("branch")
    core = s % 2
    chip = s // 2
    partner = s - core + (1 - core)
    barrier = pltpu.get_barrier_semaphore()
    pl.semaphore_signal(barrier, inc=1, device_id=(partner, k), device_id_type=MESH_ID)

    def greet(d, carry):
        peer = 2 * lax.rem(chip + d, chips) + core
        pl.semaphore_signal(barrier, inc=1, device_id=(peer, k), device_id_type=MESH_ID)
        return carry

    lax.fori_loop(1, chips, greet, 0)
    pl.semaphore_wait(barrier, chips)

    def to_partner(m):
        return pltpu.make_async_remote_copy(
            src_ref=packed.at[2 * m + 1 - core],
            dst_ref=pair_buf.at[m],
            send_sem=sems_a.at[m],
            recv_sem=sems_b.at[m],
            device_id=(partner, k),
            device_id_type=MESH_ID,
        )

    def first_send(m, carry):
        to_partner(m).start()
        return carry

    lax.fori_loop(0, chips, first_send, 0)

    def to_chip(c):
        return pltpu.make_async_remote_copy(
            src_ref=pair_sum.at[c],
            dst_ref=held.at[chip],
            send_sem=sems_c.at[c],
            recv_sem=sems_d.at[chip],
            device_id=(2 * c + core, k),
            device_id_type=MESH_ID,
        )

    to_partner(chip).wait_recv()
    pair_sum[chip] = packed[2 * chip + core] + pair_buf[chip]
    held[chip] = pair_sum[chip]

    def add_and_send(d, carry):
        c = lax.rem(chip + d, chips)
        to_partner(c).wait_recv()
        pair_sum[c] = packed[2 * c + core] + pair_buf[c]
        to_chip(c).start()
        return carry

    lax.fori_loop(1, chips, add_and_send, 0)

    def second_recv(d, carry):
        c = lax.rem(chip + chips - d, chips)
        pltpu.make_async_remote_copy(
            src_ref=held.at[c],
            dst_ref=held.at[c],
            send_sem=sems_c.at[c],
            recv_sem=sems_d.at[c],
            device_id=(2 * c + core, k),
            device_id_type=MESH_ID,
        ).wait_recv()
        return carry

    lax.fori_loop(1, chips, second_recv, 0)

    def first_sent(m, carry):
        to_partner(m).wait_send()
        return carry

    lax.fori_loop(0, chips, first_sent, 0)

    def second_sent(d, carry):
        to_chip(lax.rem(chip + d, chips)).wait_send()
        return carry

    lax.fori_loop(1, chips, second_sent, 0)
    total = lax.fori_loop(1, chips, lambda j, acc: acc + held[j], held[0])
    for q in range(per):
        o_ref[q] = total[:, q * width : (q + 1) * width]


def pair_scatter(x, n, collective_id):
    per = x.shape[0] // n
    chunk = (x.shape[1], per * x.shape[2])
    return pl.pallas_call(
        pair_scatter_kernel,
        out_shape=jax.ShapeDtypeStruct((per,) + x.shape[1:], jnp.float32),
        in_specs=[pl.BlockSpec(memory_space=pltpu.VMEM)],
        out_specs=pl.BlockSpec(memory_space=pltpu.VMEM),
        scratch_shapes=[
            pltpu.VMEM((n,) + chunk, jnp.float32),
            pltpu.VMEM((n // 2,) + chunk, jnp.float32),
            pltpu.VMEM((n // 2,) + chunk, jnp.float32),
            pltpu.VMEM((n // 2,) + chunk, jnp.float32),
            pltpu.SemaphoreType.DMA((n // 2,)),
            pltpu.SemaphoreType.DMA((n // 2,)),
            pltpu.SemaphoreType.DMA((n // 2,)),
            pltpu.SemaphoreType.DMA((n // 2,)),
        ],
        compiler_params=pltpu.CompilerParams(collective_id=collective_id, has_side_effects=True),
    )(x)


def pair_gather_kernel(x_ref, o_ref, held, sems_a, sems_b, sems_c, sems_d):
    n = held.shape[0]
    chips = n // 2
    s = lax.axis_index("site")
    k = lax.axis_index("branch")
    core = s % 2
    chip = s // 2
    partner = s - core + (1 - core)
    barrier = pltpu.get_barrier_semaphore()
    pl.semaphore_signal(barrier, inc=1, device_id=(partner, k), device_id_type=MESH_ID)

    def greet(d, carry):
        peer = 2 * lax.rem(chip + d, chips) + core
        pl.semaphore_signal(barrier, inc=1, device_id=(peer, k), device_id_type=MESH_ID)
        return carry

    lax.fori_loop(1, chips, greet, 0)
    pl.semaphore_wait(barrier, chips)
    held[s] = x_ref[...]

    def to_chip(d):
        c = lax.rem(chip + d, chips)
        return pltpu.make_async_remote_copy(
            src_ref=x_ref,
            dst_ref=held.at[s],
            send_sem=sems_a.at[c],
            recv_sem=sems_b.at[chip],
            device_id=(2 * c + core, k),
            device_id_type=MESH_ID,
        )

    def first_send(d, carry):
        to_chip(d).start()
        return carry

    lax.fori_loop(1, chips, first_send, 0)

    def to_partner(c):
        return pltpu.make_async_remote_copy(
            src_ref=held.at[2 * c + core],
            dst_ref=held.at[2 * c + core],
            send_sem=sems_c.at[c],
            recv_sem=sems_d.at[c],
            device_id=(partner, k),
            device_id_type=MESH_ID,
        )

    own = pltpu.make_async_remote_copy(
        src_ref=x_ref,
        dst_ref=held.at[s],
        send_sem=sems_c.at[chip],
        recv_sem=sems_d.at[chip],
        device_id=(partner, k),
        device_id_type=MESH_ID,
    )
    own.start()

    def relay(d, carry):
        c = lax.rem(chip + chips - d, chips)
        pltpu.make_async_remote_copy(
            src_ref=held.at[2 * c + core],
            dst_ref=held.at[2 * c + core],
            send_sem=sems_a.at[c],
            recv_sem=sems_b.at[c],
            device_id=(2 * c + core, k),
            device_id_type=MESH_ID,
        ).wait_recv()
        to_partner(c).start()
        return carry

    lax.fori_loop(1, chips, relay, 0)

    def second_recv(c, carry):
        pltpu.make_async_remote_copy(
            src_ref=held.at[2 * c + 1 - core],
            dst_ref=held.at[2 * c + 1 - core],
            send_sem=sems_c.at[c],
            recv_sem=sems_d.at[c],
            device_id=(partner, k),
            device_id_type=MESH_ID,
        ).wait_recv()
        return carry

    lax.fori_loop(0, chips, second_recv, 0)

    def first_sent(d, carry):
        to_chip(d).wait_send()
        return carry

    lax.fori_loop(1, chips, first_sent, 0)
    own.wait_send()

    def second_sent(d, carry):
        to_partner(lax.rem(chip + d, chips)).wait_send()
        return carry

    lax.fori_loop(1, chips, second_sent, 0)
    per = o_ref.shape[0] // n
    width = o_ref.shape[2]

    def unpack(p, carry):
        for q in range(per):
            o_ref[per * p + q] = held[p, :, q * width : (q + 1) * width]
        return carry

    lax.fori_loop(0, n, unpack, 0)


def pair_gather(x, n, collective_id):
    per = x.shape[1] // x.shape[0]
    return pl.pallas_call(
        pair_gather_kernel,
        out_shape=jax.ShapeDtypeStruct((n * per, x.shape[0], x.shape[0]), jnp.float32),
        in_specs=[pl.BlockSpec(memory_space=pltpu.VMEM)],
        out_specs=pl.BlockSpec(memory_space=pltpu.VMEM),
        scratch_shapes=[
            pltpu.VMEM((n,) + x.shape, jnp.float32),
            pltpu.SemaphoreType.DMA((n // 2,)),
            pltpu.SemaphoreType.DMA((n // 2,)),
            pltpu.SemaphoreType.DMA((n // 2,)),
            pltpu.SemaphoreType.DMA((n // 2,)),
        ],
        compiler_params=pltpu.CompilerParams(collective_id=collective_id, has_side_effects=True),
    )(x)


def body(
    states, gap_mask, weights, leaf_order, exchanges, codon_freq, omega_ratio, lengths, classes
):
    site_count = lax.axis_size("site")
    site_pos = lax.axis_index("site")
    subtree = lax.axis_index("branch")
    site_span = states.shape[1]
    total_sites = site_span * site_count
    total_taxa = LEAF_DEV * lax.axis_size("branch")
    rate_matrix, stationary = build_rates(exchanges, codon_freq, omega_ratio)
    slot_len = jnp.concatenate([lengths, jnp.zeros((1,), lengths.dtype)])
    slot_cls = jnp.concatenate([classes, jnp.zeros((1,), jnp.int32)])
    class_pick = (slot_cls[:, None] == jnp.arange(CLASSES, dtype=jnp.int32)[None, :]).astype(
        jnp.float32
    )
    slot_rates = jnp.einsum("bc,cij->bij", class_pick, rate_matrix, precision=lax.Precision.HIGH)
    scaled = slot_rates * slot_len[:, None, None]
    per_dev = SLOTS // site_count
    own_start = site_pos * per_dev
    own_scaled = lax.dynamic_slice_in_dim(scaled, own_start, per_dev, 0)
    own_pull = None
    own_probs, own_pull = jax.vjp(expm_taylor, own_scaled)
    packed_probs = own_probs.transpose(1, 0, 2).reshape(own_probs.shape[1], -1)
    probs = pair_gather(packed_probs, site_count, 1)
    taxon_rows = lax.dynamic_slice_in_dim(leaf_order, subtree * LEAF_DEV, LEAF_DEV, 0)
    leaves = leaf_partials(
        jnp.take(states, taxon_rows, axis=0), jnp.take(gap_mask, taxon_rows, axis=0)
    )
    levels, messages, logscale = up_pass(probs, leaves)
    top_pack = jnp.concatenate([messages[-1][0], logscale[None, :]], axis=0)
    top_all = lax.all_gather(top_pack, "branch", axis=0, tiled=False)
    top_messages, top_logs = top_all[:, :64, :], top_all[:, 64, :]
    site_ll, above_all = root_terms(stationary, top_messages, top_logs)
    site_weight = weights.astype(jnp.float32)
    loglik_part = jnp.sum(site_weight * site_ll)
    above_top = lax.dynamic_slice_in_dim(above_all, subtree, 1, 0)
    a_list = down_pass(probs, levels, messages, above_top)
    weighted = weigh(a_list, messages, site_weight, total_sites)
    level_counts = [
        jnp.einsum("bis,bjs->bij", vector, partial_value, precision=lax.Precision.HIGH)
        for vector, partial_value in zip(weighted, levels)
    ]
    spare = site_count * per_dev - sum(c.shape[0] for c in level_counts)
    part_counts = jnp.concatenate(level_counts + [jnp.zeros((spare, 64, 64), jnp.float32)], axis=0)
    own_counts = pair_scatter(part_counts, site_count, 2)
    d_scaled = own_pull(own_counts)[0]
    use_rates = lax.dynamic_slice_in_dim(slot_rates, own_start, per_dev, 0)
    use_len = lax.dynamic_slice_in_dim(slot_len, own_start, per_dev, 0)
    use_pick = lax.dynamic_slice_in_dim(class_pick, own_start, per_dev, 0)
    d_length = jnp.sum(d_scaled * use_rates, axis=(1, 2))
    d_rates = jnp.einsum(
        "bc,bij->cij", use_pick, d_scaled * use_len[:, None, None], precision=lax.Precision.HIGH
    )
    unused_rates, pull_rates = jax.vjp(
        lambda table, ratio: build_rates(table, codon_freq, ratio)[0], exchanges, omega_ratio
    )
    d_exch, d_omega = pull_rates(d_rates)
    n_branch = lax.axis_size("branch")
    length_slab = jnp.zeros((n_branch, SLOTS), jnp.float32)
    length_slab = lax.dynamic_update_slice(length_slab, d_length[None, :], (subtree, own_start))
    loglik_keep = jnp.where(subtree == 0, loglik_part, jnp.float32(0.0))
    packed = jnp.concatenate(
        [d_exch.reshape(-1), d_omega, length_slab.reshape(-1), loglik_keep[None]]
    )
    rows = -(-packed.shape[0] // (8 * 128)) * 8
    packed = jnp.pad(packed, (0, rows * 128 - packed.shape[0])).reshape(rows, 128)
    summed = allreduce_all(packed, site_count, n_branch).reshape(-1)
    grad_exch = summed[: 64 * 64].reshape(64, 64)
    grad_omega = summed[64 * 64 : 64 * 64 + CLASSES]
    length_all = summed[64 * 64 + CLASSES : 64 * 64 + CLASSES + n_branch * SLOTS].reshape(n_branch, SLOTS)
    log_total = summed[64 * 64 + CLASSES + n_branch * SLOTS]
    loglik = log_total / total_sites / total_taxa
    length_out = lax.dynamic_index_in_dim(length_all, subtree, 0, keepdims=False)[:EDGES]
    return (grad_exch, grad_omega, length_out, loglik)


def solution(mesh):
    return jax.shard_map(
        body,
        mesh=mesh,
        in_specs=(
            P(None, "site"),
            P(None, "site"),
            P("site"),
            P(),
            P(),
            P(),
            P(),
            P("branch"),
            P("branch"),
        ),
        out_specs=(P(), P(), P("branch"), P()),
        check_vma=False,
    )
```

```python
import jax
import jax.numpy as jnp
import numpy as np
from jax import lax
from jax.sharding import PartitionSpec as P
from jax.experimental import pallas as pl
from jax.experimental.pallas import tpu as pltpu
import functools

MESH_ID = pl.DeviceIdType.MESH

LEVELS = 6
LEAF_DEV = 64
EDGES = 127
SLOTS = 128
CLASSES = 8


CODE_TABLE = "FFLLSSSSYYXXCCXWLLLLPPPPHHQQRRRRIIIMTTTTNNKKSSRRVVVVAAAADDEEGGGG"


def codon_tables():
    amino_acid = np.array(list(CODE_TABLE))
    codon_index = np.arange(64)
    digits = np.stack([codon_index // 16, codon_index // 4 % 4, codon_index % 4], 1)
    differ = (digits[:, None, :] != digits[None, :, :]).sum(-1)
    is_sense = amino_acid != "X"
    single = (differ == 1) & is_sense[:, None] & is_sense[None, :]
    nonsyn = single & (amino_acid[:, None] != amino_acid[None, :])
    return (is_sense.astype(np.float32), single.astype(np.float32), nonsyn.astype(np.float32))


def build_rates(exchanges, codon_freq, omega_ratio):
    is_sense, single, nonsyn = codon_tables()
    stationary = codon_freq * is_sense / jnp.sum(codon_freq * is_sense)
    symmetric = 0.5 * (exchanges + exchanges.T)
    factor = 1.0 + nonsyn[None, :, :] * (omega_ratio[:, None, None] - 1.0)
    off_diag = symmetric[None, :, :] * stationary[None, None, :] * factor * single[None, :, :]
    row_total = jnp.sum(off_diag, axis=2)
    mean_rate = jnp.sum(stationary[None, :] * row_total, axis=1)
    identity = jnp.eye(64, dtype=exchanges.dtype)
    rate_matrix = (off_diag - row_total[:, :, None] * identity[None]) / mean_rate[:, None, None]
    return (rate_matrix, stationary)


def product(left, right):
    return jnp.einsum("bij,bjk->bik", left, right, precision=lax.Precision.HIGH)


def expm_taylor(scaled):
    reduced = scaled / 16.0
    identity = jnp.eye(64, dtype=scaled.dtype)
    series = jnp.broadcast_to(identity, scaled.shape)
    for degree in range(8, 0, -1):
        series = identity + product(reduced, series) / degree
    for square_step in range(4):
        series = product(series, series)
    return series


def forward(probs, vectors):
    return jnp.einsum("bij,bjs->bis", probs, vectors, precision=lax.Precision.HIGH)


def carried(probs, vectors):
    return jnp.einsum("bji,bjs->bis", probs, vectors, precision=lax.Precision.HIGH)


def leaf_partials(leaf_states, gap_rows):
    codon_axis = jnp.arange(64, dtype=jnp.int32)
    indicator = (leaf_states[:, None, :] == codon_axis[None, :, None]).astype(jnp.float32)
    return jnp.where(gap_rows[:, None, :] > 0, jnp.float32(1.0), indicator)


def up_pass(probs, leaves):
    levels = [leaves]
    messages = []
    logscale = jnp.zeros(leaves.shape[2:], jnp.float32)
    current = leaves
    for height in range(LEVELS):
        amount = current.shape[0]
        offset = 2 * LEAF_DEV - 2 * amount
        message = forward(probs[offset : offset + amount], current)
        messages.append(message)
        raw_parent = message[0::2] * message[1::2]
        scaling = jnp.sum(raw_parent, axis=1)
        current = raw_parent / scaling[:, None, :]
        logscale = logscale + jnp.sum(jnp.log(scaling), axis=0)
        levels.append(current)
    messages.append(forward(probs[EDGES - 1 : EDGES], current))
    return (levels, messages, logscale)


def root_terms(stationary, top_messages, top_logs):
    members = top_messages.shape[0]
    joint = stationary[:, None] * top_messages[0]
    for member in range(1, members):
        joint = joint * top_messages[member]
    site_ll = jnp.log(jnp.sum(joint, axis=0)) + jnp.sum(top_logs, axis=0)
    above_list = []
    for member in range(members):
        vector = jnp.broadcast_to(stationary[:, None], top_messages.shape[1:])
        for other in range(members):
            if other != member:
                vector = vector * top_messages[other]
        above_list.append(vector)
    return (site_ll, jnp.stack(above_list))


def down_pass(probs, levels, messages, above_top):
    a_list = [above_top]
    current = above_top
    for height in range(LEVELS, 0, -1):
        amount = levels[height].shape[0]
        offset = 2 * LEAF_DEV - 2 * amount
        down_part = carried(probs[offset : offset + amount], current)
        down_part = down_part / jnp.sum(down_part, axis=1, keepdims=True)
        message = messages[height - 1]
        pairs = message.reshape((amount, 2) + message.shape[1:])
        current = (down_part[:, None] * pairs[:, ::-1]).reshape(message.shape)
        a_list.append(current)
    return a_list[::-1]


def weigh(a_list, messages, site_weight, total_sites):
    weighted = []
    for vector, message in zip(a_list, messages):
        likelihood = jnp.sum(vector * message, axis=1)
        weighted.append(vector * (site_weight / (likelihood * total_sites))[:, None, :])
    return weighted


def sum_groups(n_site, n_branch):
    s = lax.axis_index("site")
    k = lax.axis_index("branch")
    core = s % 2
    plane = s // 2
    return [
        (2, core, lambda c: (s - core + c, k)),
        (n_branch, k, lambda c: (s, c)),
        (n_site // 2, plane, lambda c: (2 * c + core, k)),
    ]


def allreduce_kernel(n_site, n_branch, x_ref, o_ref, held, send_sems, recv_sems):
    stages = sum_groups(n_site, n_branch)
    barrier = pltpu.get_barrier_semaphore()
    count = 0
    for size, mine, where in stages:
        for d in range(1, size):
            other = lax.rem(mine + d, size)
            pl.semaphore_signal(barrier, inc=1, device_id=where(other), device_id_type=MESH_ID)
            count += 1
    pl.semaphore_wait(barrier, count)
    total = x_ref[...]
    for st, (size, mine, where) in enumerate(stages):
        held[st, mine] = total
        sends = []
        for d in range(1, size):
            other = lax.rem(mine + d, size)
            copy = pltpu.make_async_remote_copy(
                src_ref=held.at[st, mine],
                dst_ref=held.at[st, mine],
                send_sem=send_sems.at[st, other],
                recv_sem=recv_sems.at[st, mine],
                device_id=where(other),
                device_id_type=MESH_ID,
            )
            copy.start()
            sends.append(copy)
        for d in range(1, size):
            other = lax.rem(mine + d, size)
            incoming = pltpu.make_async_remote_copy(
                src_ref=held.at[st, other],
                dst_ref=held.at[st, other],
                send_sem=send_sems.at[st, other],
                recv_sem=recv_sems.at[st, other],
                device_id=where(other),
                device_id_type=MESH_ID,
            )
            incoming.wait_recv()
        for copy in sends:
            copy.wait_send()
        total = held[st, 0]
        for c in range(1, size):
            total = total + held[st, c]
    o_ref[...] = total


def allreduce_all(x, n_site, n_branch):
    rows = x.shape[0]
    return pl.pallas_call(
        functools.partial(allreduce_kernel, n_site, n_branch),
        out_shape=jax.ShapeDtypeStruct(x.shape, jnp.float32),
        in_specs=[pl.BlockSpec(memory_space=pltpu.VMEM)],
        out_specs=pl.BlockSpec(memory_space=pltpu.VMEM),
        scratch_shapes=[
            pltpu.VMEM((3, n_site // 2, rows, 128), jnp.float32),
            pltpu.SemaphoreType.DMA((3, n_site // 2)),
            pltpu.SemaphoreType.DMA((3, n_site // 2)),
        ],
        compiler_params=pltpu.CompilerParams(collective_id=0, has_side_effects=True),
    )(x)


def exchange_kernel(axis, gather, x_ref, o_ref, held, send_sems, recv_sems):
    n = held.shape[0]
    me = lax.axis_index(axis)
    other_axis = "branch" if axis == "site" else "site"
    fixed = lax.axis_index(other_axis)

    def device(p):
        return (p, fixed) if axis == "site" else (fixed, p)

    barrier = pltpu.get_barrier_semaphore()

    def greet(d, carry):
        pl.semaphore_signal(
            barrier, inc=1, device_id=device(lax.rem(me + d, n)), device_id_type=MESH_ID
        )
        return carry

    lax.fori_loop(1, n, greet, 0)
    pl.semaphore_wait(barrier, n - 1)
    if gather:
        held[me] = x_ref[...]
    else:
        held[me] = x_ref[me]

    def outgoing(d):
        p = lax.rem(me + d, n)
        return pltpu.make_async_remote_copy(
            src_ref=x_ref if gather else x_ref.at[p],
            dst_ref=held.at[me],
            send_sem=send_sems.at[p],
            recv_sem=recv_sems.at[me],
            device_id=device(p),
            device_id_type=MESH_ID,
        )

    def send(d, carry):
        outgoing(d).start()
        return carry

    lax.fori_loop(1, n, send, 0)

    def receive(d, carry):
        p = lax.rem(me + n - d, n)
        pltpu.make_async_remote_copy(
            src_ref=held.at[p],
            dst_ref=held.at[p],
            send_sem=send_sems.at[p],
            recv_sem=recv_sems.at[p],
            device_id=device(p),
            device_id_type=MESH_ID,
        ).wait_recv()
        return carry

    lax.fori_loop(1, n, receive, 0)

    def sent(d, carry):
        outgoing(d).wait_send()
        return carry

    lax.fori_loop(1, n, sent, 0)
    if gather:
        o_ref[...] = held[...]
    else:
        o_ref[...] = lax.fori_loop(1, n, lambda j, acc: acc + held[j], held[0])


def exchange(x, axis, n, gather, collective_id):
    chunk = x.shape if gather else x.shape[1:]
    out_shape = (n,) + chunk if gather else chunk
    return pl.pallas_call(
        functools.partial(exchange_kernel, axis, gather),
        out_shape=jax.ShapeDtypeStruct(out_shape, jnp.float32),
        in_specs=[pl.BlockSpec(memory_space=pltpu.VMEM)],
        out_specs=pl.BlockSpec(memory_space=pltpu.VMEM),
        scratch_shapes=[
            pltpu.VMEM((n,) + chunk, jnp.float32),
            pltpu.SemaphoreType.DMA((n,)),
            pltpu.SemaphoreType.DMA((n,)),
        ],
        compiler_params=pltpu.CompilerParams(collective_id=collective_id, has_side_effects=True),
    )(x)


def pair_scatter_kernel(x_ref, o_ref, packed, pair_buf, pair_sum, held, sems_a, sems_b, sems_c, sems_d):
    n = packed.shape[0]
    per = o_ref.shape[0]
    width = o_ref.shape[2]

    def pack(p, carry):
        for q in range(per):
            packed[p, :, q * width : (q + 1) * width] = x_ref[per * p + q]
        return carry

    lax.fori_loop(0, n, pack, 0)
    chips = n // 2
    s = lax.axis_index("site")
    k = lax.axis_index("branch")
    core = s % 2
    chip = s // 2
    partner = s - core + (1 - core)
    barrier = pltpu.get_barrier_semaphore()
    pl.semaphore_signal(barrier, inc=1, device_id=(partner, k), device_id_type=MESH_ID)

    def greet(d, carry):
        peer = 2 * lax.rem(chip + d, chips) + core
        pl.semaphore_signal(barrier, inc=1, device_id=(peer, k), device_id_type=MESH_ID)
        return carry

    lax.fori_loop(1, chips, greet, 0)
    pl.semaphore_wait(barrier, chips)

    def to_partner(m):
        return pltpu.make_async_remote_copy(
            src_ref=packed.at[2 * m + 1 - core],
            dst_ref=pair_buf.at[m],
            send_sem=sems_a.at[m],
            recv_sem=sems_b.at[m],
            device_id=(partner, k),
            device_id_type=MESH_ID,
        )

    def first_send(m, carry):
        to_partner(m).start()
        return carry

    lax.fori_loop(0, chips, first_send, 0)

    def to_chip(c):
        return pltpu.make_async_remote_copy(
            src_ref=pair_sum.at[c],
            dst_ref=held.at[chip],
            send_sem=sems_c.at[c],
            recv_sem=sems_d.at[chip],
            device_id=(2 * c + core, k),
            device_id_type=MESH_ID,
        )

    to_partner(chip).wait_recv()
    pair_sum[chip] = packed[2 * chip + core] + pair_buf[chip]
    held[chip] = pair_sum[chip]

    def add_and_send(d, carry):
        c = lax.rem(chip + d, chips)
        to_partner(c).wait_recv()
        pair_sum[c] = packed[2 * c + core] + pair_buf[c]
        to_chip(c).start()
        return carry

    lax.fori_loop(1, chips, add_and_send, 0)

    def second_recv(d, carry):
        c = lax.rem(chip + chips - d, chips)
        pltpu.make_async_remote_copy(
            src_ref=held.at[c],
            dst_ref=held.at[c],
            send_sem=sems_c.at[c],
            recv_sem=sems_d.at[c],
            device_id=(2 * c + core, k),
            device_id_type=MESH_ID,
        ).wait_recv()
        return carry

    lax.fori_loop(1, chips, second_recv, 0)

    def first_sent(m, carry):
        to_partner(m).wait_send()
        return carry

    lax.fori_loop(0, chips, first_sent, 0)

    def second_sent(d, carry):
        to_chip(lax.rem(chip + d, chips)).wait_send()
        return carry

    lax.fori_loop(1, chips, second_sent, 0)
    total = lax.fori_loop(1, chips, lambda j, acc: acc + held[j], held[0])
    for q in range(per):
        o_ref[q] = total[:, q * width : (q + 1) * width]


def pair_scatter(x, n, collective_id):
    per = x.shape[0] // n
    chunk = (x.shape[1], per * x.shape[2])
    return pl.pallas_call(
        pair_scatter_kernel,
        out_shape=jax.ShapeDtypeStruct((per,) + x.shape[1:], jnp.float32),
        in_specs=[pl.BlockSpec(memory_space=pltpu.VMEM)],
        out_specs=pl.BlockSpec(memory_space=pltpu.VMEM),
        scratch_shapes=[
            pltpu.VMEM((n,) + chunk, jnp.float32),
            pltpu.VMEM((n // 2,) + chunk, jnp.float32),
            pltpu.VMEM((n // 2,) + chunk, jnp.float32),
            pltpu.VMEM((n // 2,) + chunk, jnp.float32),
            pltpu.SemaphoreType.DMA((n // 2,)),
            pltpu.SemaphoreType.DMA((n // 2,)),
            pltpu.SemaphoreType.DMA((n // 2,)),
            pltpu.SemaphoreType.DMA((n // 2,)),
        ],
        compiler_params=pltpu.CompilerParams(collective_id=collective_id, has_side_effects=True),
    )(x)


def pair_gather_kernel(x_ref, o_ref, held, sems_a, sems_b, sems_c, sems_d):
    n = held.shape[0]
    chips = n // 2
    s = lax.axis_index("site")
    k = lax.axis_index("branch")
    core = s % 2
    chip = s // 2
    partner = s - core + (1 - core)
    barrier = pltpu.get_barrier_semaphore()
    pl.semaphore_signal(barrier, inc=1, device_id=(partner, k), device_id_type=MESH_ID)

    def greet(d, carry):
        peer = 2 * lax.rem(chip + d, chips) + core
        pl.semaphore_signal(barrier, inc=1, device_id=(peer, k), device_id_type=MESH_ID)
        return carry

    lax.fori_loop(1, chips, greet, 0)
    pl.semaphore_wait(barrier, chips)
    held[s] = x_ref[...]

    def to_chip(d):
        c = lax.rem(chip + d, chips)
        return pltpu.make_async_remote_copy(
            src_ref=x_ref,
            dst_ref=held.at[s],
            send_sem=sems_a.at[c],
            recv_sem=sems_b.at[chip],
            device_id=(2 * c + core, k),
            device_id_type=MESH_ID,
        )

    def first_send(d, carry):
        to_chip(d).start()
        return carry

    lax.fori_loop(1, chips, first_send, 0)

    def to_partner(c):
        return pltpu.make_async_remote_copy(
            src_ref=held.at[2 * c + core],
            dst_ref=held.at[2 * c + core],
            send_sem=sems_c.at[c],
            recv_sem=sems_d.at[c],
            device_id=(partner, k),
            device_id_type=MESH_ID,
        )

    own = pltpu.make_async_remote_copy(
        src_ref=x_ref,
        dst_ref=held.at[s],
        send_sem=sems_c.at[chip],
        recv_sem=sems_d.at[chip],
        device_id=(partner, k),
        device_id_type=MESH_ID,
    )
    own.start()

    def relay(d, carry):
        c = lax.rem(chip + chips - d, chips)
        pltpu.make_async_remote_copy(
            src_ref=held.at[2 * c + core],
            dst_ref=held.at[2 * c + core],
            send_sem=sems_a.at[c],
            recv_sem=sems_b.at[c],
            device_id=(2 * c + core, k),
            device_id_type=MESH_ID,
        ).wait_recv()
        to_partner(c).start()
        return carry

    lax.fori_loop(1, chips, relay, 0)

    def second_recv(c, carry):
        pltpu.make_async_remote_copy(
            src_ref=held.at[2 * c + 1 - core],
            dst_ref=held.at[2 * c + 1 - core],
            send_sem=sems_c.at[c],
            recv_sem=sems_d.at[c],
            device_id=(partner, k),
            device_id_type=MESH_ID,
        ).wait_recv()
        return carry

    lax.fori_loop(0, chips, second_recv, 0)

    def first_sent(d, carry):
        to_chip(d).wait_send()
        return carry

    lax.fori_loop(1, chips, first_sent, 0)
    own.wait_send()

    def second_sent(d, carry):
        to_partner(lax.rem(chip + d, chips)).wait_send()
        return carry

    lax.fori_loop(1, chips, second_sent, 0)
    per = o_ref.shape[0] // n
    width = o_ref.shape[2]

    def unpack(p, carry):
        for q in range(per):
            o_ref[per * p + q] = held[p, :, q * width : (q + 1) * width]
        return carry

    lax.fori_loop(0, n, unpack, 0)


def pair_gather(x, n, collective_id):
    per = x.shape[1] // x.shape[0]
    return pl.pallas_call(
        pair_gather_kernel,
        out_shape=jax.ShapeDtypeStruct((n * per, x.shape[0], x.shape[0]), jnp.float32),
        in_specs=[pl.BlockSpec(memory_space=pltpu.VMEM)],
        out_specs=pl.BlockSpec(memory_space=pltpu.VMEM),
        scratch_shapes=[
            pltpu.VMEM((n,) + x.shape, jnp.float32),
            pltpu.SemaphoreType.DMA((n // 2,)),
            pltpu.SemaphoreType.DMA((n // 2,)),
            pltpu.SemaphoreType.DMA((n // 2,)),
            pltpu.SemaphoreType.DMA((n // 2,)),
        ],
        compiler_params=pltpu.CompilerParams(collective_id=collective_id, has_side_effects=True),
    )(x)


def body(
    states, gap_mask, weights, leaf_order, exchanges, codon_freq, omega_ratio, lengths, classes
):
    site_count = lax.axis_size("site")
    site_pos = lax.axis_index("site")
    subtree = lax.axis_index("branch")
    site_span = states.shape[1]
    total_sites = site_span * site_count
    total_taxa = LEAF_DEV * lax.axis_size("branch")
    rate_matrix, stationary = build_rates(exchanges, codon_freq, omega_ratio)
    slot_len = jnp.concatenate([lengths, jnp.zeros((1,), lengths.dtype)])
    slot_cls = jnp.concatenate([classes, jnp.zeros((1,), jnp.int32)])
    class_pick = (slot_cls[:, None] == jnp.arange(CLASSES, dtype=jnp.int32)[None, :]).astype(
        jnp.float32
    )
    slot_rates = jnp.einsum("bc,cij->bij", class_pick, rate_matrix, precision=lax.Precision.HIGH)
    scaled = slot_rates * slot_len[:, None, None]
    per_dev = SLOTS // site_count
    own_start = site_pos * per_dev
    own_scaled = lax.dynamic_slice_in_dim(scaled, own_start, per_dev, 0)
    own_pull = None
    own_probs, own_pull = jax.vjp(expm_taylor, own_scaled)
    packed_probs = own_probs.transpose(1, 0, 2).reshape(own_probs.shape[1], -1)
    probs = pair_gather(packed_probs, site_count, 1)
    taxon_rows = lax.dynamic_slice_in_dim(leaf_order, subtree * LEAF_DEV, LEAF_DEV, 0)
    leaves = leaf_partials(
        jnp.take(states, taxon_rows, axis=0), jnp.take(gap_mask, taxon_rows, axis=0)
    )
    levels, messages, logscale = up_pass(probs, leaves)
    top_pack = jnp.concatenate([messages[-1][0], logscale[None, :]], axis=0)
    top_all = lax.all_gather(top_pack, "branch", axis=0, tiled=False)
    top_messages, top_logs = top_all[:, :64, :], top_all[:, 64, :]
    site_ll, above_all = root_terms(stationary, top_messages, top_logs)
    site_weight = weights.astype(jnp.float32)
    loglik_part = jnp.sum(site_weight * site_ll)
    above_top = lax.dynamic_slice_in_dim(above_all, subtree, 1, 0)
    a_list = down_pass(probs, levels, messages, above_top)
    weighted = weigh(a_list, messages, site_weight, total_sites)
    level_counts = [
        jnp.einsum("bis,bjs->bij", vector, partial_value, precision=lax.Precision.HIGH)
        for vector, partial_value in zip(weighted, levels)
    ]
    spare = site_count * per_dev - sum(c.shape[0] for c in level_counts)
    part_counts = jnp.concatenate(level_counts + [jnp.zeros((spare, 64, 64), jnp.float32)], axis=0)
    own_counts = pair_scatter(part_counts, site_count, 2)
    d_scaled = own_pull(own_counts)[0]
    use_rates = lax.dynamic_slice_in_dim(slot_rates, own_start, per_dev, 0)
    use_len = lax.dynamic_slice_in_dim(slot_len, own_start, per_dev, 0)
    use_pick = lax.dynamic_slice_in_dim(class_pick, own_start, per_dev, 0)
    d_length = jnp.sum(d_scaled * use_rates, axis=(1, 2))
    d_rates = jnp.einsum(
        "bc,bij->cij", use_pick, d_scaled * use_len[:, None, None], precision=lax.Precision.HIGH
    )
    unused_rates, pull_rates = jax.vjp(
        lambda table, ratio: build_rates(table, codon_freq, ratio)[0], exchanges, omega_ratio
    )
    d_exch, d_omega = pull_rates(d_rates)
    n_branch = lax.axis_size("branch")
    length_slab = jnp.zeros((n_branch, SLOTS), jnp.float32)
    length_slab = lax.dynamic_update_slice(length_slab, d_length[None, :], (subtree, own_start))
    loglik_keep = jnp.where(subtree == 0, loglik_part, jnp.float32(0.0))
    packed = jnp.concatenate(
        [d_exch.reshape(-1), d_omega, length_slab.reshape(-1), loglik_keep[None]]
    )
    rows = -(-packed.shape[0] // (8 * 128)) * 8
    packed = jnp.pad(packed, (0, rows * 128 - packed.shape[0])).reshape(rows, 128)
    summed = allreduce_all(packed, site_count, n_branch).reshape(-1)
    grad_exch = summed[: 64 * 64].reshape(64, 64)
    grad_omega = summed[64 * 64 : 64 * 64 + CLASSES]
    length_all = summed[64 * 64 + CLASSES : 64 * 64 + CLASSES + n_branch * SLOTS].reshape(n_branch, SLOTS)
    log_total = summed[64 * 64 + CLASSES + n_branch * SLOTS]
    loglik = log_total / total_sites / total_taxa
    length_out = lax.dynamic_index_in_dim(length_all, subtree, 0, keepdims=False)[:EDGES]
    return (grad_exch, grad_omega, length_out, loglik)


def solution(mesh):
    return jax.shard_map(
        body,
        mesh=mesh,
        in_specs=(
            P(None, "site"),
            P(None, "site"),
            P("site"),
            P(),
            P(),
            P(),
            P(),
            P("branch"),
            P("branch"),
        ),
        out_specs=(P(), P(), P("branch"), P()),
        check_vma=False,
    )
```

```python
import jax
import jax.numpy as jnp
import numpy as np
from jax import lax
from jax.sharding import PartitionSpec as P
from jax.experimental import pallas as pl
from jax.experimental.pallas import tpu as pltpu
import functools

MESH_ID = pl.DeviceIdType.MESH

LEVELS = 6
LEAF_DEV = 64
EDGES = 127
SLOTS = 128
CLASSES = 8


CODE_TABLE = "FFLLSSSSYYXXCCXWLLLLPPPPHHQQRRRRIIIMTTTTNNKKSSRRVVVVAAAADDEEGGGG"


def codon_tables():
    amino_acid = np.array(list(CODE_TABLE))
    codon_index = np.arange(64)
    digits = np.stack([codon_index // 16, codon_index // 4 % 4, codon_index % 4], 1)
    differ = (digits[:, None, :] != digits[None, :, :]).sum(-1)
    is_sense = amino_acid != "X"
    single = (differ == 1) & is_sense[:, None] & is_sense[None, :]
    nonsyn = single & (amino_acid[:, None] != amino_acid[None, :])
    return (is_sense.astype(np.float32), single.astype(np.float32), nonsyn.astype(np.float32))


def build_rates(exchanges, codon_freq, omega_ratio):
    is_sense, single, nonsyn = codon_tables()
    stationary = codon_freq * is_sense / jnp.sum(codon_freq * is_sense)
    symmetric = 0.5 * (exchanges + exchanges.T)
    factor = 1.0 + nonsyn[None, :, :] * (omega_ratio[:, None, None] - 1.0)
    off_diag = symmetric[None, :, :] * stationary[None, None, :] * factor * single[None, :, :]
    row_total = jnp.sum(off_diag, axis=2)
    mean_rate = jnp.sum(stationary[None, :] * row_total, axis=1)
    identity = jnp.eye(64, dtype=exchanges.dtype)
    rate_matrix = (off_diag - row_total[:, :, None] * identity[None]) / mean_rate[:, None, None]
    return (rate_matrix, stationary)


def product(left, right):
    return jnp.einsum("bij,bjk->bik", left, right, precision=lax.Precision.HIGH)


def expm_taylor(scaled):
    reduced = scaled / 16.0
    identity = jnp.eye(64, dtype=scaled.dtype)
    series = jnp.broadcast_to(identity, scaled.shape)
    for degree in range(8, 0, -1):
        series = identity + product(reduced, series) / degree
    for square_step in range(4):
        series = product(series, series)
    return series


def forward(probs, vectors):
    return jnp.einsum("bij,bjs->bis", probs, vectors, precision=lax.Precision.HIGH)


def carried(probs, vectors):
    return jnp.einsum("bji,bjs->bis", probs, vectors, precision=lax.Precision.HIGH)


def leaf_partials(leaf_states, gap_rows):
    codon_axis = jnp.arange(64, dtype=jnp.int32)
    indicator = (leaf_states[:, None, :] == codon_axis[None, :, None]).astype(jnp.float32)
    return jnp.where(gap_rows[:, None, :] > 0, jnp.float32(1.0), indicator)


def up_pass(probs, leaves):
    levels = [leaves]
    messages = []
    logscale = jnp.zeros(leaves.shape[2:], jnp.float32)
    current = leaves
    for height in range(LEVELS):
        amount = current.shape[0]
        offset = 2 * LEAF_DEV - 2 * amount
        message = forward(probs[offset : offset + amount], current)
        messages.append(message)
        halves = message.reshape((amount // 2, 2) + message.shape[1:])
        raw_parent = halves[:, 0] * halves[:, 1]
        scaling = jnp.sum(raw_parent, axis=1)
        current = raw_parent / scaling[:, None, :]
        logscale = logscale + jnp.sum(jnp.log(scaling), axis=0)
        levels.append(current)
    messages.append(forward(probs[EDGES - 1 : EDGES], current))
    return (levels, messages, logscale)


def root_terms(stationary, top_messages, top_logs):
    members = top_messages.shape[0]
    joint = stationary[:, None] * top_messages[0]
    for member in range(1, members):
        joint = joint * top_messages[member]
    site_ll = jnp.log(jnp.sum(joint, axis=0)) + jnp.sum(top_logs, axis=0)
    above_list = []
    for member in range(members):
        vector = jnp.broadcast_to(stationary[:, None], top_messages.shape[1:])
        for other in range(members):
            if other != member:
                vector = vector * top_messages[other]
        above_list.append(vector)
    return (site_ll, jnp.stack(above_list))


def down_pass(probs, levels, messages, above_top):
    a_list = [above_top]
    current = above_top
    for height in range(LEVELS, 0, -1):
        amount = levels[height].shape[0]
        offset = 2 * LEAF_DEV - 2 * amount
        down_part = carried(probs[offset : offset + amount], current)
        down_part = down_part / jnp.sum(down_part, axis=1, keepdims=True)
        message = messages[height - 1]
        pairs = message.reshape((amount, 2) + message.shape[1:])
        current = (down_part[:, None] * pairs[:, ::-1]).reshape(message.shape)
        a_list.append(current)
    return a_list[::-1]


def weigh(a_list, messages, site_weight, total_sites):
    weighted = []
    for vector, message in zip(a_list, messages):
        likelihood = jnp.sum(vector * message, axis=1)
        weighted.append(vector * (site_weight / (likelihood * total_sites))[:, None, :])
    return weighted


def sum_groups(n_site, n_branch):
    s = lax.axis_index("site")
    k = lax.axis_index("branch")
    core = s % 2
    plane = s // 2
    return [
        (2, core, lambda c: (s - core + c, k)),
        (n_branch, k, lambda c: (s, c)),
        (n_site // 2, plane, lambda c: (2 * c + core, k)),
    ]


def allreduce_kernel(n_site, n_branch, x_ref, o_ref, held, send_sems, recv_sems):
    stages = sum_groups(n_site, n_branch)
    barrier = pltpu.get_barrier_semaphore()
    count = 0
    for size, mine, where in stages:
        for d in range(1, size):
            other = lax.rem(mine + d, size)
            pl.semaphore_signal(barrier, inc=1, device_id=where(other), device_id_type=MESH_ID)
            count += 1
    pl.semaphore_wait(barrier, count)
    total = x_ref[...]
    for st, (size, mine, where) in enumerate(stages):
        held[st, mine] = total
        sends = []
        for d in range(1, size):
            other = lax.rem(mine + d, size)
            copy = pltpu.make_async_remote_copy(
                src_ref=held.at[st, mine],
                dst_ref=held.at[st, mine],
                send_sem=send_sems.at[st, other],
                recv_sem=recv_sems.at[st, mine],
                device_id=where(other),
                device_id_type=MESH_ID,
            )
            copy.start()
            sends.append(copy)
        for d in range(1, size):
            other = lax.rem(mine + d, size)
            incoming = pltpu.make_async_remote_copy(
                src_ref=held.at[st, other],
                dst_ref=held.at[st, other],
                send_sem=send_sems.at[st, other],
                recv_sem=recv_sems.at[st, other],
                device_id=where(other),
                device_id_type=MESH_ID,
            )
            incoming.wait_recv()
        for copy in sends:
            copy.wait_send()
        total = held[st, 0]
        for c in range(1, size):
            total = total + held[st, c]
    o_ref[...] = total


def allreduce_all(x, n_site, n_branch):
    rows = x.shape[0]
    return pl.pallas_call(
        functools.partial(allreduce_kernel, n_site, n_branch),
        out_shape=jax.ShapeDtypeStruct(x.shape, jnp.float32),
        in_specs=[pl.BlockSpec(memory_space=pltpu.VMEM)],
        out_specs=pl.BlockSpec(memory_space=pltpu.VMEM),
        scratch_shapes=[
            pltpu.VMEM((3, n_site // 2, rows, 128), jnp.float32),
            pltpu.SemaphoreType.DMA((3, n_site // 2)),
            pltpu.SemaphoreType.DMA((3, n_site // 2)),
        ],
        compiler_params=pltpu.CompilerParams(collective_id=0, has_side_effects=True),
    )(x)


def exchange_kernel(axis, gather, x_ref, o_ref, held, send_sems, recv_sems):
    n = held.shape[0]
    me = lax.axis_index(axis)
    other_axis = "branch" if axis == "site" else "site"
    fixed = lax.axis_index(other_axis)

    def device(p):
        return (p, fixed) if axis == "site" else (fixed, p)

    barrier = pltpu.get_barrier_semaphore()

    def greet(d, carry):
        pl.semaphore_signal(
            barrier, inc=1, device_id=device(lax.rem(me + d, n)), device_id_type=MESH_ID
        )
        return carry

    lax.fori_loop(1, n, greet, 0)
    pl.semaphore_wait(barrier, n - 1)
    if gather:
        held[me] = x_ref[...]
    else:
        held[me] = x_ref[me]

    def outgoing(d):
        p = lax.rem(me + d, n)
        return pltpu.make_async_remote_copy(
            src_ref=x_ref if gather else x_ref.at[p],
            dst_ref=held.at[me],
            send_sem=send_sems.at[p],
            recv_sem=recv_sems.at[me],
            device_id=device(p),
            device_id_type=MESH_ID,
        )

    def send(d, carry):
        outgoing(d).start()
        return carry

    lax.fori_loop(1, n, send, 0)

    def receive(d, carry):
        p = lax.rem(me + n - d, n)
        pltpu.make_async_remote_copy(
            src_ref=held.at[p],
            dst_ref=held.at[p],
            send_sem=send_sems.at[p],
            recv_sem=recv_sems.at[p],
            device_id=device(p),
            device_id_type=MESH_ID,
        ).wait_recv()
        return carry

    lax.fori_loop(1, n, receive, 0)

    def sent(d, carry):
        outgoing(d).wait_send()
        return carry

    lax.fori_loop(1, n, sent, 0)
    if gather:
        o_ref[...] = held[...]
    else:
        o_ref[...] = lax.fori_loop(1, n, lambda j, acc: acc + held[j], held[0])


def exchange(x, axis, n, gather, collective_id):
    chunk = x.shape if gather else x.shape[1:]
    out_shape = (n,) + chunk if gather else chunk
    return pl.pallas_call(
        functools.partial(exchange_kernel, axis, gather),
        out_shape=jax.ShapeDtypeStruct(out_shape, jnp.float32),
        in_specs=[pl.BlockSpec(memory_space=pltpu.VMEM)],
        out_specs=pl.BlockSpec(memory_space=pltpu.VMEM),
        scratch_shapes=[
            pltpu.VMEM((n,) + chunk, jnp.float32),
            pltpu.SemaphoreType.DMA((n,)),
            pltpu.SemaphoreType.DMA((n,)),
        ],
        compiler_params=pltpu.CompilerParams(collective_id=collective_id, has_side_effects=True),
    )(x)


def pair_scatter_kernel(x_ref, o_ref, packed, pair_buf, pair_sum, held, sems_a, sems_b, sems_c, sems_d):
    n = packed.shape[0]
    per = o_ref.shape[0]
    width = o_ref.shape[2]

    def pack(p, carry):
        for q in range(per):
            packed[p, :, q * width : (q + 1) * width] = x_ref[per * p + q]
        return carry

    lax.fori_loop(0, n, pack, 0)
    chips = n // 2
    s = lax.axis_index("site")
    k = lax.axis_index("branch")
    core = s % 2
    chip = s // 2
    partner = s - core + (1 - core)
    barrier = pltpu.get_barrier_semaphore()
    pl.semaphore_signal(barrier, inc=1, device_id=(partner, k), device_id_type=MESH_ID)

    def greet(d, carry):
        peer = 2 * lax.rem(chip + d, chips) + core
        pl.semaphore_signal(barrier, inc=1, device_id=(peer, k), device_id_type=MESH_ID)
        return carry

    lax.fori_loop(1, chips, greet, 0)
    pl.semaphore_wait(barrier, chips)

    def to_partner(m):
        return pltpu.make_async_remote_copy(
            src_ref=packed.at[2 * m + 1 - core],
            dst_ref=pair_buf.at[m],
            send_sem=sems_a.at[m],
            recv_sem=sems_b.at[m],
            device_id=(partner, k),
            device_id_type=MESH_ID,
        )

    def first_send(m, carry):
        to_partner(m).start()
        return carry

    lax.fori_loop(0, chips, first_send, 0)

    def to_chip(c):
        return pltpu.make_async_remote_copy(
            src_ref=pair_sum.at[c],
            dst_ref=held.at[chip],
            send_sem=sems_c.at[c],
            recv_sem=sems_d.at[chip],
            device_id=(2 * c + core, k),
            device_id_type=MESH_ID,
        )

    to_partner(chip).wait_recv()
    pair_sum[chip] = packed[2 * chip + core] + pair_buf[chip]
    held[chip] = pair_sum[chip]

    def add_and_send(d, carry):
        c = lax.rem(chip + d, chips)
        to_partner(c).wait_recv()
        pair_sum[c] = packed[2 * c + core] + pair_buf[c]
        to_chip(c).start()
        return carry

    lax.fori_loop(1, chips, add_and_send, 0)

    def second_recv(d, carry):
        c = lax.rem(chip + chips - d, chips)
        pltpu.make_async_remote_copy(
            src_ref=held.at[c],
            dst_ref=held.at[c],
            send_sem=sems_c.at[c],
            recv_sem=sems_d.at[c],
            device_id=(2 * c + core, k),
            device_id_type=MESH_ID,
        ).wait_recv()
        return carry

    lax.fori_loop(1, chips, second_recv, 0)

    def first_sent(m, carry):
        to_partner(m).wait_send()
        return carry

    lax.fori_loop(0, chips, first_sent, 0)

    def second_sent(d, carry):
        to_chip(lax.rem(chip + d, chips)).wait_send()
        return carry

    lax.fori_loop(1, chips, second_sent, 0)
    total = lax.fori_loop(1, chips, lambda j, acc: acc + held[j], held[0])
    for q in range(per):
        o_ref[q] = total[:, q * width : (q + 1) * width]


def pair_scatter(x, n, collective_id):
    per = x.shape[0] // n
    chunk = (x.shape[1], per * x.shape[2])
    return pl.pallas_call(
        pair_scatter_kernel,
        out_shape=jax.ShapeDtypeStruct((per,) + x.shape[1:], jnp.float32),
        in_specs=[pl.BlockSpec(memory_space=pltpu.VMEM)],
        out_specs=pl.BlockSpec(memory_space=pltpu.VMEM),
        scratch_shapes=[
            pltpu.VMEM((n,) + chunk, jnp.float32),
            pltpu.VMEM((n // 2,) + chunk, jnp.float32),
            pltpu.VMEM((n // 2,) + chunk, jnp.float32),
            pltpu.VMEM((n // 2,) + chunk, jnp.float32),
            pltpu.SemaphoreType.DMA((n // 2,)),
            pltpu.SemaphoreType.DMA((n // 2,)),
            pltpu.SemaphoreType.DMA((n // 2,)),
            pltpu.SemaphoreType.DMA((n // 2,)),
        ],
        compiler_params=pltpu.CompilerParams(collective_id=collective_id, has_side_effects=True),
    )(x)


def pair_gather_kernel(x_ref, o_ref, held, sems_a, sems_b, sems_c, sems_d):
    n = held.shape[0]
    chips = n // 2
    s = lax.axis_index("site")
    k = lax.axis_index("branch")
    core = s % 2
    chip = s // 2
    partner = s - core + (1 - core)
    barrier = pltpu.get_barrier_semaphore()
    pl.semaphore_signal(barrier, inc=1, device_id=(partner, k), device_id_type=MESH_ID)

    def greet(d, carry):
        peer = 2 * lax.rem(chip + d, chips) + core
        pl.semaphore_signal(barrier, inc=1, device_id=(peer, k), device_id_type=MESH_ID)
        return carry

    lax.fori_loop(1, chips, greet, 0)
    pl.semaphore_wait(barrier, chips)
    held[s] = x_ref[...]

    def to_chip(d):
        c = lax.rem(chip + d, chips)
        return pltpu.make_async_remote_copy(
            src_ref=x_ref,
            dst_ref=held.at[s],
            send_sem=sems_a.at[c],
            recv_sem=sems_b.at[chip],
            device_id=(2 * c + core, k),
            device_id_type=MESH_ID,
        )

    def first_send(d, carry):
        to_chip(d).start()
        return carry

    lax.fori_loop(1, chips, first_send, 0)

    def to_partner(c):
        return pltpu.make_async_remote_copy(
            src_ref=held.at[2 * c + core],
            dst_ref=held.at[2 * c + core],
            send_sem=sems_c.at[c],
            recv_sem=sems_d.at[c],
            device_id=(partner, k),
            device_id_type=MESH_ID,
        )

    own = pltpu.make_async_remote_copy(
        src_ref=x_ref,
        dst_ref=held.at[s],
        send_sem=sems_c.at[chip],
        recv_sem=sems_d.at[chip],
        device_id=(partner, k),
        device_id_type=MESH_ID,
    )
    own.start()

    def relay(d, carry):
        c = lax.rem(chip + chips - d, chips)
        pltpu.make_async_remote_copy(
            src_ref=held.at[2 * c + core],
            dst_ref=held.at[2 * c + core],
            send_sem=sems_a.at[c],
            recv_sem=sems_b.at[c],
            device_id=(2 * c + core, k),
            device_id_type=MESH_ID,
        ).wait_recv()
        to_partner(c).start()
        return carry

    lax.fori_loop(1, chips, relay, 0)

    def second_recv(c, carry):
        pltpu.make_async_remote_copy(
            src_ref=held.at[2 * c + 1 - core],
            dst_ref=held.at[2 * c + 1 - core],
            send_sem=sems_c.at[c],
            recv_sem=sems_d.at[c],
            device_id=(partner, k),
            device_id_type=MESH_ID,
        ).wait_recv()
        return carry

    lax.fori_loop(0, chips, second_recv, 0)

    def first_sent(d, carry):
        to_chip(d).wait_send()
        return carry

    lax.fori_loop(1, chips, first_sent, 0)
    own.wait_send()

    def second_sent(d, carry):
        to_partner(lax.rem(chip + d, chips)).wait_send()
        return carry

    lax.fori_loop(1, chips, second_sent, 0)
    per = o_ref.shape[0] // n
    width = o_ref.shape[2]

    def unpack(p, carry):
        for q in range(per):
            o_ref[per * p + q] = held[p, :, q * width : (q + 1) * width]
        return carry

    lax.fori_loop(0, n, unpack, 0)


def pair_gather(x, n, collective_id):
    per = x.shape[1] // x.shape[0]
    return pl.pallas_call(
        pair_gather_kernel,
        out_shape=jax.ShapeDtypeStruct((n * per, x.shape[0], x.shape[0]), jnp.float32),
        in_specs=[pl.BlockSpec(memory_space=pltpu.VMEM)],
        out_specs=pl.BlockSpec(memory_space=pltpu.VMEM),
        scratch_shapes=[
            pltpu.VMEM((n,) + x.shape, jnp.float32),
            pltpu.SemaphoreType.DMA((n // 2,)),
            pltpu.SemaphoreType.DMA((n // 2,)),
            pltpu.SemaphoreType.DMA((n // 2,)),
            pltpu.SemaphoreType.DMA((n // 2,)),
        ],
        compiler_params=pltpu.CompilerParams(collective_id=collective_id, has_side_effects=True),
    )(x)


def body(
    states, gap_mask, weights, leaf_order, exchanges, codon_freq, omega_ratio, lengths, classes
):
    site_count = lax.axis_size("site")
    site_pos = lax.axis_index("site")
    subtree = lax.axis_index("branch")
    site_span = states.shape[1]
    total_sites = site_span * site_count
    total_taxa = LEAF_DEV * lax.axis_size("branch")
    rate_matrix, stationary = build_rates(exchanges, codon_freq, omega_ratio)
    slot_len = jnp.concatenate([lengths, jnp.zeros((1,), lengths.dtype)])
    slot_cls = jnp.concatenate([classes, jnp.zeros((1,), jnp.int32)])
    class_pick = (slot_cls[:, None] == jnp.arange(CLASSES, dtype=jnp.int32)[None, :]).astype(
        jnp.float32
    )
    slot_rates = jnp.einsum("bc,cij->bij", class_pick, rate_matrix, precision=lax.Precision.HIGH)
    scaled = slot_rates * slot_len[:, None, None]
    per_dev = SLOTS // site_count
    own_start = site_pos * per_dev
    own_scaled = lax.dynamic_slice_in_dim(scaled, own_start, per_dev, 0)
    own_pull = None
    own_probs, own_pull = jax.vjp(expm_taylor, own_scaled)
    packed_probs = own_probs.transpose(1, 0, 2).reshape(own_probs.shape[1], -1)
    probs = pair_gather(packed_probs, site_count, 1)
    taxon_rows = lax.dynamic_slice_in_dim(leaf_order, subtree * LEAF_DEV, LEAF_DEV, 0)
    leaves = leaf_partials(
        jnp.take(states, taxon_rows, axis=0), jnp.take(gap_mask, taxon_rows, axis=0)
    )
    levels, messages, logscale = up_pass(probs, leaves)
    top_pack = jnp.concatenate([messages[-1][0], logscale[None, :]], axis=0)
    top_all = lax.all_gather(top_pack, "branch", axis=0, tiled=False)
    top_messages, top_logs = top_all[:, :64, :], top_all[:, 64, :]
    site_ll, above_all = root_terms(stationary, top_messages, top_logs)
    site_weight = weights.astype(jnp.float32)
    loglik_part = jnp.sum(site_weight * site_ll)
    above_top = lax.dynamic_slice_in_dim(above_all, subtree, 1, 0)
    a_list = down_pass(probs, levels, messages, above_top)
    weighted = weigh(a_list, messages, site_weight, total_sites)
    level_counts = [
        jnp.einsum("bis,bjs->bij", vector, partial_value, precision=lax.Precision.HIGH)
        for vector, partial_value in zip(weighted, levels)
    ]
    spare = site_count * per_dev - sum(c.shape[0] for c in level_counts)
    part_counts = jnp.concatenate(level_counts + [jnp.zeros((spare, 64, 64), jnp.float32)], axis=0)
    own_counts = pair_scatter(part_counts, site_count, 2)
    d_scaled = own_pull(own_counts)[0]
    use_rates = lax.dynamic_slice_in_dim(slot_rates, own_start, per_dev, 0)
    use_len = lax.dynamic_slice_in_dim(slot_len, own_start, per_dev, 0)
    use_pick = lax.dynamic_slice_in_dim(class_pick, own_start, per_dev, 0)
    d_length = jnp.sum(d_scaled * use_rates, axis=(1, 2))
    d_rates = jnp.einsum(
        "bc,bij->cij", use_pick, d_scaled * use_len[:, None, None], precision=lax.Precision.HIGH
    )
    unused_rates, pull_rates = jax.vjp(
        lambda table, ratio: build_rates(table, codon_freq, ratio)[0], exchanges, omega_ratio
    )
    d_exch, d_omega = pull_rates(d_rates)
    n_branch = lax.axis_size("branch")
    length_slab = jnp.zeros((n_branch, SLOTS), jnp.float32)
    length_slab = lax.dynamic_update_slice(length_slab, d_length[None, :], (subtree, own_start))
    loglik_keep = jnp.where(subtree == 0, loglik_part, jnp.float32(0.0))
    packed = jnp.concatenate(
        [d_exch.reshape(-1), d_omega, length_slab.reshape(-1), loglik_keep[None]]
    )
    rows = -(-packed.shape[0] // (8 * 128)) * 8
    packed = jnp.pad(packed, (0, rows * 128 - packed.shape[0])).reshape(rows, 128)
    summed = allreduce_all(packed, site_count, n_branch).reshape(-1)
    grad_exch = summed[: 64 * 64].reshape(64, 64)
    grad_omega = summed[64 * 64 : 64 * 64 + CLASSES]
    length_all = summed[64 * 64 + CLASSES : 64 * 64 + CLASSES + n_branch * SLOTS].reshape(n_branch, SLOTS)
    log_total = summed[64 * 64 + CLASSES + n_branch * SLOTS]
    loglik = log_total / total_sites / total_taxa
    length_out = lax.dynamic_index_in_dim(length_all, subtree, 0, keepdims=False)[:EDGES]
    return (grad_exch, grad_omega, length_out, loglik)


def solution(mesh):
    return jax.shard_map(
        body,
        mesh=mesh,
        in_specs=(
            P(None, "site"),
            P(None, "site"),
            P("site"),
            P(),
            P(),
            P(),
            P(),
            P("branch"),
            P("branch"),
        ),
        out_specs=(P(), P(), P("branch"), P()),
        check_vma=False,
    )
```
